32 devices in a mesh: dp: 8 (over y, x, core), tensor: 4 (over z).
Axes of the slice: x: 2, y: 2, z: 4, core: 2. Of those that a mesh axis runs over, the one named last changes fastest.
Arguments:
- tokens: bfloat16 [2, 8, 1984, 1024], P(None, 'dp', 'tensor'), may hold values from -6 to 6
- segment_ids: int32 [2, 8, 1984], P(None, 'dp'), may hold values from 0 to 5, never falling along the last dimension, each value on 1 to 661 neighbouring positions
- pad_mask: int32 [2, 8, 1984], P(None, 'dp'), may hold values from 0 to 1, as said below
- cotangent: bfloat16 [2, 8, 1984, 1024], P(None, 'dp', 'tensor'), may hold values from -6 to 6
- ln1_gain: bfloat16 [1024], P('dp'), may hold values from 0.099609375 to 1.8984375
- ln1_bias: bfloat16 [1024], P('dp'), may hold values from -3 to 3
- qkv_weight: bfloat16 [1024, 3, 1024], P('dp', None, 'tensor'), may hold values from -0.25 to 0.25
- qv_bias: bfloat16 [2, 16, 64], P(None, 'tensor', 'dp'), may hold values from -3 to 3
- proj_weight: bfloat16 [1024, 1024], P('tensor', 'dp'), may hold values from -1.5 to 1.5
- proj_bias: bfloat16 [1024], P('dp'), may hold values from -3 to 3
- ln2_gain: bfloat16 [1024], P('dp'), may hold values from 0.099609375 to 1.8984375
- ln2_bias: bfloat16 [1024], P('dp'), may hold values from -3 to 3
- fc1_weight: bfloat16 [1024, 4096], P('dp', 'tensor'), may hold values from -0.1875 to 0.1875
- fc1_bias: bfloat16 [4, 1024], P('tensor', 'dp'), may hold values from -3 to 3
- fc2_weight: bfloat16 [4096, 1024], P('tensor', 'dp'), may hold values from -0.09375 to 0.09375
- fc2_bias: bfloat16 [1024], P('dp'), may hold values from -3 to 3
Outputs:
- out: bfloat16 [2, 8, 1984, 1024], P(None, 'dp', 'tensor')
- tokens_grad: bfloat16 [2, 8, 1984, 1024], P(None, 'dp', 'tensor')
- ln1_gain_grad: float32 [1024], P('dp')
- ln1_bias_grad: float32 [1024], P('dp')
- qkv_weight_grad: float32 [1024, 3, 1024], P('dp', None, 'tensor')
- qv_bias_grad: float32 [2, 16, 64], P(None, 'tensor', 'dp')
- proj_weight_grad: float32 [1024, 1024], P('tensor', 'dp')
- proj_bias_grad: float32 [1024], P('dp')
- ln2_gain_grad: float32 [1024], P('dp')
- ln2_bias_grad: float32 [1024], P('dp')
- fc1_weight_grad: float32 [1024, 4096], P('dp', 'tensor')
- fc1_bias_grad: float32 [4, 1024], P('tensor', 'dp')
- fc2_weight_grad: float32 [4096, 1024], P('tensor', 'dp')
- fc2_bias_grad: float32 [1024], P('dp')
The draws below stay inside these ranges and needn't reach their ends.
Inputs may be any that keep to these rules, and one draw needn't show every extreme that they name: In each sequence pad_mask is 1 on a leading run of slots and 0 on the rest; the run of zeros is at least one slot long.
All inputs are finite; a program needn't handle non-finite values.
Results may differ from the reference program's by a relative error of at most 0.02.
Values may be sent and summed in bfloat16 or wider, within the bound.
A program may use at most 256 MiB of HBM per device.

```python
import math
import jax
import jax.numpy as jnp
import numpy as np
from jax import lax

D = 1024
H = 16
HD = 64
FF = 4096
SEQ_LEN = 1984
MB = 2
SEQS = 8
N_TENSOR = 4


def draw_pad_mask(key, part):
    tail_size = jax.random.randint(key, (MB, SEQS, 1), 1, SEQ_LEN // 8 + 1)
    positions = jnp.arange(SEQ_LEN, dtype=jnp.int32)[None, None, :]
    return (positions < SEQ_LEN - tail_size).astype(jnp.int32)


def block_scale(stream_key, shape, cuts, low, high):
    gain, own = 1.0, jax.random.fold_in(stream_key, 6)
    for position, blocks in cuts:
        heights = jnp.exp(jax.random.uniform(jax.random.fold_in(own, position), (blocks,), jnp.float32, low / len(cuts), high / len(cuts)))
        gain = gain * jnp.repeat(heights, shape[position] // blocks).reshape([-1 if axis == position else 1 for axis in range(len(shape))])
    return gain


def split_up(count, total, reach, skew):
    loads = [(1 << 20) // math.isqrt(standing ** skew) + 1 for standing in range(2, count + 1)]
    spare, counts = total - reach - (count - 1), [1] * (count - 1)
    while spare > 0:
        movable = [i for i in range(count - 1) if counts[i] < reach]
        whole, budget = sum([loads[i] for i in movable]), spare
        for i in movable:
            addition = min(reach - counts[i], max(1, budget * loads[i] // whole), spare)
            counts[i] = counts[i] + addition
            spare = spare - addition
    return np.array([reach] + counts)


def uneven(stream_key, amount, total, most, slope):
    if amount == 2:
        one = jax.random.randint(stream_key, (), max(1, total - most), min(most, total - 1) + 1)
        return jnp.stack([one, total - one])
    lengths = jnp.asarray(split_up(amount, total, most, slope), jnp.int32)
    twos = (amount - 1) // 2
    giver, taker = lengths[1:1 + 2 * twos:2], lengths[2:2 + 2 * twos:2]
    margin = jnp.minimum(giver - 1, most - taker)
    passed = jax.random.randint(jax.random.fold_in(stream_key, 1), (twos,), 0, 1 << 20) % (margin + 1)
    lengths = lengths.at[1:1 + 2 * twos:2].set(giver - passed).at[2:2 + 2 * twos:2].set(taker + passed)
    return lengths[jax.random.permutation(jax.random.fold_in(stream_key, 2), amount)]


def bell_draw(key, shape, width, reach, split=(), held_as=jnp.bfloat16):
    entries = jax.random.normal(key, shape, jnp.float32) * width
    if len(split) > 0:
        entries = block_scale(key, shape, split, -0.22, 0.18) * entries
    return jnp.clip(entries, min=-reach, max=reach).astype(held_as)


def setup_inputs(seed: int = 0) -> dict:
    key_of = jax.random.split(jax.random.key(seed), 17)
    return {
        "tokens": bell_draw(key_of[0], (MB, SEQS, SEQ_LEN, D), 1.0, 6.0, ((1, 8), (2, 4))),
        "segment_ids": jax.vmap(lambda own: jnp.searchsorted(jnp.cumsum(uneven(own, 6, SEQ_LEN, SEQ_LEN // 3, 1)), jnp.arange(SEQ_LEN), side="right"))(jax.random.split(key_of[1], MB * SEQS)).reshape((MB, SEQS, SEQ_LEN)).astype(jnp.int32),
        "pad_mask": draw_pad_mask(jax.random.fold_in(key_of[16], 71), 0),
        "cotangent": bell_draw(key_of[3], (MB, SEQS, SEQ_LEN, D), 1.0, 6.0, ((1, 8), (2, 4))),
        "ln1_gain": jnp.clip(1.0 + 0.18 * jax.random.normal(key_of[4], (D,), jnp.float32), 0.099609375, 1.8984375).astype(jnp.bfloat16),
        "ln1_bias": bell_draw(key_of[5], (D,), 0.3, 3.0, ((0, 8),)),
        "qkv_weight": bell_draw(key_of[6], (D, 3, D), (D // 2) ** -0.5, 0.25, ((0, 8), (2, 4))),
        "qv_bias": bell_draw(key_of[7], (2, H, HD), 0.5, 3.0, ((1, 4), (2, 8))),
        "proj_weight": bell_draw(key_of[8], (D, D), (D // 64) ** -0.5, 1.5, ((0, 4), (1, 8))),
        "proj_bias": bell_draw(key_of[9], (D,), 0.5, 3.0, ((0, 8),)),
        "ln2_gain": jnp.clip(1.0 + 0.18 * jax.random.normal(key_of[10], (D,), jnp.float32), 0.099609375, 1.8984375).astype(jnp.bfloat16),
        "ln2_bias": bell_draw(key_of[11], (D,), 0.3, 3.0, ((0, 8),)),
        "fc1_weight": bell_draw(key_of[12], (D, FF), D ** -0.5, 0.1875, ((0, 8), (1, 4))),
        "fc1_bias": bell_draw(key_of[13], (N_TENSOR, FF // N_TENSOR), 0.5, 3.0, ((0, 4), (1, 8))),
        "fc2_weight": bell_draw(key_of[14], (FF, D), FF ** -0.5, 0.09375, ((0, 4), (1, 8))),
        "fc2_bias": bell_draw(key_of[15], (D,), 0.5, 3.0, ((0, 8),)),
    }


epsilon = 1e-06
score_scale = 0.125
masked_score = -1e+30
highest = lax.Precision.HIGHEST

@jax.custom_vjp
def low(v):
    return lax.optimization_barrier(v.astype(jnp.bfloat16)).astype(jnp.float32)

@jax.custom_vjp
def low_back(v):
    return v

def low_keep(v):
    return (low(v), None)

def low_pass(kept, grad):
    return (grad,)

def back_keep(v):
    return (v, None)

def back_low(kept, grad):
    return (low(grad),)
low.defvjp(low_keep, low_pass)
low_back.defvjp(back_keep, back_low)

def normalize(operand, scale_vec, shift_vec):
    centred = operand - lax.optimization_barrier(jnp.mean(operand, axis=-1, keepdims=True))
    inverse = lax.rsqrt(lax.optimization_barrier(jnp.mean(centred * centred, axis=-1, keepdims=True)) + epsilon)
    return centred * inverse * scale_vec + shift_vec

def attention(queries, keys_all, values_all, seg_all, valid_all):
    length = seg_all.shape[0]
    half_rows = length // 2
    positions = jnp.arange(length, dtype=jnp.int32)

    def one_block(block_item):
        query_blk, seg_blk, pos_blk = block_item
        scores = jnp.einsum('qhd,khd->hqk', query_blk, keys_all, precision=highest) * score_scale
        scores = low_back(scores)
        same_segment = seg_blk[:, None] == seg_all[None, :]
        key_live = (valid_all[None, :] == 1) | (pos_blk[:, None] == positions[None, :])
        scores = jnp.where((same_segment & key_live)[None], scores, masked_score)
        prob_low = low(jax.nn.softmax(scores, axis=-1))
        return jnp.einsum('hqk,khd->qhd', prob_low, values_all, precision=highest)
    mixture = lax.map(jax.checkpoint(one_block), (queries.reshape(2, half_rows, H, HD), seg_all.reshape(2, half_rows), positions.reshape(2, half_rows)))
    return mixture.reshape(length, H, HD)

def one_sequence(resid, seg_all, valid_all, params):
    gain_one, shift_one, qkv_mat, qkv_bias, proj_mat, proj_shift, gain_two, shift_two, fc1_mat, fc1_shift, fc2_mat, fc2_shift = params
    length = resid.shape[0]
    normed_in = low(normalize(resid, gain_one, shift_one))
    projected = jnp.dot(normed_in, qkv_mat.reshape(D, 3 * D), precision=highest).reshape(length, 3, H, HD)
    bias_rows = jnp.stack([qkv_bias[0], jnp.zeros((H, HD), jnp.float32), qkv_bias[1]])
    heads_qkv = low_back(low(projected + bias_rows))
    mixture = attention(heads_qkv[:, 0], heads_qkv[:, 1], heads_qkv[:, 2], seg_all, valid_all)
    heads_low = low_back(low(mixture.reshape(length, D)))
    attn_branch = low_back(jnp.dot(heads_low, proj_mat, precision=highest) + proj_shift)
    hidden_res = resid + attn_branch
    normed_mid = low(normalize(hidden_res, gain_two, shift_two))
    pre_act = low_back(jnp.dot(normed_mid, fc1_mat, precision=highest) + fc1_shift.reshape(FF))
    act_low = low(jax.nn.gelu(pre_act, approximate=False))
    mlp_branch = low_back(jnp.dot(act_low, fc2_mat, precision=highest) + fc2_shift)
    return hidden_res + mlp_branch

def reference(tokens, segment_ids, pad_mask, cotangent, ln1_gain, ln1_bias, qkv_weight, qv_bias, proj_weight, proj_bias, ln2_gain, ln2_bias, fc1_weight, fc1_bias, fc2_weight, fc2_bias):
    params = tuple((item.astype(jnp.float32) for item in (ln1_gain, ln1_bias, qkv_weight, qv_bias, proj_weight, proj_bias, ln2_gain, ln2_bias, fc1_weight, fc1_bias, fc2_weight, fc2_bias)))
    seq_total = MB * SEQS
    rows_all = tokens.astype(jnp.float32).reshape(seq_total, SEQ_LEN, D)
    seg_rows = segment_ids.reshape(seq_total, SEQ_LEN)
    valid_rows = pad_mask.reshape(seq_total, SEQ_LEN)

    def whole(rows_in, params_in):
        return lax.map(lambda seq_item: one_sequence(seq_item[0], seq_item[1], seq_item[2], params_in), (rows_in, seg_rows, valid_rows))
    result, pullback = jax.vjp(whole, rows_all, params)
    grad_rows, grad_params = pullback(cotangent.astype(jnp.float32).reshape(seq_total, SEQ_LEN, D))
    out = result.reshape(tokens.shape).astype(jnp.bfloat16)
    tokens_grad = grad_rows.reshape(tokens.shape).astype(jnp.bfloat16)
    return (out, tokens_grad, grad_params[0], grad_params[1], grad_params[2], grad_params[3], grad_params[4], grad_params[5], grad_params[6], grad_params[7], grad_params[8], grad_params[9], grad_params[10], grad_params[11])
```

```python
import functools
import math

import jax
import jax.numpy as jnp
from jax import lax
from jax.experimental import pallas as pl
from jax.experimental.pallas import tpu as pltpu
from jax.sharding import PartitionSpec as P

bf16 = jnp.bfloat16
f32 = jnp.float32
epsilon = 1e-06
score_scale = 0.125
log2e = 1.4426950408889634
low_score = -1e30
block = 256
mib = 1 << 20


def dot_nn(left, right):
    return lax.dot_general(left, right, (((1,), (0,)), ((), ())), preferred_element_type=f32)


def dot_nt(left, right):
    return lax.dot_general(left, right, (((1,), (1,)), ((), ())), preferred_element_type=f32)


def dot_tn(left, right):
    return lax.dot_general(left, right, (((0,), (0,)), ((), ())), preferred_element_type=f32)


def lane_halves(rows):
    lane = lax.broadcasted_iota(jnp.int32, rows.shape, 1)
    zero = jnp.zeros_like(rows)
    return jnp.where(lane < 64, rows, zero), jnp.where(lane < 64, zero, rows)


def attend_kernel(
    info, qo, ko, vo, qr, kr, vr, seg_col, seg_row, out_own, out_oth, lse_ref,
    qs, k0s, k1s, v0s, v1s, os,
):
    half = qo.shape[0]
    blocks = 2 * half // block
    side = info[0]
    own_at = pl.multiple_of(side * half, half)
    oth_at = pl.multiple_of((1 - side) * half, half)
    lane = lax.broadcasted_iota(jnp.int32, (half, 128), 1)
    for at, q_in, k_in, v_in in ((own_at, qo, ko, vo), (oth_at, qr, kr, vr)):
        rows = pl.ds(at, half)
        qs[rows, :] = q_in[...]
        k0s[rows, :], k1s[rows, :] = lane_halves(k_in[...])
        v_all = v_in[...]
        v0s[rows, :] = jnp.where(lane < 64, v_all, (lane == 64).astype(bf16))
        v1s[rows, :] = jnp.where(lane < 64, (lane == 0).astype(bf16), v_all)

    diff = lax.broadcasted_iota(jnp.int32, (block, block), 0) - lax.broadcasted_iota(
        jnp.int32, (block, block), 1
    )
    factor = score_scale * log2e

    def per_rows(qb, carry):
        q_at = pl.multiple_of(qb * block, block)
        q_rows = qs[pl.ds(q_at, block), :]
        q_seg = seg_col[pl.ds(q_at, block), :]

        def per_keys(kb, state):
            m0, m1, a0, a1 = state
            k_at = pl.multiple_of(kb * block, block)
            keys = pl.ds(k_at, block)
            mask = (q_seg == seg_row[0:1, keys]) | (diff == k_at - q_at)

            def one(k_ref, v_ref, m_old, acc):
                s = jnp.where(mask, dot_nt(q_rows, k_ref[keys, :]), low_score)
                m_new = jnp.maximum(m_old, jnp.max(s, axis=1, keepdims=True))
                p = jnp.exp2((s - m_new) * factor).astype(bf16)
                fade = jnp.exp2((m_old - m_new) * factor)
                return m_new, acc * fade + dot_nn(p, v_ref[keys, :])

            m0, a0 = one(k0s, v0s, m0, a0)
            m1, a1 = one(k1s, v1s, m1, a1)
            return m0, m1, a0, a1

        start = jnp.full((block, 1), low_score, f32)
        zero = jnp.zeros((block, 128), f32)
        m0, m1, a0, a1 = lax.fori_loop(
            info[1 + qb], info[1 + blocks + qb], per_keys, (start, start, zero, zero)
        )
        t0 = a0[:, 64:65]
        t1 = a1[:, 0:1]
        lane_q = lax.broadcasted_iota(jnp.int32, (block, 128), 1)
        os[pl.ds(q_at, block), :] = jnp.where(lane_q < 64, a0 / t0, a1 / t1).astype(bf16)
        both = jnp.where(
            lane_q < 64, m0 * factor + jnp.log2(t0), m1 * factor + jnp.log2(t1)
        )
        turned = both.T
        lse_ref[0, 0:1, pl.ds(q_at, block)] = turned[0:1, :]
        lse_ref[0, 1:2, pl.ds(q_at, block)] = turned[64:65, :]
        return carry

    lax.fori_loop(0, blocks, per_rows, 0)
    out_own[...] = os[pl.ds(own_at, half), :]
    out_oth[...] = os[pl.ds(oth_at, half), :]


def attend(info, own, oth, seg_col, seg_row):
    half = own.shape[0]
    rows = 2 * half
    pairs = own.shape[1] // 384

    def part(which):
        return pl.BlockSpec((half, 128), lambda i, _: (0, (i // 2) * 6 + which * 2 + i % 2))

    whole = lambda shape: pl.BlockSpec(shape, lambda i, _: (0,) * len(shape))
    return pl.pallas_call(
        attend_kernel,
        grid_spec=pltpu.PrefetchScalarGridSpec(
            num_scalar_prefetch=1,
            grid=(pairs,),
            in_specs=[part(0), part(1), part(2)] * 2 + [whole((rows, 1)), whole((1, rows))],
            out_specs=[
                pl.BlockSpec((half, 128), lambda i, _: (0, i)),
                pl.BlockSpec((half, 128), lambda i, _: (0, i)),
                pl.BlockSpec((1, 8, rows), lambda i, _: (i, 0, 0)),
            ],
            scratch_shapes=[pltpu.VMEM((rows, 128), bf16)] * 6,
        ),
        out_shape=(
            jax.ShapeDtypeStruct((half, pairs * 128), bf16),
            jax.ShapeDtypeStruct((half, pairs * 128), bf16),
            jax.ShapeDtypeStruct((pairs, 8, rows), f32),
        ),
        compiler_params=pltpu.CompilerParams(vmem_limit_bytes=32 * mib),
        cost_estimate=pl.CostEstimate(
            flops=int(pairs * 2 * rows * rows * 256 * 1.5), bytes_accessed=int(own.size * 5), transcendentals=0
        ),
        name="attend",
    )(info, own, own, own, oth, oth, oth, seg_col, seg_row)


def attend_back_kernel(
    info, qo, ko, vo, qr, kr, vr, go, gr, oo, orr, lse_ref, seg_col, seg_row,
    dqo, dko, dvo, dqr, dkr, dvr,
    q0s, q1s, k0s, k1s, v0s, v1s, g0s, g1s, os, dqs, dks, dvs,
):
    half = qo.shape[0]
    blocks = 2 * half // block
    side = info[0]
    own_at = pl.multiple_of(side * half, half)
    oth_at = pl.multiple_of((1 - side) * half, half)
    for at, q_in, k_in, v_in, g_in, o_in in (
        (own_at, qo, ko, vo, go, oo),
        (oth_at, qr, kr, vr, gr, orr),
    ):
        rows = pl.ds(at, half)
        q0s[rows, :], q1s[rows, :] = lane_halves(q_in[...])
        k0s[rows, :], k1s[rows, :] = lane_halves(k_in[...])
        v0s[rows, :], v1s[rows, :] = lane_halves(v_in[...])
        g0s[rows, :], g1s[rows, :] = lane_halves(g_in[...])
        os[rows, :] = o_in[...]
    dks[...] = jnp.zeros_like(dks)
    dvs[...] = jnp.zeros_like(dvs)

    diff = lax.broadcasted_iota(jnp.int32, (block, block), 1) - lax.broadcasted_iota(
        jnp.int32, (block, block), 0
    )
    factor = score_scale * log2e

    def per_rows(qb, carry):
        q_at = pl.multiple_of(qb * block, block)
        rows = pl.ds(q_at, block)
        g_sum = (g0s[rows, :] + g1s[rows, :]).astype(f32) * os[rows, :].astype(f32)
        turned = g_sum.T
        d0 = jnp.sum(turned[0:64, :], axis=0, keepdims=True)
        d1 = jnp.sum(turned[64:128, :], axis=0, keepdims=True)
        l0 = lse_ref[0, 0:1, rows]
        l1 = lse_ref[0, 1:2, rows]
        q_seg = seg_row[0:1, rows]
        q0, q1, g0, g1 = q0s[rows, :], q1s[rows, :], g0s[rows, :], g1s[rows, :]

        def per_keys(kb, dq):
            k_at = pl.multiple_of(kb * block, block)
            keys = pl.ds(k_at, block)
            mask = (q_seg == seg_col[keys, :]) | (diff == k_at - q_at)

            def one(q, g, k_ref, v_ref, lse, d):
                k = k_ref[keys, :]
                s = jnp.where(mask, dot_nt(k, q) * factor - lse, low_score)
                p = jnp.exp2(s)
                dv = dot_nn(p.astype(bf16), g)
                dp = dot_nt(v_ref[keys, :], g)
                ds = (p * (dp - d)).astype(bf16)
                return dv, dot_nn(ds, q), dot_tn(ds, k)

            dv_a, dk_a, dq_a = one(q0, g0, k0s, v0s, l0, d0)
            dv_b, dk_b, dq_b = one(q1, g1, k1s, v1s, l1, d1)
            dvs[keys, :] += dv_a + dv_b
            dks[keys, :] += dk_a + dk_b
            return dq + (dq_a + dq_b)

        dq = lax.fori_loop(
            info[1 + qb], info[1 + blocks + qb], per_keys, jnp.zeros((block, 128), f32)
        )
        dqs[rows, :] = dq
        return carry

    lax.fori_loop(0, blocks, per_rows, 0)
    for at, dq_out, dk_out, dv_out in ((own_at, dqo, dko, dvo), (oth_at, dqr, dkr, dvr)):
        rows = pl.ds(at, half)
        dq_out[...] = (dqs[rows, :] * score_scale).astype(bf16)
        dk_out[...] = (dks[rows, :] * score_scale).astype(bf16)
        dv_out[...] = dvs[rows, :].astype(bf16)


def attend_back(info, own, oth, g_own, g_oth, o_own, o_oth, lse, seg_row_k, seg_col_k):
    half = own.shape[0]
    rows = 2 * half
    pairs = own.shape[1] // 384

    def part(which):
        return pl.BlockSpec((half, 128), lambda i, _: (0, (i // 2) * 6 + which * 2 + i % 2))

    col = pl.BlockSpec((half, 128), lambda i, _: (0, i))
    whole = lambda shape: pl.BlockSpec(shape, lambda i, _: (0,) * len(shape))
    shape = jax.ShapeDtypeStruct((half, pairs * 128), bf16)
    return pl.pallas_call(
        attend_back_kernel,
        grid_spec=pltpu.PrefetchScalarGridSpec(
            num_scalar_prefetch=1,
            grid=(pairs,),
            in_specs=[part(0), part(1), part(2)] * 2
            + [col] * 4
            + [pl.BlockSpec((1, 8, rows), lambda i, _: (i, 0, 0))]
            + [whole((rows, 1)), whole((1, rows))],
            out_specs=[col] * 6,
            scratch_shapes=[pltpu.VMEM((rows, 128), bf16)] * 9 + [pltpu.VMEM((rows, 128), f32)] * 3,
        ),
        out_shape=(shape,) * 6,
        compiler_params=pltpu.CompilerParams(vmem_limit_bytes=40 * mib),
        cost_estimate=pl.CostEstimate(
            flops=int(pairs * 5 * rows * rows * 256), bytes_accessed=int(own.size * 10), transcendentals=0
        ),
        name="attend_back",
    )(info, own, own, own, oth, oth, oth, g_own, g_oth, o_own, o_oth, lse, seg_col_k, seg_row_k)


def ingest_kernel(order, a_ref, b_ref, o_ref):
    rows, width = a_ref.shape
    count = order.shape[0] - 1
    size = width // count
    first = order[count]
    for place in range(count):
        src = pl.ds(pl.multiple_of(order[place] * size, size), size)
        dst = slice(place * size, (place + 1) * size)

        @pl.when(first == 0)
        def _():
            o_ref[0:rows, dst] = a_ref[:, src]
            o_ref[rows : 2 * rows, dst] = b_ref[:, src]

        @pl.when(first != 0)
        def _():
            o_ref[0:rows, dst] = b_ref[:, src]
            o_ref[rows : 2 * rows, dst] = a_ref[:, src]

    o_ref[2 * rows :, :] = jnp.zeros((o_ref.shape[0] - 2 * rows, width), o_ref.dtype)


def ingest(order, first, a, b, padded):
    rows, width = a.shape
    count = order.shape[0]
    if width // count % 128:
        both = jnp.where(first == 0, jnp.concatenate([a, b]), jnp.concatenate([b, a]))
        both = jnp.take(both.reshape(2 * rows, count, -1), order, axis=1).reshape(2 * rows, width)
        return jnp.pad(both, ((0, padded - 2 * rows), (0, 0)))
    scalars = jnp.concatenate([order, first[None]]).astype(jnp.int32)
    return pl.pallas_call(
        ingest_kernel,
        grid_spec=pltpu.PrefetchScalarGridSpec(
            num_scalar_prefetch=1,
            grid=(1,),
            in_specs=[pl.BlockSpec((rows, width), lambda i, _: (0, 0))] * 2,
            out_specs=pl.BlockSpec((padded, width), lambda i, _: (0, 0)),
        ),
        out_shape=jax.ShapeDtypeStruct((padded, width), a.dtype),
        compiler_params=pltpu.CompilerParams(vmem_limit_bytes=20 * mib),
        name="ingest",
    )(scalars, a, b)


def egress_kernel(order, x_ref, a_ref, b_ref):
    rows, width = a_ref.shape
    count = order.shape[0] - 1
    size = width // count
    first = order[count]
    for place in range(count):
        dst = pl.ds(pl.multiple_of(order[place] * size, size), size)
        src = slice(place * size, (place + 1) * size)

        @pl.when(first == 0)
        def _():
            a_ref[:, dst] = x_ref[0:rows, src]
            b_ref[:, dst] = x_ref[rows : 2 * rows, src]

        @pl.when(first != 0)
        def _():
            b_ref[:, dst] = x_ref[0:rows, src]
            a_ref[:, dst] = x_ref[rows : 2 * rows, src]


def egress(order, inverse, first, x, rows):
    width = x.shape[1]
    count = order.shape[0]
    if width // count % 128:
        both = jnp.take(x.reshape(-1, count, width // count), inverse, axis=1).reshape(-1, width)
        top, low = both[:rows], both[rows : 2 * rows]
        return jnp.where(first == 0, top, low), jnp.where(first == 0, low, top)
    scalars = jnp.concatenate([order, first[None]]).astype(jnp.int32)
    return pl.pallas_call(
        egress_kernel,
        grid_spec=pltpu.PrefetchScalarGridSpec(
            num_scalar_prefetch=1,
            grid=(1,),
            in_specs=[pl.BlockSpec(x.shape, lambda i, _: (0, 0))],
            out_specs=[pl.BlockSpec((rows, width), lambda i, _: (0, 0))] * 2,
        ),
        out_shape=(jax.ShapeDtypeStruct((rows, width), x.dtype),) * 2,
        compiler_params=pltpu.CompilerParams(vmem_limit_bytes=20 * mib),
        name="egress",
    )(scalars, x)


def norm_parts(operand):
    centred = operand - jnp.mean(operand, axis=-1, keepdims=True)
    inverse = lax.rsqrt(jnp.mean(centred * centred, axis=-1, keepdims=True) + epsilon)
    return centred * inverse, inverse


def norm_back(scaled, normed, inverse):
    return inverse * (
        scaled
        - jnp.mean(scaled, axis=-1, keepdims=True)
        - normed * jnp.mean(scaled * normed, axis=-1, keepdims=True)
    )


def make_body(n_dp, n_t):
    bits = n_dp.bit_length() - 1
    reverse = [int(format(i, "b").zfill(bits)[::-1], 2) for i in range(n_dp)]
    axes = ("dp", "tensor")

    def at(dp, t):
        return dp * n_t + t

    go_a, go_b = [], []
    for dp in range(n_dp):
        c, base = dp % 2, dp - dp % 2
        for j in range(n_t):
            go_a.append((at(dp, j), at(base + j // 2, 2 * (j % 2) + c)))
            go_b.append((at(dp, j), at(base + j // 2, 2 * (1 - j % 2) + c)))
    back_a = [(d, s) for s, d in go_a]
    back_b = [(d, s) for s, d in go_b]
    ring = [(j, (j + 1) % n_t) for j in range(n_t)]

    def swap(value, bit):
        return lax.ppermute(value, "dp", [(i, i ^ (1 << bit)) for i in range(n_dp)])

    def step_z(value):
        return lax.ppermute(value, "tensor", ring)

    def spread(own):
        pieces = [own]
        for _ in range(n_t - 1):
            pieces.append(step_z(pieces[-1]))
        halves = []
        middle = list(range(1, bits))
        for cols, order in ((pieces[:2], middle), (pieces[2:], middle[::-1])):
            start = jnp.concatenate(cols, axis=1)
            if bits <= 3:
                held = {0: start}
                for bit in order + [0]:
                    for key in list(held):
                        held[key ^ (1 << bit)] = swap(held[key], bit)
                halves.append(jnp.concatenate([held[reverse[p]] for p in range(n_dp)], axis=0))
            else:
                grid = start.reshape((1,) * bits + start.shape)
                for bit in order + [0]:
                    grid = jnp.concatenate([grid, swap(grid, bit)], axis=bit)
                halves.append(grid.reshape(-1, start.shape[1]))
        return halves

    def collect(x, g_halves):
        rows = x.shape[1] // 2
        outs = []
        middle = list(range(1, bits))
        for g, order in zip(g_halves, (middle, middle[::-1])):
            away = dot_tn(x[:, rows:], g).astype(bf16)
            came = swap(away, 0)
            held = (dot_tn(x[:, :rows], g) + came.astype(f32)).astype(bf16)
            held = held.reshape((2,) * (bits - 1) + (-1, g.shape[1]))
            left = list(middle)
            for bit in order:
                axis = left.index(bit)
                left.pop(axis)
                mine = lax.index_in_dim(held, 0, axis, keepdims=False)
                send = lax.index_in_dim(held, 1, axis, keepdims=False)
                held = (mine.astype(f32) + swap(send, bit).astype(f32)).astype(bf16)
            size = g.shape[1] // 2
            outs += [held[:, :size], held[:, size:]]
        total = outs[1]
        for k in range(2, n_t):
            total = (step_z(total).astype(f32) + outs[k].astype(f32)).astype(bf16)
        return step_z(total).astype(f32) + outs[0].astype(f32)

    def body(
        tokens, segment_ids, pad_mask, cotangent, ln1_gain, ln1_bias, qkv_weight, qv_bias,
        proj_weight, proj_bias, ln2_gain, ln2_bias, fc1_weight, fc1_bias, fc2_weight, fc2_bias,
    ):
        me = lax.axis_index("dp")
        z = lax.axis_index("tensor")
        side = me % 2
        quarter, width = tokens.shape[2], tokens.shape[3]
        length = segment_ids.shape[2]
        half = -(-2 * quarter // block) * block
        size = width // n_dp
        micro = z // 2
        odd = z % 2
        order = jnp.stack([me ^ reverse[p] for p in range(n_dp)]).astype(jnp.int32)
        inverse = jnp.stack(
            [sum((((me ^ d) >> b) & 1) << (bits - 1 - b) for b in range(bits)) for d in range(n_dp)]
        ).astype(jnp.int32)

        def bring(array):
            a = lax.ppermute(lax.dynamic_index_in_dim(array[:, 0], odd, 0, False), axes, go_a)
            b = lax.ppermute(lax.dynamic_index_in_dim(array[:, 0], 1 - odd, 0, False), axes, go_b)
            return ingest(order, micro, a, b, half)

        def give(x):
            a, b = egress(order, inverse, micro, x, quarter)
            a = lax.ppermute(a, axes, back_a)
            b = lax.ppermute(b, axes, back_b)
            return jnp.where(odd == 0, jnp.stack([a, b]), jnp.stack([b, a]))[:, None]

        x_low = bring(tokens)

        packed = jnp.concatenate(
            [
                ln1_gain, ln1_bias, proj_bias, ln2_gain, ln2_bias, fc2_bias,
                fc1_bias.reshape(-1), qv_bias.reshape(-1),
            ]
        )
        small = lax.all_gather(packed, axes, axis=0, tiled=False).reshape(n_dp, n_t, -1)
        by_t = jnp.take(small, (z - jnp.arange(n_t)) % n_t, axis=1).astype(f32)
        wide = jnp.take(by_t[:, 0, : 6 * size], order, axis=0).reshape(n_dp, 6, size)
        wide = jnp.transpose(wide, (1, 0, 2)).reshape(6, width)
        gain_one, shift_one, proj_shift, gain_two, shift_two, fc2_shift = [wide[i] for i in range(6)]
        fc1_shift = jnp.transpose(by_t[:, :, 6 * size : 7 * size], (1, 0, 2)).reshape(2, -1)
        heads_t, hd = qv_bias.shape[1], qv_bias.shape[2] * n_dp
        qv = by_t[:, :, 7 * size :].reshape(n_dp, n_t, 2, heads_t, hd // n_dp)
        qv = jnp.transpose(qv, (1, 2, 3, 0, 4)).reshape(n_t, 2, heads_t * hd)
        qkv_shift = jnp.stack([qv[:, 0], jnp.zeros_like(qv[:, 0]), qv[:, 1]], axis=1).reshape(2, -1)

        w_qkv = spread(qkv_weight.reshape(size, -1))
        w_proj = spread(proj_weight.T)
        w_fc1 = spread(fc1_weight)
        w_fc2 = spread(fc2_weight.T)

        which = z % 2
        packed_ids = jnp.stack([segment_ids[:, 0], pad_mask[:, 0]])
        packed_oth = swap(packed_ids, 0)
        ids = jnp.where(which == side, packed_ids, packed_oth)
        ids = lax.dynamic_index_in_dim(ids, micro, 1, False)
        seg, live = ids[0], ids[1]
        gap = half - length // 2

        def stretch(v, fill):
            return jnp.pad(v.reshape(2, -1), ((0, 0), (0, gap)), constant_values=fill).reshape(-1)

        q_ids = stretch(seg, -1)
        k_ids = stretch(jnp.where(live == 1, seg, -2), -2)
        per_half = half // block
        first_pos = jnp.array([h * (length // 2) + b * block for h in range(2) for b in range(per_half)])
        last_pos = jnp.array(
            [min(h * (length // 2) + (b + 1) * block, (h + 1) * (length // 2)) - 1 for h in range(2) for b in range(per_half)]
        )
        lo = jnp.sum((seg[None, :] < seg[first_pos][:, None]).astype(jnp.int32), axis=1)
        hi = jnp.sum((seg[None, :] <= seg[last_pos][:, None]).astype(jnp.int32), axis=1) - 1
        place = lambda v: jnp.where(v >= length // 2, v + gap, v) // block
        info = jnp.concatenate([side[None], place(lo), place(hi) + 1]).astype(jnp.int32)

        x = x_low.astype(f32)
        hat_one, inv_one = norm_parts(x)
        rows_one = (hat_one * gain_one + shift_one).astype(bf16)
        qkv = [(dot_nn(rows_one, w_qkv[i]) + qkv_shift[i]).astype(bf16) for i in range(2)]
        own = jnp.where(side == 0, qkv[0], qkv[1])
        oth = swap(jnp.where(side == 0, qkv[1], qkv[0]), 0)
        o_own, o_oth, lse = attend(info, own, oth, q_ids[:, None], k_ids[None, :])
        o_came = swap(o_oth, 0)
        heads = [jnp.where(side == 0, o_own, o_came), jnp.where(side == 0, o_came, o_own)]
        hidden = x + (dot_nt(heads[0], w_proj[0]) + dot_nt(heads[1], w_proj[1]) + proj_shift)
        hat_two, inv_two = norm_parts(hidden)
        rows_two = (hat_two * gain_two + shift_two).astype(bf16)
        acts, slopes = [], []
        for i in range(2):
            pre = dot_nn(rows_two, w_fc1[i]) + fc1_shift[i]
            cdf = 0.5 * (1.0 + lax.erf(pre * 0.7071067811865476))
            acts.append((pre * cdf).astype(bf16))
            slopes.append((cdf + pre * jnp.exp(-0.5 * pre * pre) * 0.3989422804014327).astype(bf16))
        y = hidden + (dot_nt(acts[0], w_fc2[0]) + dot_nt(acts[1], w_fc2[1]) + fc2_shift)
        out = give(y.astype(bf16))

        gy_low = bring(cotangent)
        gy = gy_low.astype(f32)
        fc2_shift_grad = jnp.sum(gy, axis=0)
        g_pre = [(dot_nn(gy_low, w_fc2[i]) * slopes[i].astype(f32)).astype(bf16) for i in range(2)]
        fc2_grad = collect(gy_low, acts)
        fc1_shift_grad = jnp.concatenate([jnp.sum(g, axis=0, dtype=f32) for g in g_pre])
        fc1_grad = collect(rows_two, g_pre)
        g_c = dot_nt(g_pre[0], w_fc1[0]) + dot_nt(g_pre[1], w_fc1[1])
        gain_two_grad = jnp.sum(g_c * hat_two, axis=0)
        shift_two_grad = jnp.sum(g_c, axis=0)
        g_hidden = gy + norm_back(g_c * gain_two, hat_two, inv_two)
        g_attn = g_hidden.astype(bf16)
        proj_shift_grad = jnp.sum(g_attn, axis=0, dtype=f32)
        proj_grad = collect(g_attn, heads)
        g_heads = [dot_nn(g_attn, w_proj[i]).astype(bf16) for i in range(2)]
        g_own = jnp.where(side == 0, g_heads[0], g_heads[1])
        g_oth = swap(jnp.where(side == 0, g_heads[1], g_heads[0]), 0)
        parts = attend_back(
            info, own, oth, g_own, g_oth, o_own, o_oth, lse, q_ids[None, :], k_ids[:, None]
        )

        def join(q, k, v):
            wide_t = q.shape[1] // 2
            return jnp.concatenate([p[:, i * wide_t : (i + 1) * wide_t] for i in range(2) for p in (q, k, v)], axis=1)

        d_own = join(*parts[:3])
        d_came = swap(join(*parts[3:]), 0)
        d_qkv = [jnp.where(side == 0, d_own, d_came), jnp.where(side == 0, d_came, d_own)]
        qkv_grad = collect(rows_one, d_qkv)
        qkv_sum = jnp.concatenate([jnp.sum(d, axis=0, dtype=f32) for d in d_qkv]).reshape(n_t, 3, -1)
        g_a = dot_nt(d_qkv[0], w_qkv[0]) + dot_nt(d_qkv[1], w_qkv[1])
        gain_one_grad = jnp.sum(g_a * hat_one, axis=0)
        shift_one_grad = jnp.sum(g_a, axis=0)
        tokens_grad = give((g_hidden + norm_back(g_a * gain_one, hat_one, inv_one)).astype(bf16))

        wide_g = jnp.stack(
            [gain_one_grad, shift_one_grad, proj_shift_grad, gain_two_grad, shift_two_grad, fc2_shift_grad]
        ).reshape(6, n_dp, size)
        wide_g = jnp.take(wide_g, inverse, axis=1)
        t_order = (z - jnp.arange(n_t)) % n_t
        fc1_g = jnp.take(fc1_shift_grad.reshape(n_t, n_dp, size), t_order, axis=0)
        qv_g = jnp.take(jnp.stack([qkv_sum[:, 0], qkv_sum[:, 2]], axis=1), t_order, axis=0)
        flat = lax.psum(
            jnp.concatenate([wide_g.reshape(-1), fc1_g.reshape(-1), qv_g.reshape(-1)]), axes
        )
        wide_g = lax.dynamic_index_in_dim(flat[: 6 * width].reshape(6, n_dp, size), me, 1, False)
        fc1_g = flat[6 * width : 6 * width + n_t * width].reshape(n_t, n_dp, size)
        fc1_g = lax.dynamic_index_in_dim(lax.dynamic_index_in_dim(fc1_g, z, 0, False), me, 0, True)
        qv_g = flat[(6 + n_t) * width :].reshape(n_t, 2, heads_t, n_dp, hd // n_dp)
        qv_g = lax.dynamic_index_in_dim(lax.dynamic_index_in_dim(qv_g, z, 0, False), me, 2, False)
        return (
            out,
            tokens_grad,
            wide_g[0],
            wide_g[1],
            qkv_grad.reshape(qkv_weight.shape),
            qv_g,
            proj_grad.T,
            wide_g[2],
            wide_g[3],
            wide_g[4],
            fc1_grad,
            fc1_g,
            fc2_grad.T,
            wide_g[5],
        )

    return body


def solution(mesh):
    in_specs = (
        P(None, "dp", "tensor", None),
        P(None, "dp", None),
        P(None, "dp", None),
        P(None, "dp", "tensor", None),
        P("dp"),
        P("dp"),
        P("dp", None, "tensor"),
        P(None, "tensor", "dp"),
        P("tensor", "dp"),
        P("dp"),
        P("dp"),
        P("dp"),
        P("dp", "tensor"),
        P("tensor", "dp"),
        P("tensor", "dp"),
        P("dp"),
    )
    out_specs = (
        P(None, "dp", "tensor", None),
        P(None, "dp", "tensor", None),
        P("dp"),
        P("dp"),
        P("dp", None, "tensor"),
        P(None, "tensor", "dp"),
        P("tensor", "dp"),
        P("dp"),
        P("dp"),
        P("dp"),
        P("dp", "tensor"),
        P("tensor", "dp"),
        P("tensor", "dp"),
        P("dp"),
    )
    body = make_body(mesh.shape["dp"], mesh.shape["tensor"])
    return jax.shard_map(body, mesh=mesh, in_specs=in_specs, out_specs=out_specs, check_vma=False)
```

```python
import functools
import math

import jax
import jax.numpy as jnp
from jax import lax
from jax.experimental import pallas as pl
from jax.experimental.pallas import tpu as pltpu
from jax.sharding import PartitionSpec as P

bf16 = jnp.bfloat16
f32 = jnp.float32
epsilon = 1e-06
score_scale = 0.125
log2e = 1.4426950408889634
low_score = -1e30
block = 256
mib = 1 << 20


def dot_nn(left, right):
    return lax.dot_general(left, right, (((1,), (0,)), ((), ())), preferred_element_type=f32)


def dot_nt(left, right):
    return lax.dot_general(left, right, (((1,), (1,)), ((), ())), preferred_element_type=f32)


def dot_tn(left, right):
    return lax.dot_general(left, right, (((0,), (0,)), ((), ())), preferred_element_type=f32)


def lane_halves(rows):
    lane = lax.broadcasted_iota(jnp.int32, rows.shape, 1)
    zero = jnp.zeros_like(rows)
    return jnp.where(lane < 64, rows, zero), jnp.where(lane < 64, zero, rows)


def attend_kernel(
    info, qo, ko, vo, qr, kr, vr, seg_col, seg_row, out_own, out_oth, lse_ref,
    qs, k0s, k1s, v0s, v1s, os,
):
    half = qo.shape[0]
    blocks = 2 * half // block
    side = info[0]
    own_at = pl.multiple_of(side * half, half)
    oth_at = pl.multiple_of((1 - side) * half, half)
    lane = lax.broadcasted_iota(jnp.int32, (half, 128), 1)
    for at, q_in, k_in, v_in in ((own_at, qo, ko, vo), (oth_at, qr, kr, vr)):
        rows = pl.ds(at, half)
        qs[rows, :] = q_in[...]
        k0s[rows, :], k1s[rows, :] = lane_halves(k_in[...])
        v_all = v_in[...]
        v0s[rows, :] = jnp.where(lane < 64, v_all, (lane == 64).astype(bf16))
        v1s[rows, :] = jnp.where(lane < 64, (lane == 0).astype(bf16), v_all)

    diff = lax.broadcasted_iota(jnp.int32, (block, block), 0) - lax.broadcasted_iota(
        jnp.int32, (block, block), 1
    )
    factor = score_scale * log2e

    def per_rows(qb, carry):
        q_at = pl.multiple_of(qb * block, block)
        q_rows = qs[pl.ds(q_at, block), :]
        q_seg = seg_col[pl.ds(q_at, block), :]

        def per_keys(kb, state):
            m0, m1, a0, a1 = state
            k_at = pl.multiple_of(kb * block, block)
            keys = pl.ds(k_at, block)
            mask = (q_seg == seg_row[0:1, keys]) | (diff == k_at - q_at)

            def one(k_ref, v_ref, m_old, acc):
                s = jnp.where(mask, dot_nt(q_rows, k_ref[keys, :]), low_score)
                m_new = jnp.maximum(m_old, jnp.max(s, axis=1, keepdims=True))
                p = jnp.exp2((s - m_new) * factor).astype(bf16)
                fade = jnp.exp2((m_old - m_new) * factor)
                return m_new, acc * fade + dot_nn(p, v_ref[keys, :])

            m0, a0 = one(k0s, v0s, m0, a0)
            m1, a1 = one(k1s, v1s, m1, a1)
            return m0, m1, a0, a1

        start = jnp.full((block, 1), low_score, f32)
        zero = jnp.zeros((block, 128), f32)
        m0, m1, a0, a1 = lax.fori_loop(
            info[1 + qb], info[1 + blocks + qb], per_keys, (start, start, zero, zero)
        )
        t0 = a0[:, 64:65]
        t1 = a1[:, 0:1]
        lane_q = lax.broadcasted_iota(jnp.int32, (block, 128), 1)
        os[pl.ds(q_at, block), :] = jnp.where(lane_q < 64, a0 / t0, a1 / t1).astype(bf16)
        both = jnp.where(
            lane_q < 64, m0 * factor + jnp.log2(t0), m1 * factor + jnp.log2(t1)
        )
        turned = both.T
        lse_ref[0, 0:1, pl.ds(q_at, block)] = turned[0:1, :]
        lse_ref[0, 1:2, pl.ds(q_at, block)] = turned[64:65, :]
        return carry

    lax.fori_loop(0, blocks, per_rows, 0)
    out_own[...] = os[pl.ds(own_at, half), :]
    out_oth[...] = os[pl.ds(oth_at, half), :]


def attend(info, own, oth, seg_col, seg_row):
    half = own.shape[0]
    rows = 2 * half
    pairs = own.shape[1] // 384

    def part(which):
        return pl.BlockSpec((half, 128), lambda i, _: (0, (i // 2) * 6 + which * 2 + i % 2))

    whole = lambda shape: pl.BlockSpec(shape, lambda i, _: (0,) * len(shape))
    return pl.pallas_call(
        attend_kernel,
        grid_spec=pltpu.PrefetchScalarGridSpec(
            num_scalar_prefetch=1,
            grid=(pairs,),
            in_specs=[part(0), part(1), part(2)] * 2 + [whole((rows, 1)), whole((1, rows))],
            out_specs=[
                pl.BlockSpec((half, 128), lambda i, _: (0, i)),
                pl.BlockSpec((half, 128), lambda i, _: (0, i)),
                pl.BlockSpec((1, 8, rows), lambda i, _: (i, 0, 0)),
            ],
            scratch_shapes=[pltpu.VMEM((rows, 128), bf16)] * 6,
        ),
        out_shape=(
            jax.ShapeDtypeStruct((half, pairs * 128), bf16),
            jax.ShapeDtypeStruct((half, pairs * 128), bf16),
            jax.ShapeDtypeStruct((pairs, 8, rows), f32),
        ),
        compiler_params=pltpu.CompilerParams(vmem_limit_bytes=32 * mib),
        cost_estimate=pl.CostEstimate(
            flops=int(pairs * 2 * rows * rows * 256 * 1.5), bytes_accessed=int(own.size * 5), transcendentals=0
        ),
        name="attend",
    )(info, own, own, own, oth, oth, oth, seg_col, seg_row)


def attend_back_kernel(
    info, qo, ko, vo, qr, kr, vr, go, gr, oo, orr, lse_ref, seg_col, seg_row,
    dqo, dko, dvo, dqr, dkr, dvr,
    q0s, q1s, k0s, k1s, v0s, v1s, g0s, g1s, os, dqs, dks, dvs,
):
    half = qo.shape[0]
    blocks = 2 * half // block
    side = info[0]
    own_at = pl.multiple_of(side * half, half)
    oth_at = pl.multiple_of((1 - side) * half, half)
    for at, q_in, k_in, v_in, g_in, o_in in (
        (own_at, qo, ko, vo, go, oo),
        (oth_at, qr, kr, vr, gr, orr),
    ):
        rows = pl.ds(at, half)
        q0s[rows, :], q1s[rows, :] = lane_halves(q_in[...])
        k0s[rows, :], k1s[rows, :] = lane_halves(k_in[...])
        v0s[rows, :], v1s[rows, :] = lane_halves(v_in[...])
        g0s[rows, :], g1s[rows, :] = lane_halves(g_in[...])
        os[rows, :] = o_in[...]
    dks[...] = jnp.zeros_like(dks)
    dvs[...] = jnp.zeros_like(dvs)

    diff = lax.broadcasted_iota(jnp.int32, (block, block), 1) - lax.broadcasted_iota(
        jnp.int32, (block, block), 0
    )
    factor = score_scale * log2e

    def per_rows(qb, carry):
        q_at = pl.multiple_of(qb * block, block)
        rows = pl.ds(q_at, block)
        g_sum = (g0s[rows, :] + g1s[rows, :]).astype(f32) * os[rows, :].astype(f32)
        turned = g_sum.T
        d0 = jnp.sum(turned[0:64, :], axis=0, keepdims=True)
        d1 = jnp.sum(turned[64:128, :], axis=0, keepdims=True)
        l0 = lse_ref[0, 0:1, rows]
        l1 = lse_ref[0, 1:2, rows]
        q_seg = seg_row[0:1, rows]
        q0, q1, g0, g1 = q0s[rows, :], q1s[rows, :], g0s[rows, :], g1s[rows, :]

        def per_keys(kb, dq):
            k_at = pl.multiple_of(kb * block, block)
            keys = pl.ds(k_at, block)
            mask = (q_seg == seg_col[keys, :]) | (diff == k_at - q_at)

            def one(q, g, k_ref, v_ref, lse, d):
                k = k_ref[keys, :]
                s = jnp.where(mask, dot_nt(k, q) * factor - lse, low_score)
                p = jnp.exp2(s)
                dv = dot_nn(p.astype(bf16), g)
                dp = dot_nt(v_ref[keys, :], g)
                ds = (p * (dp - d)).astype(bf16)
                return dv, dot_nn(ds, q), dot_tn(ds, k)

            dv_a, dk_a, dq_a = one(q0, g0, k0s, v0s, l0, d0)
            dv_b, dk_b, dq_b = one(q1, g1, k1s, v1s, l1, d1)
            dvs[keys, :] += dv_a + dv_b
            dks[keys, :] += dk_a + dk_b
            return dq + (dq_a + dq_b)

        dq = lax.fori_loop(
            info[1 + qb], info[1 + blocks + qb], per_keys, jnp.zeros((block, 128), f32)
        )
        dqs[rows, :] = dq
        return carry

    lax.fori_loop(0, blocks, per_rows, 0)
    for at, dq_out, dk_out, dv_out in ((own_at, dqo, dko, dvo), (oth_at, dqr, dkr, dvr)):
        rows = pl.ds(at, half)
        dq_out[...] = (dqs[rows, :] * score_scale).astype(bf16)
        dk_out[...] = (dks[rows, :] * score_scale).astype(bf16)
        dv_out[...] = dvs[rows, :].astype(bf16)


def attend_back(info, own, oth, g_own, g_oth, o_own, o_oth, lse, seg_row_k, seg_col_k):
    half = own.shape[0]
    rows = 2 * half
    pairs = own.shape[1] // 384

    def part(which):
        return pl.BlockSpec((half, 128), lambda i, _: (0, (i // 2) * 6 + which * 2 + i % 2))

    col = pl.BlockSpec((half, 128), lambda i, _: (0, i))
    whole = lambda shape: pl.BlockSpec(shape, lambda i, _: (0,) * len(shape))
    shape = jax.ShapeDtypeStruct((half, pairs * 128), bf16)
    return pl.pallas_call(
        attend_back_kernel,
        grid_spec=pltpu.PrefetchScalarGridSpec(
            num_scalar_prefetch=1,
            grid=(pairs,),
            in_specs=[part(0), part(1), part(2)] * 2
            + [col] * 4
            + [pl.BlockSpec((1, 8, rows), lambda i, _: (i, 0, 0))]
            + [whole((rows, 1)), whole((1, rows))],
            out_specs=[col] * 6,
            scratch_shapes=[pltpu.VMEM((rows, 128), bf16)] * 9 + [pltpu.VMEM((rows, 128), f32)] * 3,
        ),
        out_shape=(shape,) * 6,
        compiler_params=pltpu.CompilerParams(vmem_limit_bytes=40 * mib),
        cost_estimate=pl.CostEstimate(
            flops=int(pairs * 5 * rows * rows * 256), bytes_accessed=int(own.size * 10), transcendentals=0
        ),
        name="attend_back",
    )(info, own, own, own, oth, oth, oth, g_own, g_oth, o_own, o_oth, lse, seg_col_k, seg_row_k)


def plan_gather(loads, bits, n_t, rows_load):
    tasks = {}
    for w, load in enumerate(loads):
        for s in range(n_t):
            last = None
            if s:
                last = (w, s, "z")
                tasks[last] = (None if s == 1 else (w, s - 1, "z"), "z", load)
            middle = list(range(1, bits))
            for k, bit in enumerate((middle if (w + s) % 2 == 0 else middle[::-1]) + [0]):
                tasks[(w, s, k)] = (last, bit, load << k)
                last = (w, s, k)
    for q in range(2):
        tasks[("rows", q, 0)] = (None, "z", rows_load)
    free, done, waiting = {}, {}, list(tasks)
    while waiting:
        ready = [
            (0.0 if tasks[t][0] is None else done[tasks[t][0]], i, t)
            for i, t in enumerate(waiting)
            if tasks[t][0] is None or tasks[t][0] in done
        ]
        start, _, task = min((max(r, free.get(tasks[t][1], 0.0)), i, t) for r, i, t in ready)
        _, link, load = tasks[task]
        done[task] = start + load / (300e3 if link == 0 else 44e3) + 1.0
        free[link] = done[task] - 1.0
        waiting.remove(task)
    order = sorted(done, key=lambda t: done[t])
    return {t: tasks[t][0] for t in order}, order


def gather_kernel(n_dp, n_t, count, parents, arrivals, *refs):
    rows_ref, own = refs[0], refs[1 : 1 + count]
    rows_out, outs = refs[1 + count], refs[2 + count : 2 + 2 * count]
    send, recv, near = refs[2 + 2 * count :]
    bits = n_dp.bit_length() - 1
    me, z = lax.axis_index("dp"), lax.axis_index("tensor")
    side = lax.rem(me, 2)
    base = me - side
    number = {task: i for i, task in enumerate(arrivals)}

    greet(n_t, bits, me, z)
    flips = [bit_flip(me, bit) for bit in range(bits)]

    def slot(w, s, index):
        cols = own[w].shape[1]
        return outs[w].at[index + (slice(None), pl.ds(s * cols, cols))]

    def copy_of(task):
        w, s, k = task
        i = number[task]
        if k == "z":
            src = own[w] if s == 1 else slot(w, s - 1, (0,) * bits)
            dst = slot(w, s, (0,) * bits)
            where = (me, lax.rem(z + 1, n_t))
        else:
            middle = list(range(1, bits))
            order = (middle if (w + s) % 2 == 0 else middle[::-1]) + [0]
            bit = order[k]
            src_at, dst_at = [], []
            for axis in range(bits):
                if axis == bit:
                    src_at.append(0)
                    dst_at.append(1)
                else:
                    held = slice(None) if axis in order[:k] else 0
                    src_at.append(held)
                    dst_at.append(held)
            src = own[w] if (k == 0 and s == 0) else slot(w, s, tuple(src_at))
            dst = slot(w, s, tuple(dst_at))
            where = (flips[bit], z)
        return pltpu.make_async_remote_copy(
            src_ref=src, dst_ref=dst, send_sem=send.at[i], recv_sem=recv.at[i],
            device_id=where, device_id_type=pl.DeviceIdType.MESH,
        )

    placed = []
    for w in range(count):
        placed.append(pltpu.make_async_copy(own[w], slot(w, 0, (0,) * bits), near.at[w]))
        placed[-1].start()

    place = lax.rem(z, 2)
    target_core = base + z // 2

    def rows_copy(m):
        i = [number[("rows", q, 0)] for q in range(2)]
        where = (target_core, 2 * m + side)
        mine = (side == z // 2) & (z == 2 * m + side)
        return i, where, mine

    def start_rows():
        for m in range(2):
            i, where, mine = rows_copy(m)
            for q in range(2):

                @pl.when((place == q) & mine)
                def _():
                    pltpu.make_async_copy(rows_ref.at[m], rows_out.at[q], recv.at[i[q]]).start()

                @pl.when((place == q) & jnp.logical_not(mine))
                def _():
                    pltpu.make_async_remote_copy(
                        src_ref=rows_ref.at[m], dst_ref=rows_out.at[q], send_sem=near.at[count + m],
                        recv_sem=recv.at[i[q]], device_id=where, device_id_type=pl.DeviceIdType.MESH,
                    ).start()

    copies = {task: copy_of(task) for task in arrivals if task[0] != "rows"}
    for task in arrivals:
        if task[0] != "rows" and parents[task] is None:
            copies[task].start()
    start_rows()
    landed = {w: False for w in range(count)}
    for task in arrivals:
        if task[0] == "rows":
            q = task[1]
            pltpu.make_async_copy(rows_ref.at[0], rows_out.at[q], recv.at[number[task]]).wait()
            continue
        copies[task].wait_recv()
        for child in arrivals:
            if parents[child] == task:
                if child[1] == 0 and not landed[child[0]]:
                    placed[child[0]].wait()
                    landed[child[0]] = True
                copies[child].start()
    for w in range(count):
        if not landed[w]:
            placed[w].wait()
    for task in arrivals:
        if task[0] != "rows":
            copies[task].wait_send()
    for m in range(2):
        i, where, mine = rows_copy(m)

        @pl.when(jnp.logical_not(mine))
        def _():
            pltpu.make_async_remote_copy(
                src_ref=rows_ref.at[m], dst_ref=rows_out.at[0], send_sem=near.at[count + m],
                recv_sem=recv.at[i[0]], device_id=where, device_id_type=pl.DeviceIdType.MESH,
            ).wait_send()


def bit_flip(me, bit):
    span = 1 << bit
    return me + span - 2 * span * lax.rem(me // span, 2)


def gather_all(rows, own, n_dp, n_t):
    bits = n_dp.bit_length() - 1
    parents, arrivals = plan_gather(
        [w.shape[0] * w.shape[1] * 2 for w in own], bits, n_t, rows[0].size * 2
    )
    count = len(own)
    hbm = pl.BlockSpec(memory_space=pl.ANY)
    return pl.pallas_call(
        functools.partial(gather_kernel, n_dp, n_t, count, parents, arrivals),
        in_specs=[hbm] * (1 + count),
        out_specs=[hbm] * (1 + count),
        out_shape=(jax.ShapeDtypeStruct(rows.shape, rows.dtype),)
        + tuple(
            jax.ShapeDtypeStruct((2,) * bits + (w.shape[0], n_t * w.shape[1]), w.dtype) for w in own
        ),
        scratch_shapes=[
            pltpu.SemaphoreType.DMA((len(arrivals),)),
            pltpu.SemaphoreType.DMA((len(arrivals),)),
            pltpu.SemaphoreType.DMA((count + 2,)),
        ],
        compiler_params=pltpu.CompilerParams(collective_id=0, has_side_effects=True),
        cost_estimate=pl.CostEstimate(flops=0, bytes_accessed=300 * mib, transcendentals=0),
        name="gather_all",
    )(rows, *own)


def stage_bits(w, s, bits):
    middle = list(range(1, bits))
    return [0] + (middle if (w + s) % 2 == 0 else middle[::-1])


def plan_reduce(widths, size, bits, n_t, rows_load):
    turn = list(range(1, n_t)) + [0]
    last = len(widths)
    chunks = [(last, s) for s in turn] + [(w, s) for w in range(last) for s in turn]
    ready, free, core, order = {}, {"z": rows_load / 44e3}, 0.0, []
    pending = {("make", w, s): 0.0 for w, s in chunks}
    rank = {c: i for i, c in enumerate(chunks)}
    arrived = {}
    while pending:
        def key(item):
            kind, w, s = item[0][0], item[0][1], item[0][2]
            begin = max(core, item[1])
            return (begin, kind == "make", rank[(w, s)])

        action, when = min(pending.items(), key=key)
        del pending[action]
        order.append(action)
        w, s = action[1], action[2]
        cols = 64 if w == last else widths[w]
        rows = 16 if w == last else size << (bits - 1)
        share = rows * cols / (512 * 1024)
        begin = max(core, when)
        core = begin + (4.5 * share if action[0] == "make" else 1.2 * share / (1 << action[3] if action[0] == "add" else 4) + 0.3)
        flow = stage_bits(w, s, bits)
        k = 0 if action[0] == "make" else action[3] + 1 if action[0] == "add" else None

        def send(link, load):
            begin = max(core, free.get(link, 0.0))
            free[link] = begin + load / (300e3 if link == 0 else 44e3)
            return free[link] + 2.0

        def to_z():
            if s != 0:
                nxt = turn[turn.index(s) + 1]
                arrived[(w, nxt)] = send("z", (rows >> (bits - 1)) * cols * 2)
                if (w, nxt) in ready:
                    pending[("z", w, nxt)] = arrived[(w, nxt)]

        if k is not None and k < bits:
            load = (rows >> k) * cols * 2
            pending[("add", w, s, k)] = send(flow[k], load)
        elif k is not None:
            ready[(w, s)] = core
            if s == turn[0]:
                to_z()
            elif (w, s) in arrived:
                pending[("z", w, s)] = arrived[(w, s)]
        else:
            to_z()
    return order


def greet(n_t, bits, me, z):
    side = lax.rem(me, 2)
    barrier = pltpu.get_barrier_semaphore()
    for dz in range(n_t):
        for other in range(2):
            if dz or other:
                where = (me - side + lax.rem(side + other, 2), lax.rem(z + dz, n_t))
                pl.semaphore_signal(barrier, inc=1, device_id=where, device_id_type=pl.DeviceIdType.MESH)
    for bit in range(1, bits):
        where = (bit_flip(me, bit), z)
        pl.semaphore_signal(barrier, inc=1, device_id=where, device_id_type=pl.DeviceIdType.MESH)
    pl.semaphore_wait(barrier, 2 * n_t - 1 + bits - 1)


def reduce_kernel(n_dp, n_t, plan, widths, *refs):
    bits = n_dp.bit_length() - 1
    count = len(widths)
    refs = list(refs)
    take = lambda n: [refs.pop(0) for _ in range(n)]
    xs, gs, (small_in, rows_in) = take(count), take(count), take(2)
    outs, (small_out, rows_out) = take(count), take(2)
    kept, came, zcame = take(count + 1), take(count + 1), take(count + 1)
    later = [take(bits - 1) for _ in range(count + 1)]
    (away, away_small, x_buf, x_turn, g_buf) = take(5)
    (x_sem, g_sem, s_sem, r_sem, send, recv, zsend, zrecv) = take(8)
    me, z = lax.axis_index("dp"), lax.axis_index("tensor")
    turn = list(range(1, n_t)) + [0]
    blk = kept[0].shape[-2]
    tall = blk << (bits - 1)
    greet(n_t, bits, me, z)

    side = lax.rem(me, 2)
    micro, owner = z // 2, lax.rem(z, 2)

    def rows_to(q):
        where = (me - side + owner, 2 * side + q)
        mine = (owner == side) & (2 * side + q == z)
        return where, mine

    def rows_from(m):
        return (side == z // 2) & (2 * m + side == z)

    for q in range(2):
        where, mine = rows_to(q)
        for m in range(2):

            @pl.when((micro == m) & mine)
            def _():
                pltpu.make_async_copy(rows_in.at[q], rows_out.at[m], r_sem.at[2 + m]).start()

            @pl.when((micro == m) & jnp.logical_not(mine))
            def _():
                pltpu.make_async_remote_copy(
                    src_ref=rows_in.at[q], dst_ref=rows_out.at[m], send_sem=r_sem.at[q],
                    recv_sem=r_sem.at[2 + m], device_id=where, device_id_type=pl.DeviceIdType.MESH,
                ).start()

    made = [a for a in plan if a[0] == "make" and a[1] < count]

    def fetch(i):
        _, w, s = made[i]
        c = widths[w]
        return pltpu.make_async_copy(
            gs[w].at[:, pl.ds(s * c, c)], g_buf.at[i % 2, :, pl.ds(0, c)], g_sem.at[i % 2]
        )

    def fetch_x(w):
        return pltpu.make_async_copy(xs[w], x_buf, x_sem)

    def at_stage(w, s, k, taken):
        flow = stage_bits(w, s, bits)
        return tuple(
            0 if bit in flow[:k] else (taken if bit == flow[k] else slice(None)) for bit in range(1, bits)
        )

    def landing(w, s, k):
        ref = came[w] if k == 0 else later[w][k - 1]
        return ref.at[s]

    def copy_of(w, s, k):
        flow = stage_bits(w, s, bits)
        if k == 0:
            src = away_small.at[s] if w == count else away_view(w, s)
        else:
            src = kept[w].at[(s,) + at_stage(w, s, k, 1)]
        return pltpu.make_async_remote_copy(
            src_ref=src, dst_ref=landing(w, s, k), send_sem=send.at[w, s, k], recv_sem=recv.at[w, s, k],
            device_id=(bit_flip(me, flow[k]), z), device_id_type=pl.DeviceIdType.MESH,
        )

    def away_view(w, s):
        i = made.index(("make", w, s)) % 2
        return away.at[(i,) + (slice(None),) * bits + (pl.ds(0, widths[w]),)]

    def zcopy(w, s):
        nxt = turn[turn.index(s) + 1]
        return pltpu.make_async_remote_copy(
            src_ref=kept[w].at[(s,) + (0,) * (bits - 1)], dst_ref=zcame[w].at[nxt],
            send_sem=zsend.at[w, s], recv_sem=zrecv.at[w, nxt],
            device_id=(me, lax.rem(z + 1, n_t)), device_id_type=pl.DeviceIdType.MESH,
        )

    def finish(w, s, total):
        ref = small_out if w == count else outs[w]
        ref[...] = total

    last_of = {}
    for i, (_, w, s) in enumerate(made):
        last_of[w] = i
    fetch(0).start()
    fetch_x(made[0][1]).start()
    loaded = set()
    for action in plan:
        kind, w, s = action[:3]
        if kind == "make" and w == count:
            lanes = small_out.shape[-1]
            cols = pl.ds(s * lanes, lanes)
            for half, dst in ((1, away_small.at[s]), (0, kept[w].at[s])):
                src = small_in.at[(half,) + (slice(None),) * bits + (cols,)]
                pltpu.make_async_copy(src, dst, s_sem.at[half]).start()
            for half, dst in ((1, away_small.at[s]), (0, kept[w].at[s])):
                src = small_in.at[(half,) + (slice(None),) * bits + (cols,)]
                pltpu.make_async_copy(src, dst, s_sem.at[half]).wait()
            copy_of(w, s, 0).start()
        elif kind == "make":
            i = made.index(action)
            c = widths[w]
            if w not in loaded:
                loaded.add(w)
                fetch_x(w).wait()
                for a in range(x_buf.shape[1] // 256):

                    def turn_block(b, carry, a=a):
                        rows = pl.ds(pl.multiple_of(b * 256, 256), 256)
                        x_turn[a * 256 : (a + 1) * 256, rows] = x_buf[rows, a * 256 : (a + 1) * 256].T
                        return carry

                    lax.fori_loop(0, x_buf.shape[0] // 256, turn_block, 0)
                if i + n_t < len(made):
                    fetch_x(made[i + n_t][1]).start()
            fetch(i).wait()
            if i + 1 < len(made):
                fetch(i + 1).start()
            if i >= 2:
                copy_of(*made[i - 2][1:], 0).wait_send()
            whole = (slice(None),) * bits

            def away_block(n, carry):
                cols = pl.ds(pl.multiple_of(n * 256, 256), 256)
                value = dot_nn(x_turn[tall:, :], g_buf[i % 2, :, cols]).astype(bf16)
                away[(i % 2,) + whole + (cols,)] = value.reshape((2,) * (bits - 1) + (blk, 256))
                return carry

            lax.fori_loop(0, c // 256, away_block, 0)
            copy_of(w, s, 0).start()

            def kept_block(n, carry):
                cols = pl.ds(pl.multiple_of(n * 256, 256), 256)
                value = dot_nn(x_turn[:tall, :], g_buf[i % 2, :, cols]).astype(bf16)
                kept[w][(s,) + whole + (cols,)] = value.reshape((2,) * (bits - 1) + (blk, 256))
                return carry

            lax.fori_loop(0, c // 256, kept_block, 0)
        elif kind == "add":
            k = action[3]
            copy_of(w, s, k).wait_recv()
            place = (s,) + (slice(None),) * (bits - 1) if k == 0 else (s,) + at_stage(w, s, k, 0)
            got = (came[w] if k == 0 else later[w][k - 1])[s]
            held = kept[w][place]
            kept[w][place] = (held.astype(f32) + got.astype(f32)).astype(held.dtype)
            if k + 1 < bits:
                copy_of(w, s, k + 1).start()
            elif s == turn[0]:
                zcopy(w, s).start()
        else:
            before = turn[turn.index(s) - 1]
            zcopy(w, before).wait_recv()
            place = (s,) + (0,) * (bits - 1)
            total = kept[w][place].astype(f32) + zcame[w][s].astype(f32)
            if s == turn[-1]:
                finish(w, s, total)
            else:
                kept[w][place] = total.astype(kept[w].dtype)
                zcopy(w, s).start()
    for w in range(count + 1):
        for s in turn:
            for k in range(bits):
                if k == 0 and w < count and made.index(("make", w, s)) < len(made) - 2:
                    continue
                copy_of(w, s, k).wait_send()
            if s != turn[-1]:
                zcopy(w, s).wait_send()
    for q in range(2):
        where, mine = rows_to(q)

        @pl.when(jnp.logical_not(mine))
        def _():
            pltpu.make_async_remote_copy(
                src_ref=rows_in.at[q], dst_ref=rows_out.at[0], send_sem=r_sem.at[q],
                recv_sem=r_sem.at[2], device_id=where, device_id_type=pl.DeviceIdType.MESH,
            ).wait_send()
    for m in range(2):
        pltpu.make_async_copy(rows_in.at[0], rows_out.at[m], r_sem.at[2 + m]).wait()


def reduce_all(xs, gs, small, rows, n_dp, n_t):
    bits = n_dp.bit_length() - 1
    count = len(xs)
    width = xs[0].shape[1]
    size = width // n_dp
    widths = [g.shape[1] // n_t for g in gs]
    lanes = small.shape[-1] // n_t
    plan = plan_reduce(widths, size, bits, n_t, rows[0].size * 2)
    cells = (2,) * (bits - 1)
    shapes = [(size, c, bf16) for c in widths] + [(small.shape[-2], lanes, f32)]
    hbm, vmem = pl.BlockSpec(memory_space=pl.ANY), pl.BlockSpec(memory_space=pltpu.VMEM)
    scratch = [pltpu.VMEM((n_t,) + cells + (r, c), t) for r, c, t in shapes]
    scratch += [pltpu.VMEM((n_t,) + cells + (r, c), t) for r, c, t in shapes]
    scratch += [pltpu.VMEM((n_t, r, c), t) for r, c, t in shapes]
    for r, c, t in shapes:
        scratch += [pltpu.VMEM((n_t,) + (2,) * (bits - 1 - k) + (r, c), t) for k in range(1, bits)]
    scratch += [
        pltpu.VMEM((2,) + cells + (size, max(widths)), bf16),
        pltpu.VMEM((n_t,) + cells + (small.shape[-2], lanes), f32),
        pltpu.VMEM(xs[0].shape, bf16),
        pltpu.VMEM((width, xs[0].shape[0]), bf16),
        pltpu.VMEM((2, gs[0].shape[0], max(widths)), bf16),
        pltpu.SemaphoreType.DMA,
        pltpu.SemaphoreType.DMA((2,)),
        pltpu.SemaphoreType.DMA((2,)),
        pltpu.SemaphoreType.DMA((4,)),
        pltpu.SemaphoreType.DMA((count + 1, n_t, bits)),
        pltpu.SemaphoreType.DMA((count + 1, n_t, bits)),
        pltpu.SemaphoreType.DMA((count + 1, n_t)),
        pltpu.SemaphoreType.DMA((count + 1, n_t)),
    ]
    return pl.pallas_call(
        functools.partial(reduce_kernel, n_dp, n_t, plan, widths),
        in_specs=[hbm] * (2 * count + 2),
        out_specs=[vmem] * (count + 1) + [hbm],
        out_shape=tuple(jax.ShapeDtypeStruct((size, c), f32) for c in widths)
        + (
            jax.ShapeDtypeStruct((small.shape[-2], lanes), f32),
            jax.ShapeDtypeStruct(rows.shape, rows.dtype),
        ),
        scratch_shapes=scratch,
        compiler_params=pltpu.CompilerParams(
            collective_id=1, has_side_effects=True, vmem_limit_bytes=60 * mib
        ),
        cost_estimate=pl.CostEstimate(
            flops=2 * xs[0].size * n_t * sum(widths), bytes_accessed=200 * mib, transcendentals=0
        ),
        name="reduce_all",
    )(*xs, *gs, small, rows)


def ingest_kernel(order, a_ref, b_ref, o_ref):
    rows, width = a_ref.shape
    count = order.shape[0] - 1
    size = width // count
    first = order[count]
    for place in range(count):
        src = pl.ds(pl.multiple_of(order[place] * size, size), size)
        dst = slice(place * size, (place + 1) * size)

        @pl.when(first == 0)
        def _():
            o_ref[0:rows, dst] = a_ref[:, src]
            o_ref[rows : 2 * rows, dst] = b_ref[:, src]

        @pl.when(first != 0)
        def _():
            o_ref[0:rows, dst] = b_ref[:, src]
            o_ref[rows : 2 * rows, dst] = a_ref[:, src]

    o_ref[2 * rows :, :] = jnp.zeros((o_ref.shape[0] - 2 * rows, width), o_ref.dtype)


def ingest(order, first, a, b, padded):
    rows, width = a.shape
    count = order.shape[0]
    if width // count % 128:
        both = jnp.where(first == 0, jnp.concatenate([a, b]), jnp.concatenate([b, a]))
        both = jnp.take(both.reshape(2 * rows, count, -1), order, axis=1).reshape(2 * rows, width)
        return jnp.pad(both, ((0, padded - 2 * rows), (0, 0)))
    scalars = jnp.concatenate([order, first[None]]).astype(jnp.int32)
    return pl.pallas_call(
        ingest_kernel,
        grid_spec=pltpu.PrefetchScalarGridSpec(
            num_scalar_prefetch=1,
            grid=(1,),
            in_specs=[pl.BlockSpec((rows, width), lambda i, _: (0, 0))] * 2,
            out_specs=pl.BlockSpec((padded, width), lambda i, _: (0, 0)),
        ),
        out_shape=jax.ShapeDtypeStruct((padded, width), a.dtype),
        compiler_params=pltpu.CompilerParams(vmem_limit_bytes=20 * mib),
        name="ingest",
    )(scalars, a, b)


def egress_kernel(order, x_ref, a_ref, b_ref):
    rows, width = a_ref.shape
    count = order.shape[0] - 1
    size = width // count
    first = order[count]
    for place in range(count):
        dst = pl.ds(pl.multiple_of(order[place] * size, size), size)
        src = slice(place * size, (place + 1) * size)

        @pl.when(first == 0)
        def _():
            a_ref[:, dst] = x_ref[0:rows, src]
            b_ref[:, dst] = x_ref[rows : 2 * rows, src]

        @pl.when(first != 0)
        def _():
            b_ref[:, dst] = x_ref[0:rows, src]
            a_ref[:, dst] = x_ref[rows : 2 * rows, src]


def egress(order, inverse, first, x, rows):
    width = x.shape[1]
    count = order.shape[0]
    if width // count % 128:
        both = jnp.take(x.reshape(-1, count, width // count), inverse, axis=1).reshape(-1, width)
        top, low = both[:rows], both[rows : 2 * rows]
        return jnp.where(first == 0, top, low), jnp.where(first == 0, low, top)
    scalars = jnp.concatenate([order, first[None]]).astype(jnp.int32)
    return pl.pallas_call(
        egress_kernel,
        grid_spec=pltpu.PrefetchScalarGridSpec(
            num_scalar_prefetch=1,
            grid=(1,),
            in_specs=[pl.BlockSpec(x.shape, lambda i, _: (0, 0))],
            out_specs=[pl.BlockSpec((rows, width), lambda i, _: (0, 0))] * 2,
        ),
        out_shape=(jax.ShapeDtypeStruct((rows, width), x.dtype),) * 2,
        compiler_params=pltpu.CompilerParams(vmem_limit_bytes=20 * mib),
        name="egress",
    )(scalars, x)


def norm_parts(operand):
    centred = operand - jnp.mean(operand, axis=-1, keepdims=True)
    inverse = lax.rsqrt(jnp.mean(centred * centred, axis=-1, keepdims=True) + epsilon)
    return centred * inverse, inverse


def norm_back(scaled, normed, inverse):
    return inverse * (
        scaled
        - jnp.mean(scaled, axis=-1, keepdims=True)
        - normed * jnp.mean(scaled * normed, axis=-1, keepdims=True)
    )


def make_body(n_dp, n_t):
    bits = n_dp.bit_length() - 1
    reverse = [int(format(i, "b").zfill(bits)[::-1], 2) for i in range(n_dp)]
    axes = ("dp", "tensor")

    def at(dp, t):
        return dp * n_t + t

    go_a, go_b = [], []
    for dp in range(n_dp):
        c, base = dp % 2, dp - dp % 2
        for j in range(n_t):
            go_a.append((at(dp, j), at(base + j // 2, 2 * (j % 2) + c)))
            go_b.append((at(dp, j), at(base + j // 2, 2 * (1 - j % 2) + c)))
    back_a = [(d, s) for s, d in go_a]
    back_b = [(d, s) for s, d in go_b]
    ring = [(j, (j + 1) % n_t) for j in range(n_t)]

    def swap(value, bit):
        return lax.ppermute(value, "dp", [(i, i ^ (1 << bit)) for i in range(n_dp)])

    def step_z(value):
        return lax.ppermute(value, "tensor", ring)

    def body(
        tokens, segment_ids, pad_mask, cotangent, ln1_gain, ln1_bias, qkv_weight, qv_bias,
        proj_weight, proj_bias, ln2_gain, ln2_bias, fc1_weight, fc1_bias, fc2_weight, fc2_bias,
    ):
        me = lax.axis_index("dp")
        z = lax.axis_index("tensor")
        side = me % 2
        quarter, width = tokens.shape[2], tokens.shape[3]
        length = segment_ids.shape[2]
        half = -(-2 * quarter // block) * block
        size = width // n_dp
        micro = z // 2
        odd = z % 2
        order = jnp.stack([me ^ reverse[p] for p in range(n_dp)]).astype(jnp.int32)
        inverse = jnp.stack(
            [sum((((me ^ d) >> b) & 1) << (bits - 1 - b) for b in range(bits)) for d in range(n_dp)]
        ).astype(jnp.int32)

        def bring(array):
            a = lax.ppermute(lax.dynamic_index_in_dim(array[:, 0], odd, 0, False), axes, go_a)
            b = lax.ppermute(lax.dynamic_index_in_dim(array[:, 0], 1 - odd, 0, False), axes, go_b)
            return ingest(order, micro, a, b, half)

        def give(x):
            a, b = egress(order, inverse, micro, x, quarter)
            a = lax.ppermute(a, axes, back_a)
            b = lax.ppermute(b, axes, back_b)
            return jnp.where(odd == 0, jnp.stack([a, b]), jnp.stack([b, a]))[:, None]

        lanes = max(128, size)

        def row_of(v):
            return jnp.pad(v.reshape(1, -1), ((0, 0), (0, lanes - v.size)))

        fields = [ln1_gain, ln1_bias, proj_bias, ln2_gain, ln2_bias, fc2_bias, fc1_bias, qv_bias]
        packed = jnp.concatenate([row_of(v) for v in fields] + [jnp.zeros((8, lanes), bf16)])
        rows_in, w_qkv, w_fc1, w_fc2, w_proj, small = gather_all(
            tokens[:, 0],
            (qkv_weight.reshape(size, -1), fc1_weight, fc2_weight.T, proj_weight.T, packed),
            n_dp, n_t,
        )

        w_qkv, w_fc1, w_fc2, w_proj = [w.reshape(width, -1) for w in (w_qkv, w_fc1, w_fc2, w_proj)]
        x_low = ingest(order, jnp.int32(0), rows_in[0], rows_in[1], half)

        small = small.reshape(n_dp, packed.shape[0], n_t, lanes).astype(f32)
        gain_one, shift_one, proj_shift, gain_two, shift_two, fc2_shift = [
            small[:, i, 0, :size].reshape(-1) for i in range(6)
        ]
        ordered = jnp.take(small[:, 6:8], inverse, axis=0)
        fc1_shift = jnp.transpose(ordered[:, 0, :, :size], (1, 0, 2)).reshape(-1)
        heads_t, hd = qv_bias.shape[1], qv_bias.shape[2] * n_dp
        qv = ordered[:, 1, :, : qv_bias.size].reshape(n_dp, n_t, 2, heads_t, hd // n_dp)
        qv = jnp.transpose(qv, (1, 2, 3, 0, 4)).reshape(n_t, 2, heads_t * hd)
        qkv_shift = jnp.stack([qv[:, 0], jnp.zeros_like(qv[:, 0]), qv[:, 1]], axis=1).reshape(-1)

        which = z % 2
        packed_ids = jnp.stack([segment_ids[:, 0], pad_mask[:, 0]])
        packed_oth = swap(packed_ids, 0)
        ids = jnp.where(which == side, packed_ids, packed_oth)
        ids = lax.dynamic_index_in_dim(ids, micro, 1, False)
        seg, live = ids[0], ids[1]
        gap = half - length // 2

        def stretch(v, fill):
            return jnp.pad(v.reshape(2, -1), ((0, 0), (0, gap)), constant_values=fill).reshape(-1)

        q_ids = stretch(seg, -1)
        k_ids = stretch(jnp.where(live == 1, seg, -2), -2)
        per_half = half // block
        first_pos = jnp.array([h * (length // 2) + b * block for h in range(2) for b in range(per_half)])
        last_pos = jnp.array(
            [min(h * (length // 2) + (b + 1) * block, (h + 1) * (length // 2)) - 1 for h in range(2) for b in range(per_half)]
        )
        lo = jnp.sum((seg[None, :] < seg[first_pos][:, None]).astype(jnp.int32), axis=1)
        hi = jnp.sum((seg[None, :] <= seg[last_pos][:, None]).astype(jnp.int32), axis=1) - 1
        place = lambda v: jnp.where(v >= length // 2, v + gap, v) // block
        info = jnp.concatenate([side[None], place(lo), place(hi) + 1]).astype(jnp.int32)

        x = x_low.astype(f32)
        hat_one, inv_one = norm_parts(x)
        rows_one = (hat_one * gain_one + shift_one).astype(bf16)
        qkv = (dot_nn(rows_one, w_qkv) + qkv_shift).astype(bf16)
        qkv = (qkv[:, : qkv.shape[1] // 2], qkv[:, qkv.shape[1] // 2 :])
        own = jnp.where(side == 0, qkv[0], qkv[1])
        oth = swap(jnp.where(side == 0, qkv[1], qkv[0]), 0)
        o_own, o_oth, lse = attend(info, own, oth, q_ids[:, None], k_ids[None, :])
        o_came = swap(o_oth, 0)
        heads = jnp.where(
            side == 0, jnp.concatenate([o_own, o_came], axis=1), jnp.concatenate([o_came, o_own], axis=1)
        )
        hidden = x + (dot_nt(heads, w_proj) + proj_shift)
        hat_two, inv_two = norm_parts(hidden)
        rows_two = (hat_two * gain_two + shift_two).astype(bf16)
        pre = dot_nn(rows_two, w_fc1) + fc1_shift
        cdf = 0.5 * (1.0 + lax.erf(pre * 0.7071067811865476))
        act = (pre * cdf).astype(bf16)
        slope = (cdf + pre * jnp.exp(-0.5 * pre * pre) * 0.3989422804014327).astype(bf16)
        y = hidden + (dot_nt(act, w_fc2) + fc2_shift)
        out = give(y.astype(bf16))

        gy_low = bring(cotangent)
        gy = gy_low.astype(f32)
        fc2_shift_grad = jnp.sum(gy, axis=0)
        g_pre = (dot_nn(gy_low, w_fc2) * slope.astype(f32)).astype(bf16)
        cut = lambda v: (v[:, : v.shape[1] // 2], v[:, v.shape[1] // 2 :])
        fc1_shift_grad = jnp.sum(g_pre, axis=0, dtype=f32)
        g_c = dot_nt(g_pre, w_fc1)
        gain_two_grad = jnp.sum(g_c * hat_two, axis=0)
        shift_two_grad = jnp.sum(g_c, axis=0)
        g_hidden = gy + norm_back(g_c * gain_two, hat_two, inv_two)
        g_attn = g_hidden.astype(bf16)
        proj_shift_grad = jnp.sum(g_attn, axis=0, dtype=f32)
        g_heads = cut(dot_nn(g_attn, w_proj).astype(bf16))
        g_own = jnp.where(side == 0, g_heads[0], g_heads[1])
        g_oth = swap(jnp.where(side == 0, g_heads[1], g_heads[0]), 0)
        parts = attend_back(
            info, own, oth, g_own, g_oth, o_own, o_oth, lse, q_ids[None, :], k_ids[:, None]
        )

        def join(q, k, v):
            wide_t = q.shape[1] // 2
            return jnp.concatenate([p[:, i * wide_t : (i + 1) * wide_t] for i in range(2) for p in (q, k, v)], axis=1)

        d_own = join(*parts[:3])
        d_came = swap(join(*parts[3:]), 0)
        d_qkv = jnp.where(
            side == 0, jnp.concatenate([d_own, d_came], axis=1), jnp.concatenate([d_came, d_own], axis=1)
        )
        qkv_sum = jnp.sum(d_qkv, axis=0, dtype=f32).reshape(n_t, 3, -1)
        g_a = dot_nt(d_qkv, w_qkv)
        gain_one_grad = jnp.sum(g_a * hat_one, axis=0)
        shift_one_grad = jnp.sum(g_a, axis=0)
        grad_rows = (g_hidden + norm_back(g_a * gain_one, hat_one, inv_one)).astype(bf16)
        grad_rows = jnp.stack(egress(order, inverse, jnp.int32(0), grad_rows, quarter))

        fields = [gain_one_grad, shift_one_grad, proj_shift_grad, gain_two_grad, shift_two_grad, fc2_shift_grad]
        wide_g = jnp.stack(fields).reshape(6, n_dp, 1, size)
        wide_g = jnp.transpose(jnp.broadcast_to(wide_g, (6, n_dp, n_t, size)), (1, 0, 2, 3))
        fc1_g = jnp.transpose(fc1_shift_grad.reshape(n_t, n_dp, 1, size), (1, 2, 0, 3))
        qv_g = jnp.stack([qkv_sum[:, 0], qkv_sum[:, 2]], axis=1).reshape(n_t, 2, heads_t, n_dp, -1)
        qv_g = jnp.transpose(qv_g, (3, 0, 1, 2, 4)).reshape(n_dp, 1, n_t, -1)
        pad = lambda v: jnp.pad(v, ((0, 0), (0, 0), (0, 0), (0, lanes - v.shape[-1])))
        hidden_g = jnp.take(jnp.concatenate([pad(fc1_g), pad(qv_g)], axis=1), order, axis=0)
        small_g = jnp.concatenate([pad(wide_g), hidden_g], axis=1)
        small_g = small_g.reshape((2,) * bits + (8, n_t * lanes))

        fc2_grad, fc1_grad, qkv_grad, proj_grad, small_sum, tokens_grad = reduce_all(
            (gy_low, rows_two, rows_one, g_attn), (act, g_pre, d_qkv, heads), small_g, grad_rows, n_dp, n_t
        )
        wide_g = [small_sum[i, :size] for i in range(6)]
        fc1_g = small_sum[6:7, :size]
        qv_g = small_sum[7, : qv_bias.size].reshape(qv_bias.shape)
        return (
            out,
            tokens_grad[:, None],
            wide_g[0],
            wide_g[1],
            qkv_grad.reshape(qkv_weight.shape),
            qv_g,
            proj_grad.T,
            wide_g[2],
            wide_g[3],
            wide_g[4],
            fc1_grad,
            fc1_g,
            fc2_grad.T,
            wide_g[5],
        )

    return body


def solution(mesh):
    in_specs = (
        P(None, "dp", "tensor", None),
        P(None, "dp", None),
        P(None, "dp", None),
        P(None, "dp", "tensor", None),
        P("dp"),
        P("dp"),
        P("dp", None, "tensor"),
        P(None, "tensor", "dp"),
        P("tensor", "dp"),
        P("dp"),
        P("dp"),
        P("dp"),
        P("dp", "tensor"),
        P("tensor", "dp"),
        P("tensor", "dp"),
        P("dp"),
    )
    out_specs = (
        P(None, "dp", "tensor", None),
        P(None, "dp", "tensor", None),
        P("dp"),
        P("dp"),
        P("dp", None, "tensor"),
        P(None, "tensor", "dp"),
        P("tensor", "dp"),
        P("dp"),
        P("dp"),
        P("dp"),
        P("dp", "tensor"),
        P("tensor", "dp"),
        P("tensor", "dp"),
        P("dp"),
    )
    body = make_body(mesh.shape["dp"], mesh.shape["tensor"])
    return jax.shard_map(body, mesh=mesh, in_specs=in_specs, out_specs=out_specs, check_vma=False)
```

```python
import functools
import math

import jax
import jax.numpy as jnp
from jax import lax
from jax.experimental import pallas as pl
from jax.experimental.pallas import tpu as pltpu
from jax.sharding import PartitionSpec as P

bf16 = jnp.bfloat16
f32 = jnp.float32
epsilon = 1e-06
score_scale = 0.125
log2e = 1.4426950408889634
low_score = -1e30
block = 256
mib = 1 << 20


def dot_nn(left, right):
    return lax.dot_general(left, right, (((1,), (0,)), ((), ())), preferred_element_type=f32)


def dot_nt(left, right):
    return lax.dot_general(left, right, (((1,), (1,)), ((), ())), preferred_element_type=f32)


def dot_tn(left, right):
    return lax.dot_general(left, right, (((0,), (0,)), ((), ())), preferred_element_type=f32)


def lane_halves(rows):
    lane = lax.broadcasted_iota(jnp.int32, rows.shape, 1)
    zero = jnp.zeros_like(rows)
    return jnp.where(lane < 64, rows, zero), jnp.where(lane < 64, zero, rows)


def attend_kernel(
    info, qo, ko, vo, qr, kr, vr, seg_row, seg_col, out_own, out_oth, lse_ref,
    qts, vts, os, *per_head,
):
    half, wide = qo.shape
    heads = wide // 64
    blocks = 2 * half // block
    side = info[0]
    own_at = pl.multiple_of(side * half, half)
    oth_at = pl.multiple_of((1 - side) * half, half)
    ks, ss = per_head[:heads], per_head[heads:]
    for at, q_in, k_in, v_in in ((own_at, qo, ko, vo), (oth_at, qr, kr, vr)):
        rows = pl.ds(at, half)
        for i in range(heads // 2):
            pair = k_in[:, i * 128 : (i + 1) * 128]
            ks[2 * i][rows, :], ks[2 * i + 1][rows, :] = lane_halves(pair)
        for b in range(half // block):
            cols = pl.ds(pl.multiple_of(at + b * block, block), block)
            vts[:, cols] = v_in[b * block : (b + 1) * block, :].T
            qts[:, cols] = q_in[b * block : (b + 1) * block, :].T

    diff = lax.broadcasted_iota(jnp.int32, (block, block), 1) - lax.broadcasted_iota(
        jnp.int32, (block, block), 0
    )
    factor = score_scale * log2e

    def per_rows(qb, carry):
        q_at = pl.multiple_of(qb * block, block)
        q_cols = pl.ds(q_at, block)
        q_seg = seg_row[0:1, q_cols]
        first, last = info[1 + qb], info[1 + blocks + qb]

        def scan(kb, tops):
            k_at = pl.multiple_of(kb * block, block)
            keys = pl.ds(k_at, block)
            mask = (q_seg == seg_col[keys, :]) | (diff == k_at - q_at)
            out = []
            for i in range(heads):
                q = qts[i // 2 * 128 : i // 2 * 128 + 128, q_cols]
                s = jnp.where(mask, dot_nn(ks[i][keys, :], q), low_score)
                ss[i][kb] = s
                out.append(jnp.maximum(tops[i], jnp.max(s.reshape(block // 8, 8, block), axis=0)))
            return tuple(out)

        start = jnp.full((8, block), low_score, f32)
        tops = lax.fori_loop(first, last, scan, (start,) * heads)
        tops = [jnp.max(top, axis=0, keepdims=True) * factor for top in tops]

        def mix(kb, state):
            keys = pl.ds(pl.multiple_of(kb * block, block), block)
            done = []
            for i in range(heads):
                p = jnp.exp2(ss[i][kb] * factor - tops[i])
                done.append(state[2 * i] + jnp.sum(p.reshape(block // 8, 8, block), axis=0))
                done.append(
                    state[2 * i + 1] + dot_nn(vts[i * 64 : (i + 1) * 64, keys], p.astype(bf16))
                )
            return tuple(done)

        zeros = (jnp.zeros((8, block), f32), jnp.zeros((64, block), f32))
        state = lax.fori_loop(first, last, mix, zeros * heads)
        mixed = []
        for i in range(heads):
            total = jnp.sum(state[2 * i], axis=0, keepdims=True)
            mixed.append(state[2 * i + 1] / total)
            lse_ref[0, i : i + 1, q_cols] = tops[i] + jnp.log2(total)
        os[q_cols, :] = jnp.concatenate(mixed, axis=0).T.astype(bf16)
        return carry

    lax.fori_loop(0, blocks, per_rows, 0)
    out_own[...] = os[pl.ds(own_at, half), :]
    out_oth[...] = os[pl.ds(oth_at, half), :]


def attend(info, own, oth, seg_row, seg_col):
    half = own.shape[0]
    rows = 2 * half
    groups = own.shape[1] // 768

    def part(which):
        return pl.BlockSpec((half, 256), lambda i, _: (0, i * 3 + which))

    whole = lambda shape: pl.BlockSpec(shape, lambda i, _: (0,) * len(shape))
    return pl.pallas_call(
        attend_kernel,
        grid_spec=pltpu.PrefetchScalarGridSpec(
            num_scalar_prefetch=1,
            grid=(groups,),
            in_specs=[part(0), part(1), part(2)] * 2 + [whole((1, rows)), whole((rows, 1))],
            out_specs=[
                pl.BlockSpec((half, 256), lambda i, _: (0, i)),
                pl.BlockSpec((half, 256), lambda i, _: (0, i)),
                pl.BlockSpec((1, 8, rows), lambda i, _: (i, 0, 0)),
            ],
            scratch_shapes=[pltpu.VMEM((256, rows), bf16)] * 2
            + [pltpu.VMEM((rows, 256), bf16)]
            + [pltpu.VMEM((rows, 128), bf16)] * 4
            + [pltpu.VMEM((rows // block, block, block), f32)] * 4,
        ),
        out_shape=(
            jax.ShapeDtypeStruct((half, groups * 256), bf16),
            jax.ShapeDtypeStruct((half, groups * 256), bf16),
            jax.ShapeDtypeStruct((groups, 8, rows), f32),
        ),
        compiler_params=pltpu.CompilerParams(vmem_limit_bytes=40 * mib),
        cost_estimate=pl.CostEstimate(
            flops=int(groups * 4 * rows * rows * 256 * 1.5), bytes_accessed=int(own.size * 5), transcendentals=0
        ),
        name="attend",
    )(info, own, own, own, oth, oth, oth, seg_row, seg_col)


def attend_back_kernel(
    info, qo, ko, vo, qr, kr, vr, go, gr, oo, orr, lse_ref, seg_row, seg_col,
    dqo, dko, dvo, dqr, dkr, dvr,
    qts, gts, kts, os, dqs, dks, dvs, *per_head,
):
    half, wide = qo.shape
    heads = wide // 64
    blocks = 2 * half // block
    side = info[0]
    own_at = pl.multiple_of(side * half, half)
    oth_at = pl.multiple_of((1 - side) * half, half)
    qs, ks, vs, gs = [per_head[i * heads : (i + 1) * heads] for i in range(4)]
    for at, q_in, k_in, v_in, g_in, o_in in (
        (own_at, qo, ko, vo, go, oo),
        (oth_at, qr, kr, vr, gr, orr),
    ):
        rows = pl.ds(at, half)
        for refs, value in ((qs, q_in), (ks, k_in), (vs, v_in), (gs, g_in)):
            for i in range(heads // 2):
                pair = value[:, i * 128 : (i + 1) * 128]
                refs[2 * i][rows, :], refs[2 * i + 1][rows, :] = lane_halves(pair)
        for b in range(half // block):
            cols = pl.ds(pl.multiple_of(at + b * block, block), block)
            for ref, value in ((qts, q_in), (gts, g_in), (kts, k_in)):
                ref[:, cols] = value[b * block : (b + 1) * block, :].T
        os[rows, :] = o_in[...]
    dks[...] = jnp.zeros_like(dks)
    dvs[...] = jnp.zeros_like(dvs)

    diff = lax.broadcasted_iota(jnp.int32, (block, block), 1) - lax.broadcasted_iota(
        jnp.int32, (block, block), 0
    )
    factor = score_scale * log2e

    def per_rows(qb, carry):
        q_at = pl.multiple_of(qb * block, block)
        rows = pl.ds(q_at, block)
        product = gts[:, rows].astype(f32) * os[rows, :].T.astype(f32)
        inner = [jnp.sum(product[i * 64 : (i + 1) * 64], axis=0, keepdims=True) for i in range(heads)]
        lses = [lse_ref[0, i : i + 1, rows] for i in range(heads)]
        q_seg = seg_row[0:1, rows]

        def per_keys(kb, dq):
            k_at = pl.multiple_of(kb * block, block)
            keys = pl.ds(k_at, block)
            mask = (q_seg == seg_col[keys, :]) | (diff == k_at - q_at)
            dq_out, dk, dv = [], [], []
            for i in range(heads):
                pair = slice(i // 2 * 128, i // 2 * 128 + 128)
                s = dot_nn(ks[i][keys, :], qts[pair, rows]) * factor - lses[i]
                p = jnp.exp2(jnp.where(mask, s, low_score))
                dv.append(dot_nn(p.astype(bf16), gs[i][rows, :]))
                dp = dot_nn(vs[i][keys, :], gts[pair, rows])
                ds = (p * (dp - inner[i])).astype(bf16)
                dk.append(dot_nn(ds, qs[i][rows, :]))
                dq_out.append(dq[i] + dot_nn(kts[i * 64 : (i + 1) * 64, keys], ds))
            for i in range(0, heads, 2):
                pair = slice(i // 2 * 128, i // 2 * 128 + 128)
                dks[keys, pair] += dk[i] + dk[i + 1]
                dvs[keys, pair] += dv[i] + dv[i + 1]
            return tuple(dq_out)

        dq = lax.fori_loop(
            info[1 + qb], info[1 + blocks + qb], per_keys, (jnp.zeros((64, block), f32),) * heads
        )
        dqs[rows, :] = (jnp.concatenate(dq, axis=0) * score_scale).T.astype(bf16)
        return carry

    lax.fori_loop(0, blocks, per_rows, 0)
    for at, dq_out, dk_out, dv_out in ((own_at, dqo, dko, dvo), (oth_at, dqr, dkr, dvr)):
        rows = pl.ds(at, half)
        dq_out[...] = dqs[rows, :]
        dk_out[...] = (dks[rows, :] * score_scale).astype(bf16)
        dv_out[...] = dvs[rows, :].astype(bf16)


def attend_back(info, own, oth, g_own, g_oth, o_own, o_oth, lse, seg_row, seg_col):
    half = own.shape[0]
    rows = 2 * half
    groups = own.shape[1] // 768

    def part(which):
        return pl.BlockSpec((half, 256), lambda i, _: (0, i * 3 + which))

    col = pl.BlockSpec((half, 256), lambda i, _: (0, i))
    whole = lambda shape: pl.BlockSpec(shape, lambda i, _: (0,) * len(shape))
    shape = jax.ShapeDtypeStruct((half, groups * 256), bf16)
    return pl.pallas_call(
        attend_back_kernel,
        grid_spec=pltpu.PrefetchScalarGridSpec(
            num_scalar_prefetch=1,
            grid=(groups,),
            in_specs=[part(0), part(1), part(2)] * 2
            + [col] * 4
            + [pl.BlockSpec((1, 8, rows), lambda i, _: (i, 0, 0))]
            + [whole((1, rows)), whole((rows, 1))],
            out_specs=[col] * 6,
            scratch_shapes=[pltpu.VMEM((256, rows), bf16)] * 3
            + [pltpu.VMEM((rows, 256), bf16)] * 2
            + [pltpu.VMEM((rows, 256), f32)] * 2
            + [pltpu.VMEM((rows, 128), bf16)] * 16,
        ),
        out_shape=(shape,) * 6,
        compiler_params=pltpu.CompilerParams(vmem_limit_bytes=56 * mib),
        cost_estimate=pl.CostEstimate(
            flops=int(groups * 10 * rows * rows * 256), bytes_accessed=int(own.size * 10), transcendentals=0
        ),
        name="attend_back",
    )(info, own, own, own, oth, oth, oth, g_own, g_oth, o_own, o_oth, lse, seg_row, seg_col)


def plan_gather(loads, bits, n_t, rows_load):
    tasks = {}
    for w, load in enumerate(loads):
        for s in range(n_t):
            last = None
            if s:
                last = (w, s, "z")
                tasks[last] = (None if s == 1 else (w, s - 1, "z"), "z", load)
            middle = list(range(1, bits))
            for k, bit in enumerate((middle if (w + s) % 2 == 0 else middle[::-1]) + [0]):
                tasks[(w, s, k)] = (last, bit, load << k)
                last = (w, s, k)
    for q in range(2):
        tasks[("rows", q, 0)] = (None, "z", rows_load)
    free, done, waiting = {}, {}, list(tasks)
    while waiting:
        ready = [
            (0.0 if tasks[t][0] is None else done[tasks[t][0]], i, t)
            for i, t in enumerate(waiting)
            if tasks[t][0] is None or tasks[t][0] in done
        ]
        start, _, task = min((max(r, free.get(tasks[t][1], 0.0)), i, t) for r, i, t in ready)
        _, link, load = tasks[task]
        done[task] = start + load / (300e3 if link == 0 else 44e3) + 1.0
        free[link] = done[task] - 1.0
        waiting.remove(task)
    order = sorted(done, key=lambda t: done[t])
    return {t: tasks[t][0] for t in order}, order


def gather_kernel(n_dp, n_t, count, parents, arrivals, *refs):
    rows_ref, own = refs[0], refs[1 : 1 + count]
    rows_out, outs = refs[1 + count], refs[2 + count : 2 + 2 * count]
    send, recv, near = refs[2 + 2 * count :]
    bits = n_dp.bit_length() - 1
    me, z = lax.axis_index("dp"), lax.axis_index("tensor")
    side = lax.rem(me, 2)
    base = me - side
    number = {task: i for i, task in enumerate(arrivals)}

    greet(n_t, bits, me, z)
    flips = [bit_flip(me, bit) for bit in range(bits)]

    def slot(w, s, index):
        cols = own[w].shape[1]
        return outs[w].at[index + (slice(None), pl.ds(s * cols, cols))]

    def copy_of(task):
        w, s, k = task
        i = number[task]
        if k == "z":
            src = own[w] if s == 1 else slot(w, s - 1, (0,) * bits)
            dst = slot(w, s, (0,) * bits)
            where = (me, lax.rem(z + 1, n_t))
        else:
            middle = list(range(1, bits))
            order = (middle if (w + s) % 2 == 0 else middle[::-1]) + [0]
            bit = order[k]
            src_at, dst_at = [], []
            for axis in range(bits):
                if axis == bit:
                    src_at.append(0)
                    dst_at.append(1)
                else:
                    held = slice(None) if axis in order[:k] else 0
                    src_at.append(held)
                    dst_at.append(held)
            src = own[w] if (k == 0 and s == 0) else slot(w, s, tuple(src_at))
            dst = slot(w, s, tuple(dst_at))
            where = (flips[bit], z)
        return pltpu.make_async_remote_copy(
            src_ref=src, dst_ref=dst, send_sem=send.at[i], recv_sem=recv.at[i],
            device_id=where, device_id_type=pl.DeviceIdType.MESH,
        )

    placed = []
    for w in range(count):
        placed.append(pltpu.make_async_copy(own[w], slot(w, 0, (0,) * bits), near.at[w]))
        placed[-1].start()

    place = lax.rem(z, 2)
    target_core = base + z // 2

    def rows_copy(m):
        i = [number[("rows", q, 0)] for q in range(2)]
        where = (target_core, 2 * m + side)
        mine = (side == z // 2) & (z == 2 * m + side)
        return i, where, mine

    def start_rows():
        for m in range(2):
            i, where, mine = rows_copy(m)
            for q in range(2):

                @pl.when((place == q) & mine)
                def _():
                    pltpu.make_async_copy(rows_ref.at[m], rows_out.at[q], recv.at[i[q]]).start()

                @pl.when((place == q) & jnp.logical_not(mine))
                def _():
                    pltpu.make_async_remote_copy(
                        src_ref=rows_ref.at[m], dst_ref=rows_out.at[q], send_sem=near.at[count + m],
                        recv_sem=recv.at[i[q]], device_id=where, device_id_type=pl.DeviceIdType.MESH,
                    ).start()

    copies = {task: copy_of(task) for task in arrivals if task[0] != "rows"}
    for task in arrivals:
        if task[0] != "rows" and parents[task] is None:
            copies[task].start()
    start_rows()
    landed = {w: False for w in range(count)}
    for task in arrivals:
        if task[0] == "rows":
            q = task[1]
            pltpu.make_async_copy(rows_ref.at[0], rows_out.at[q], recv.at[number[task]]).wait()
            continue
        copies[task].wait_recv()
        for child in arrivals:
            if parents[child] == task:
                if child[1] == 0 and not landed[child[0]]:
                    placed[child[0]].wait()
                    landed[child[0]] = True
                copies[child].start()
    for w in range(count):
        if not landed[w]:
            placed[w].wait()
    for task in arrivals:
        if task[0] != "rows":
            copies[task].wait_send()
    for m in range(2):
        i, where, mine = rows_copy(m)

        @pl.when(jnp.logical_not(mine))
        def _():
            pltpu.make_async_remote_copy(
                src_ref=rows_ref.at[m], dst_ref=rows_out.at[0], send_sem=near.at[count + m],
                recv_sem=recv.at[i[0]], device_id=where, device_id_type=pl.DeviceIdType.MESH,
            ).wait_send()


def bit_flip(me, bit):
    span = 1 << bit
    return me + span - 2 * span * lax.rem(me // span, 2)


def gather_all(rows, own, n_dp, n_t):
    bits = n_dp.bit_length() - 1
    parents, arrivals = plan_gather(
        [w.shape[0] * w.shape[1] * 2 for w in own], bits, n_t, rows[0].size * 2
    )
    count = len(own)
    hbm = pl.BlockSpec(memory_space=pl.ANY)
    return pl.pallas_call(
        functools.partial(gather_kernel, n_dp, n_t, count, parents, arrivals),
        in_specs=[hbm] * (1 + count),
        out_specs=[hbm] * (1 + count),
        out_shape=(jax.ShapeDtypeStruct(rows.shape, rows.dtype),)
        + tuple(
            jax.ShapeDtypeStruct((2,) * bits + (w.shape[0], n_t * w.shape[1]), w.dtype) for w in own
        ),
        scratch_shapes=[
            pltpu.SemaphoreType.DMA((len(arrivals),)),
            pltpu.SemaphoreType.DMA((len(arrivals),)),
            pltpu.SemaphoreType.DMA((count + 2,)),
        ],
        compiler_params=pltpu.CompilerParams(collective_id=0, has_side_effects=True),
        cost_estimate=pl.CostEstimate(flops=0, bytes_accessed=300 * mib, transcendentals=0),
        name="gather_all",
    )(rows, *own)


def stage_bits(w, s, bits):
    middle = list(range(1, bits))
    return [0] + (middle if (w + s) % 2 == 0 else middle[::-1])


def plan_reduce(widths, size, bits, n_t, rows_load):
    turn = list(range(1, n_t)) + [0]
    last = len(widths)
    chunks = [(last, s) for s in turn] + [(w, s) for w in range(last) for s in turn]
    ready, free, core, order = {}, {"z": rows_load / 44e3}, 0.0, []
    pending = {("make", w, s): 0.0 for w, s in chunks}
    rank = {c: i for i, c in enumerate(chunks)}
    arrived = {}
    while pending:
        def key(item):
            kind, w, s = item[0][0], item[0][1], item[0][2]
            begin = max(core, item[1])
            return (begin, kind == "make", rank[(w, s)])

        action, when = min(pending.items(), key=key)
        del pending[action]
        order.append(action)
        w, s = action[1], action[2]
        cols = 64 if w == last else widths[w]
        rows = 16 if w == last else size << (bits - 1)
        share = rows * cols / (512 * 1024)
        begin = max(core, when)
        core = begin + (4.5 * share if action[0] == "make" else 1.2 * share / (1 << action[3] if action[0] == "add" else 4) + 0.3)
        flow = stage_bits(w, s, bits)
        k = 0 if action[0] == "make" else action[3] + 1 if action[0] == "add" else None

        def send(link, load):
            begin = max(core, free.get(link, 0.0))
            free[link] = begin + load / (300e3 if link == 0 else 44e3)
            return free[link] + 2.0

        def to_z():
            if s != 0:
                nxt = turn[turn.index(s) + 1]
                arrived[(w, nxt)] = send("z", (rows >> (bits - 1)) * cols * 2)
                if (w, nxt) in ready:
                    pending[("z", w, nxt)] = arrived[(w, nxt)]

        if k is not None and k < bits:
            load = (rows >> k) * cols * 2
            pending[("add", w, s, k)] = send(flow[k], load)
        elif k is not None:
            ready[(w, s)] = core
            if s == turn[0]:
                to_z()
            elif (w, s) in arrived:
                pending[("z", w, s)] = arrived[(w, s)]
        else:
            to_z()
    return order


def greet(n_t, bits, me, z):
    side = lax.rem(me, 2)
    barrier = pltpu.get_barrier_semaphore()
    for dz in range(n_t):
        for other in range(2):
            if dz or other:
                where = (me - side + lax.rem(side + other, 2), lax.rem(z + dz, n_t))
                pl.semaphore_signal(barrier, inc=1, device_id=where, device_id_type=pl.DeviceIdType.MESH)
    for bit in range(1, bits):
        where = (bit_flip(me, bit), z)
        pl.semaphore_signal(barrier, inc=1, device_id=where, device_id_type=pl.DeviceIdType.MESH)
    pl.semaphore_wait(barrier, 2 * n_t - 1 + bits - 1)


def reduce_kernel(n_dp, n_t, plan, widths, *refs):
    bits = n_dp.bit_length() - 1
    count = len(widths)
    refs = list(refs)
    take = lambda n: [refs.pop(0) for _ in range(n)]
    xs, gs, (small_in, rows_in) = take(count), take(count), take(2)
    outs, (small_out, rows_out) = take(count), take(2)
    kept, came, zcame = take(count + 1), take(count + 1), take(count + 1)
    later = [take(bits - 1) for _ in range(count + 1)]
    (away, away_small, x_buf, x_turn, g_buf) = take(5)
    (x_sem, g_sem, s_sem, r_sem, send, recv, zsend, zrecv) = take(8)
    me, z = lax.axis_index("dp"), lax.axis_index("tensor")
    turn = list(range(1, n_t)) + [0]
    blk = kept[0].shape[-2]
    tall = blk << (bits - 1)
    greet(n_t, bits, me, z)

    side = lax.rem(me, 2)
    micro, owner = z // 2, lax.rem(z, 2)

    def rows_to(q):
        where = (me - side + owner, 2 * side + q)
        mine = (owner == side) & (2 * side + q == z)
        return where, mine

    def rows_from(m):
        return (side == z // 2) & (2 * m + side == z)

    for q in range(2):
        where, mine = rows_to(q)
        for m in range(2):

            @pl.when((micro == m) & mine)
            def _():
                pltpu.make_async_copy(rows_in.at[q], rows_out.at[m], r_sem.at[2 + m]).start()

            @pl.when((micro == m) & jnp.logical_not(mine))
            def _():
                pltpu.make_async_remote_copy(
                    src_ref=rows_in.at[q], dst_ref=rows_out.at[m], send_sem=r_sem.at[q],
                    recv_sem=r_sem.at[2 + m], device_id=where, device_id_type=pl.DeviceIdType.MESH,
                ).start()

    made = [a for a in plan if a[0] == "make" and a[1] < count]

    def fetch(i):
        _, w, s = made[i]
        c = widths[w]
        return pltpu.make_async_copy(
            gs[w].at[:, pl.ds(s * c, c)], g_buf.at[i % 2, :, pl.ds(0, c)], g_sem.at[i % 2]
        )

    def fetch_x(w):
        return pltpu.make_async_copy(xs[w], x_buf, x_sem)

    def at_stage(w, s, k, taken):
        flow = stage_bits(w, s, bits)
        return tuple(
            0 if bit in flow[:k] else (taken if bit == flow[k] else slice(None)) for bit in range(1, bits)
        )

    def landing(w, s, k):
        ref = came[w] if k == 0 else later[w][k - 1]
        return ref.at[s]

    def copy_of(w, s, k):
        flow = stage_bits(w, s, bits)
        if k == 0:
            src = away_small.at[s] if w == count else away_view(w, s)
        else:
            src = kept[w].at[(s,) + at_stage(w, s, k, 1)]
        return pltpu.make_async_remote_copy(
            src_ref=src, dst_ref=landing(w, s, k), send_sem=send.at[w, s, k], recv_sem=recv.at[w, s, k],
            device_id=(bit_flip(me, flow[k]), z), device_id_type=pl.DeviceIdType.MESH,
        )

    def away_view(w, s):
        i = made.index(("make", w, s)) % 2
        return away.at[(i,) + (slice(None),) * bits + (pl.ds(0, widths[w]),)]

    def zcopy(w, s):
        nxt = turn[turn.index(s) + 1]
        return pltpu.make_async_remote_copy(
            src_ref=kept[w].at[(s,) + (0,) * (bits - 1)], dst_ref=zcame[w].at[nxt],
            send_sem=zsend.at[w, s], recv_sem=zrecv.at[w, nxt],
            device_id=(me, lax.rem(z + 1, n_t)), device_id_type=pl.DeviceIdType.MESH,
        )

    def finish(w, s, total):
        ref = small_out if w == count else outs[w]
        ref[...] = total

    last_of = {}
    for i, (_, w, s) in enumerate(made):
        last_of[w] = i
    fetch(0).start()
    fetch_x(made[0][1]).start()
    loaded = set()
    for action in plan:
        kind, w, s = action[:3]
        if kind == "make" and w == count:
            lanes = small_out.shape[-1]
            cols = pl.ds(s * lanes, lanes)
            for half, dst in ((1, away_small.at[s]), (0, kept[w].at[s])):
                src = small_in.at[(half,) + (slice(None),) * bits + (cols,)]
                pltpu.make_async_copy(src, dst, s_sem.at[half]).start()
            for half, dst in ((1, away_small.at[s]), (0, kept[w].at[s])):
                src = small_in.at[(half,) + (slice(None),) * bits + (cols,)]
                pltpu.make_async_copy(src, dst, s_sem.at[half]).wait()
            copy_of(w, s, 0).start()
        elif kind == "make":
            i = made.index(action)
            c = widths[w]
            if w not in loaded:
                loaded.add(w)
                fetch_x(w).wait()
                for a in range(x_buf.shape[1] // 256):

                    def turn_block(b, carry, a=a):
                        rows = pl.ds(pl.multiple_of(b * 256, 256), 256)
                        x_turn[a * 256 : (a + 1) * 256, rows] = x_buf[rows, a * 256 : (a + 1) * 256].T
                        return carry

                    lax.fori_loop(0, x_buf.shape[0] // 256, turn_block, 0)
                if i + n_t < len(made):
                    fetch_x(made[i + n_t][1]).start()
            fetch(i).wait()
            if i + 1 < len(made):
                fetch(i + 1).start()
            if i >= 2:
                copy_of(*made[i - 2][1:], 0).wait_send()
            whole = (slice(None),) * bits

            def away_block(n, carry):
                cols = pl.ds(pl.multiple_of(n * 256, 256), 256)
                value = dot_nn(x_turn[tall:, :], g_buf[i % 2, :, cols]).astype(bf16)
                away[(i % 2,) + whole + (cols,)] = value.reshape((2,) * (bits - 1) + (blk, 256))
                return carry

            lax.fori_loop(0, c // 256, away_block, 0)
            copy_of(w, s, 0).start()

            def kept_block(n, carry):
                cols = pl.ds(pl.multiple_of(n * 256, 256), 256)
                value = dot_nn(x_turn[:tall, :], g_buf[i % 2, :, cols]).astype(bf16)
                kept[w][(s,) + whole + (cols,)] = value.reshape((2,) * (bits - 1) + (blk, 256))
                return carry

            lax.fori_loop(0, c // 256, kept_block, 0)
        elif kind == "add":
            k = action[3]
            copy_of(w, s, k).wait_recv()
            place = (s,) + (slice(None),) * (bits - 1) if k == 0 else (s,) + at_stage(w, s, k, 0)
            got = (came[w] if k == 0 else later[w][k - 1])[s]
            held = kept[w][place]
            kept[w][place] = (held.astype(f32) + got.astype(f32)).astype(held.dtype)
            if k + 1 < bits:
                copy_of(w, s, k + 1).start()
            elif s == turn[0]:
                zcopy(w, s).start()
        else:
            before = turn[turn.index(s) - 1]
            zcopy(w, before).wait_recv()
            place = (s,) + (0,) * (bits - 1)
            total = kept[w][place].astype(f32) + zcame[w][s].astype(f32)
            if s == turn[-1]:
                finish(w, s, total)
            else:
                kept[w][place] = total.astype(kept[w].dtype)
                zcopy(w, s).start()
    for w in range(count + 1):
        for s in turn:
            for k in range(bits):
                if k == 0 and w < count and made.index(("make", w, s)) < len(made) - 2:
                    continue
                copy_of(w, s, k).wait_send()
            if s != turn[-1]:
                zcopy(w, s).wait_send()
    for q in range(2):
        where, mine = rows_to(q)

        @pl.when(jnp.logical_not(mine))
        def _():
            pltpu.make_async_remote_copy(
                src_ref=rows_in.at[q], dst_ref=rows_out.at[0], send_sem=r_sem.at[q],
                recv_sem=r_sem.at[2], device_id=where, device_id_type=pl.DeviceIdType.MESH,
            ).wait_send()
    for m in range(2):
        pltpu.make_async_copy(rows_in.at[0], rows_out.at[m], r_sem.at[2 + m]).wait()


def reduce_all(xs, gs, small, rows, n_dp, n_t):
    bits = n_dp.bit_length() - 1
    count = len(xs)
    width = xs[0].shape[1]
    size = width // n_dp
    widths = [g.shape[1] // n_t for g in gs]
    lanes = small.shape[-1] // n_t
    plan = plan_reduce(widths, size, bits, n_t, rows[0].size * 2)
    cells = (2,) * (bits - 1)
    shapes = [(size, c, bf16) for c in widths] + [(small.shape[-2], lanes, f32)]
    hbm, vmem = pl.BlockSpec(memory_space=pl.ANY), pl.BlockSpec(memory_space=pltpu.VMEM)
    scratch = [pltpu.VMEM((n_t,) + cells + (r, c), t) for r, c, t in shapes]
    scratch += [pltpu.VMEM((n_t,) + cells + (r, c), t) for r, c, t in shapes]
    scratch += [pltpu.VMEM((n_t, r, c), t) for r, c, t in shapes]
    for r, c, t in shapes:
        scratch += [pltpu.VMEM((n_t,) + (2,) * (bits - 1 - k) + (r, c), t) for k in range(1, bits)]
    scratch += [
        pltpu.VMEM((2,) + cells + (size, max(widths)), bf16),
        pltpu.VMEM((n_t,) + cells + (small.shape[-2], lanes), f32),
        pltpu.VMEM(xs[0].shape, bf16),
        pltpu.VMEM((width, xs[0].shape[0]), bf16),
        pltpu.VMEM((2, gs[0].shape[0], max(widths)), bf16),
        pltpu.SemaphoreType.DMA,
        pltpu.SemaphoreType.DMA((2,)),
        pltpu.SemaphoreType.DMA((2,)),
        pltpu.SemaphoreType.DMA((4,)),
        pltpu.SemaphoreType.DMA((count + 1, n_t, bits)),
        pltpu.SemaphoreType.DMA((count + 1, n_t, bits)),
        pltpu.SemaphoreType.DMA((count + 1, n_t)),
        pltpu.SemaphoreType.DMA((count + 1, n_t)),
    ]
    return pl.pallas_call(
        functools.partial(reduce_kernel, n_dp, n_t, plan, widths),
        in_specs=[hbm] * (2 * count + 2),
        out_specs=[vmem] * (count + 1) + [hbm],
        out_shape=tuple(jax.ShapeDtypeStruct((size, c), f32) for c in widths)
        + (
            jax.ShapeDtypeStruct((small.shape[-2], lanes), f32),
            jax.ShapeDtypeStruct(rows.shape, rows.dtype),
        ),
        scratch_shapes=scratch,
        compiler_params=pltpu.CompilerParams(
            collective_id=1, has_side_effects=True, vmem_limit_bytes=60 * mib
        ),
        cost_estimate=pl.CostEstimate(
            flops=2 * xs[0].size * n_t * sum(widths), bytes_accessed=200 * mib, transcendentals=0
        ),
        name="reduce_all",
    )(*xs, *gs, small, rows)


def ingest_kernel(order, a_ref, b_ref, o_ref):
    rows, width = a_ref.shape
    count = order.shape[0] - 1
    size = width // count
    first = order[count]
    for place in range(count):
        src = pl.ds(pl.multiple_of(order[place] * size, size), size)
        dst = slice(place * size, (place + 1) * size)

        @pl.when(first == 0)
        def _():
            o_ref[0:rows, dst] = a_ref[:, src]
            o_ref[rows : 2 * rows, dst] = b_ref[:, src]

        @pl.when(first != 0)
        def _():
            o_ref[0:rows, dst] = b_ref[:, src]
            o_ref[rows : 2 * rows, dst] = a_ref[:, src]

    o_ref[2 * rows :, :] = jnp.zeros((o_ref.shape[0] - 2 * rows, width), o_ref.dtype)


def ingest(order, first, a, b, padded):
    rows, width = a.shape
    count = order.shape[0]
    if width // count % 128:
        both = jnp.where(first == 0, jnp.concatenate([a, b]), jnp.concatenate([b, a]))
        both = jnp.take(both.reshape(2 * rows, count, -1), order, axis=1).reshape(2 * rows, width)
        return jnp.pad(both, ((0, padded - 2 * rows), (0, 0)))
    scalars = jnp.concatenate([order, first[None]]).astype(jnp.int32)
    return pl.pallas_call(
        ingest_kernel,
        grid_spec=pltpu.PrefetchScalarGridSpec(
            num_scalar_prefetch=1,
            grid=(1,),
            in_specs=[pl.BlockSpec((rows, width), lambda i, _: (0, 0))] * 2,
            out_specs=pl.BlockSpec((padded, width), lambda i, _: (0, 0)),
        ),
        out_shape=jax.ShapeDtypeStruct((padded, width), a.dtype),
        compiler_params=pltpu.CompilerParams(vmem_limit_bytes=20 * mib),
        name="ingest",
    )(scalars, a, b)


def egress_kernel(order, x_ref, a_ref, b_ref):
    rows, width = a_ref.shape
    count = order.shape[0] - 1
    size = width // count
    first = order[count]
    for place in range(count):
        dst = pl.ds(pl.multiple_of(order[place] * size, size), size)
        src = slice(place * size, (place + 1) * size)

        @pl.when(first == 0)
        def _():
            a_ref[:, dst] = x_ref[0:rows, src]
            b_ref[:, dst] = x_ref[rows : 2 * rows, src]

        @pl.when(first != 0)
        def _():
            b_ref[:, dst] = x_ref[0:rows, src]
            a_ref[:, dst] = x_ref[rows : 2 * rows, src]


def egress(order, inverse, first, x, rows):
    width = x.shape[1]
    count = order.shape[0]
    if width // count % 128:
        both = jnp.take(x.reshape(-1, count, width // count), inverse, axis=1).reshape(-1, width)
        top, low = both[:rows], both[rows : 2 * rows]
        return jnp.where(first == 0, top, low), jnp.where(first == 0, low, top)
    scalars = jnp.concatenate([order, first[None]]).astype(jnp.int32)
    return pl.pallas_call(
        egress_kernel,
        grid_spec=pltpu.PrefetchScalarGridSpec(
            num_scalar_prefetch=1,
            grid=(1,),
            in_specs=[pl.BlockSpec(x.shape, lambda i, _: (0, 0))],
            out_specs=[pl.BlockSpec((rows, width), lambda i, _: (0, 0))] * 2,
        ),
        out_shape=(jax.ShapeDtypeStruct((rows, width), x.dtype),) * 2,
        compiler_params=pltpu.CompilerParams(vmem_limit_bytes=20 * mib),
        name="egress",
    )(scalars, x)


def norm_parts(operand):
    centred = operand - jnp.mean(operand, axis=-1, keepdims=True)
    inverse = lax.rsqrt(jnp.mean(centred * centred, axis=-1, keepdims=True) + epsilon)
    return centred * inverse, inverse


def norm_back(scaled, normed, inverse):
    return inverse * (
        scaled
        - jnp.mean(scaled, axis=-1, keepdims=True)
        - normed * jnp.mean(scaled * normed, axis=-1, keepdims=True)
    )


def make_body(n_dp, n_t):
    bits = n_dp.bit_length() - 1
    reverse = [int(format(i, "b").zfill(bits)[::-1], 2) for i in range(n_dp)]
    axes = ("dp", "tensor")

    def at(dp, t):
        return dp * n_t + t

    go_a, go_b = [], []
    for dp in range(n_dp):
        c, base = dp % 2, dp - dp % 2
        for j in range(n_t):
            go_a.append((at(dp, j), at(base + j // 2, 2 * (j % 2) + c)))
            go_b.append((at(dp, j), at(base + j // 2, 2 * (1 - j % 2) + c)))
    back_a = [(d, s) for s, d in go_a]
    back_b = [(d, s) for s, d in go_b]
    ring = [(j, (j + 1) % n_t) for j in range(n_t)]

    def swap(value, bit):
        return lax.ppermute(value, "dp", [(i, i ^ (1 << bit)) for i in range(n_dp)])

    def step_z(value):
        return lax.ppermute(value, "tensor", ring)

    def body(
        tokens, segment_ids, pad_mask, cotangent, ln1_gain, ln1_bias, qkv_weight, qv_bias,
        proj_weight, proj_bias, ln2_gain, ln2_bias, fc1_weight, fc1_bias, fc2_weight, fc2_bias,
    ):
        me = lax.axis_index("dp")
        z = lax.axis_index("tensor")
        side = me % 2
        quarter, width = tokens.shape[2], tokens.shape[3]
        length = segment_ids.shape[2]
        half = -(-2 * quarter // block) * block
        size = width // n_dp
        micro = z // 2
        odd = z % 2
        order = jnp.stack([me ^ reverse[p] for p in range(n_dp)]).astype(jnp.int32)
        inverse = jnp.stack(
            [sum((((me ^ d) >> b) & 1) << (bits - 1 - b) for b in range(bits)) for d in range(n_dp)]
        ).astype(jnp.int32)

        def bring(array):
            a = lax.ppermute(lax.dynamic_index_in_dim(array[:, 0], odd, 0, False), axes, go_a)
            b = lax.ppermute(lax.dynamic_index_in_dim(array[:, 0], 1 - odd, 0, False), axes, go_b)
            return a, b

        def give(a, b):
            return lax.ppermute(a, axes, back_a), lax.ppermute(b, axes, back_b)

        lanes = max(128, size)

        def row_of(v):
            return jnp.pad(v.reshape(1, -1), ((0, 0), (0, lanes - v.size)))

        fields = [ln1_gain, ln1_bias, proj_bias, ln2_gain, ln2_bias, fc2_bias, fc1_bias, qv_bias]
        packed = jnp.concatenate([row_of(v) for v in fields] + [jnp.zeros((8, lanes), bf16)])
        rows_in, w_qkv, w_fc1, w_fc2, w_proj, small = gather_all(
            tokens[:, 0],
            (qkv_weight.reshape(size, -1), fc1_weight, fc2_weight.T, proj_weight.T, packed),
            n_dp, n_t,
        )

        w_qkv, w_fc1, w_fc2, w_proj = [w.reshape(width, -1) for w in (w_qkv, w_fc1, w_fc2, w_proj)]
        x_low = ingest(order, jnp.int32(0), rows_in[0], rows_in[1], half)

        small = small.reshape(n_dp, packed.shape[0], n_t, lanes).astype(f32)
        gain_one, shift_one, proj_shift, gain_two, shift_two, fc2_shift = [
            small[:, i, 0, :size].reshape(-1) for i in range(6)
        ]
        ordered = jnp.take(small[:, 6:8], inverse, axis=0)
        fc1_shift = jnp.transpose(ordered[:, 0, :, :size], (1, 0, 2)).reshape(-1)
        heads_t, hd = qv_bias.shape[1], qv_bias.shape[2] * n_dp
        qv = ordered[:, 1, :, : qv_bias.size].reshape(n_dp, n_t, 2, heads_t, hd // n_dp)
        qv = jnp.transpose(qv, (1, 2, 3, 0, 4)).reshape(n_t, 2, heads_t * hd)
        qkv_shift = jnp.stack([qv[:, 0], jnp.zeros_like(qv[:, 0]), qv[:, 1]], axis=1).reshape(-1)

        which = z % 2
        packed_ids = jnp.stack([segment_ids[:, 0], pad_mask[:, 0]])
        packed_oth = swap(packed_ids, 0)
        ids = jnp.where(which == side, packed_ids, packed_oth)
        ids = lax.dynamic_index_in_dim(ids, micro, 1, False)
        seg, live = ids[0], ids[1]
        gap = half - length // 2

        def stretch(v, fill):
            return jnp.pad(v.reshape(2, -1), ((0, 0), (0, gap)), constant_values=fill).reshape(-1)

        q_ids = stretch(seg, -1)
        k_ids = stretch(jnp.where(live == 1, seg, -2), -2)
        per_half = half // block
        first_pos = jnp.array([h * (length // 2) + b * block for h in range(2) for b in range(per_half)])
        last_pos = jnp.array(
            [min(h * (length // 2) + (b + 1) * block, (h + 1) * (length // 2)) - 1 for h in range(2) for b in range(per_half)]
        )
        lo = jnp.sum((seg[None, :] < seg[first_pos][:, None]).astype(jnp.int32), axis=1)
        hi = jnp.sum((seg[None, :] <= seg[last_pos][:, None]).astype(jnp.int32), axis=1) - 1
        place = lambda v: jnp.where(v >= length // 2, v + gap, v) // block
        info = jnp.concatenate([side[None], place(lo), place(hi) + 1]).astype(jnp.int32)

        x = x_low.astype(f32)
        hat_one, inv_one = norm_parts(x)
        rows_one = (hat_one * gain_one + shift_one).astype(bf16)
        qkv = (dot_nn(rows_one, w_qkv) + qkv_shift).astype(bf16)
        qkv = (qkv[:, : qkv.shape[1] // 2], qkv[:, qkv.shape[1] // 2 :])
        own = jnp.where(side == 0, qkv[0], qkv[1])
        oth = swap(jnp.where(side == 0, qkv[1], qkv[0]), 0)
        o_own, o_oth, lse = attend(info, own, oth, q_ids[None, :], k_ids[:, None])
        o_own, o_oth, lse, gy_a, gy_b = lax.optimization_barrier((o_own, o_oth, lse) + bring(cotangent))
        o_came = swap(o_oth, 0)
        heads = jnp.where(
            side == 0, jnp.concatenate([o_own, o_came], axis=1), jnp.concatenate([o_came, o_own], axis=1)
        )
        hidden = x + (dot_nt(heads, w_proj) + proj_shift)
        hat_two, inv_two = norm_parts(hidden)
        rows_two = (hat_two * gain_two + shift_two).astype(bf16)
        pre = dot_nn(rows_two, w_fc1) + fc1_shift
        cdf = 0.5 * (1.0 + lax.erf(pre * 0.7071067811865476))
        act = (pre * cdf).astype(bf16)
        slope = (cdf + pre * jnp.exp(-0.5 * pre * pre) * 0.3989422804014327).astype(bf16)
        y = hidden + (dot_nt(act, w_fc2) + fc2_shift)
        y_rows = egress(order, inverse, micro, y.astype(bf16), quarter)

        gy_low = ingest(order, micro, gy_a, gy_b, half)
        gy = gy_low.astype(f32)
        fc2_shift_grad = jnp.sum(gy, axis=0)
        g_pre = (dot_nn(gy_low, w_fc2) * slope.astype(f32)).astype(bf16)
        cut = lambda v: (v[:, : v.shape[1] // 2], v[:, v.shape[1] // 2 :])
        fc1_shift_grad = jnp.sum(g_pre, axis=0, dtype=f32)
        g_c = dot_nt(g_pre, w_fc1)
        gain_two_grad = jnp.sum(g_c * hat_two, axis=0)
        shift_two_grad = jnp.sum(g_c, axis=0)
        g_hidden = gy + norm_back(g_c * gain_two, hat_two, inv_two)
        g_attn = g_hidden.astype(bf16)
        proj_shift_grad = jnp.sum(g_attn, axis=0, dtype=f32)
        g_heads = cut(dot_nn(g_attn, w_proj).astype(bf16))
        g_own = jnp.where(side == 0, g_heads[0], g_heads[1])
        g_oth = swap(jnp.where(side == 0, g_heads[1], g_heads[0]), 0)
        own, y_rows = lax.optimization_barrier((own, y_rows))
        parts = attend_back(
            info, own, oth, g_own, g_oth, o_own, o_oth, lse, q_ids[None, :], k_ids[:, None]
        )
        parts, (out_a, out_b) = lax.optimization_barrier((parts, give(*y_rows)))
        out = jnp.where(odd == 0, jnp.stack([out_a, out_b]), jnp.stack([out_b, out_a]))[:, None]

        def join(q, k, v):
            wide_t = q.shape[1] // 2
            return jnp.concatenate([p[:, i * wide_t : (i + 1) * wide_t] for i in range(2) for p in (q, k, v)], axis=1)

        d_own = join(*parts[:3])
        d_came = swap(join(*parts[3:]), 0)
        d_qkv = jnp.where(
            side == 0, jnp.concatenate([d_own, d_came], axis=1), jnp.concatenate([d_came, d_own], axis=1)
        )
        qkv_sum = jnp.sum(d_qkv, axis=0, dtype=f32).reshape(n_t, 3, -1)
        g_a = dot_nt(d_qkv, w_qkv)
        gain_one_grad = jnp.sum(g_a * hat_one, axis=0)
        shift_one_grad = jnp.sum(g_a, axis=0)
        grad_rows = (g_hidden + norm_back(g_a * gain_one, hat_one, inv_one)).astype(bf16)
        grad_rows = jnp.stack(egress(order, inverse, jnp.int32(0), grad_rows, quarter))

        fields = [gain_one_grad, shift_one_grad, proj_shift_grad, gain_two_grad, shift_two_grad, fc2_shift_grad]
        wide_g = jnp.stack(fields).reshape(6, n_dp, 1, size)
        wide_g = jnp.transpose(jnp.broadcast_to(wide_g, (6, n_dp, n_t, size)), (1, 0, 2, 3))
        fc1_g = jnp.transpose(fc1_shift_grad.reshape(n_t, n_dp, 1, size), (1, 2, 0, 3))
        qv_g = jnp.stack([qkv_sum[:, 0], qkv_sum[:, 2]], axis=1).reshape(n_t, 2, heads_t, n_dp, -1)
        qv_g = jnp.transpose(qv_g, (3, 0, 1, 2, 4)).reshape(n_dp, 1, n_t, -1)
        pad = lambda v: jnp.pad(v, ((0, 0), (0, 0), (0, 0), (0, lanes - v.shape[-1])))
        hidden_g = jnp.take(jnp.concatenate([pad(fc1_g), pad(qv_g)], axis=1), order, axis=0)
        small_g = jnp.concatenate([pad(wide_g), hidden_g], axis=1)
        small_g = small_g.reshape((2,) * bits + (8, n_t * lanes))

        fc2_grad, fc1_grad, qkv_grad, proj_grad, small_sum, tokens_grad = reduce_all(
            (gy_low, rows_two, rows_one, g_attn), (act, g_pre, d_qkv, heads), small_g, grad_rows, n_dp, n_t
        )
        wide_g = [small_sum[i, :size] for i in range(6)]
        fc1_g = small_sum[6:7, :size]
        qv_g = small_sum[7, : qv_bias.size].reshape(qv_bias.shape)
        return (
            out,
            tokens_grad[:, None],
            wide_g[0],
            wide_g[1],
            qkv_grad.reshape(qkv_weight.shape),
            qv_g,
            proj_grad.T,
            wide_g[2],
            wide_g[3],
            wide_g[4],
            fc1_grad,
            fc1_g,
            fc2_grad.T,
            wide_g[5],
        )

    return body


def solution(mesh):
    in_specs = (
        P(None, "dp", "tensor", None),
        P(None, "dp", None),
        P(None, "dp", None),
        P(None, "dp", "tensor", None),
        P("dp"),
        P("dp"),
        P("dp", None, "tensor"),
        P(None, "tensor", "dp"),
        P("tensor", "dp"),
        P("dp"),
        P("dp"),
        P("dp"),
        P("dp", "tensor"),
        P("tensor", "dp"),
        P("tensor", "dp"),
        P("dp"),
    )
    out_specs = (
        P(None, "dp", "tensor", None),
        P(None, "dp", "tensor", None),
        P("dp"),
        P("dp"),
        P("dp", None, "tensor"),
        P(None, "tensor", "dp"),
        P("tensor", "dp"),
        P("dp"),
        P("dp"),
        P("dp"),
        P("dp", "tensor"),
        P("tensor", "dp"),
        P("tensor", "dp"),
        P("dp"),
    )
    body = make_body(mesh.shape["dp"], mesh.shape["tensor"])
    return jax.shard_map(body, mesh=mesh, in_specs=in_specs, out_specs=out_specs, check_vma=False)
```

```python
import functools
import math

import jax
import jax.numpy as jnp
from jax import lax
from jax.experimental import pallas as pl
from jax.experimental.pallas import tpu as pltpu
from jax.sharding import PartitionSpec as P

bf16 = jnp.bfloat16
f32 = jnp.float32
epsilon = 1e-06
score_scale = 0.125
log2e = 1.4426950408889634
low_score = -1e30
block = 256
mib = 1 << 20


def dot_nn(left, right):
    return lax.dot_general(left, right, (((1,), (0,)), ((), ())), preferred_element_type=f32)


def dot_nt(left, right):
    return lax.dot_general(left, right, (((1,), (1,)), ((), ())), preferred_element_type=f32)


def dot_tn(left, right):
    return lax.dot_general(left, right, (((0,), (0,)), ((), ())), preferred_element_type=f32)


def lane_halves(rows):
    lane = lax.broadcasted_iota(jnp.int32, rows.shape, 1)
    zero = jnp.zeros_like(rows)
    return jnp.where(lane < 64, rows, zero), jnp.where(lane < 64, zero, rows)


def attend_kernel(
    info, qo, ko, vo, qr, kr, vr, seg_row, seg_col, out_own, out_oth, lse_ref,
    qts, vts, os, *per_head,
):
    half, wide = qo.shape
    heads = wide // 64
    blocks = 2 * half // block
    side = info[0]
    own_at = pl.multiple_of(side * half, half)
    oth_at = pl.multiple_of((1 - side) * half, half)
    ks, ss = per_head[:heads], per_head[heads:]
    for at, q_in, k_in, v_in in ((own_at, qo, ko, vo), (oth_at, qr, kr, vr)):
        rows = pl.ds(at, half)
        for i in range(heads // 2):
            pair = k_in[:, i * 128 : (i + 1) * 128]
            ks[2 * i][rows, :], ks[2 * i + 1][rows, :] = lane_halves(pair)
        for b in range(half // block):
            cols = pl.ds(pl.multiple_of(at + b * block, block), block)
            vts[:, cols] = v_in[b * block : (b + 1) * block, :].T
            qts[:, cols] = q_in[b * block : (b + 1) * block, :].T

    diff = lax.broadcasted_iota(jnp.int32, (block, block), 1) - lax.broadcasted_iota(
        jnp.int32, (block, block), 0
    )
    factor = score_scale * log2e

    def per_rows(qb, carry):
        q_at = pl.multiple_of(qb * block, block)
        q_cols = pl.ds(q_at, block)
        q_seg = seg_row[0:1, q_cols]
        first, last = info[1 + qb], info[1 + blocks + qb]

        def scan(kb, tops):
            k_at = pl.multiple_of(kb * block, block)
            keys = pl.ds(k_at, block)
            mask = (q_seg == seg_col[keys, :]) | (diff == k_at - q_at)
            out = []
            for i in range(heads):
                q = qts[i // 2 * 128 : i // 2 * 128 + 128, q_cols]
                s = jnp.where(mask, dot_nn(ks[i][keys, :], q), low_score)
                ss[i][kb] = s
                out.append(jnp.maximum(tops[i], jnp.max(s.reshape(block // 8, 8, block), axis=0)))
            return tuple(out)

        start = jnp.full((8, block), low_score, f32)
        tops = lax.fori_loop(first, last, scan, (start,) * heads)
        tops = [jnp.max(top, axis=0, keepdims=True) * factor for top in tops]

        def mix(kb, state):
            keys = pl.ds(pl.multiple_of(kb * block, block), block)
            done = []
            for i in range(heads):
                p = jnp.exp2(ss[i][kb] * factor - tops[i])
                done.append(state[2 * i] + jnp.sum(p.reshape(block // 8, 8, block), axis=0))
                done.append(
                    state[2 * i + 1] + dot_nn(vts[i * 64 : (i + 1) * 64, keys], p.astype(bf16))
                )
            return tuple(done)

        zeros = (jnp.zeros((8, block), f32), jnp.zeros((64, block), f32))
        state = lax.fori_loop(first, last, mix, zeros * heads)
        mixed = []
        for i in range(heads):
            total = jnp.sum(state[2 * i], axis=0, keepdims=True)
            mixed.append(state[2 * i + 1] / total)
            lse_ref[0, i : i + 1, q_cols] = tops[i] + jnp.log2(total)
        os[q_cols, :] = jnp.concatenate(mixed, axis=0).T.astype(bf16)
        return carry

    lax.fori_loop(0, blocks, per_rows, 0)
    out_own[...] = os[pl.ds(own_at, half), :]
    out_oth[...] = os[pl.ds(oth_at, half), :]


def attend(info, own, oth, seg_row, seg_col):
    half = own.shape[0]
    rows = 2 * half
    groups = own.shape[1] // 768

    def part(which):
        return pl.BlockSpec((half, 256), lambda i, _: (0, i * 3 + which))

    whole = lambda shape: pl.BlockSpec(shape, lambda i, _: (0,) * len(shape))
    return pl.pallas_call(
        attend_kernel,
        grid_spec=pltpu.PrefetchScalarGridSpec(
            num_scalar_prefetch=1,
            grid=(groups,),
            in_specs=[part(0), part(1), part(2)] * 2 + [whole((1, rows)), whole((rows, 1))],
            out_specs=[
                pl.BlockSpec((half, 256), lambda i, _: (0, i)),
                pl.BlockSpec((half, 256), lambda i, _: (0, i)),
                pl.BlockSpec((1, 8, rows), lambda i, _: (i, 0, 0)),
            ],
            scratch_shapes=[pltpu.VMEM((256, rows), bf16)] * 2
            + [pltpu.VMEM((rows, 256), bf16)]
            + [pltpu.VMEM((rows, 128), bf16)] * 4
            + [pltpu.VMEM((rows // block, block, block), f32)] * 4,
        ),
        out_shape=(
            jax.ShapeDtypeStruct((half, groups * 256), bf16),
            jax.ShapeDtypeStruct((half, groups * 256), bf16),
            jax.ShapeDtypeStruct((groups, 8, rows), f32),
        ),
        compiler_params=pltpu.CompilerParams(vmem_limit_bytes=60 * mib),
        cost_estimate=pl.CostEstimate(
            flops=int(groups * 4 * rows * rows * 256 * 1.5), bytes_accessed=int(own.size * 5), transcendentals=0
        ),
        name="attend",
    )(info, own, own, own, oth, oth, oth, seg_row, seg_col)


def attend_back_kernel(
    info, qo, ko, vo, qr, kr, vr, go, gr, oo, orr, lse_ref, seg_row, seg_col,
    d_own, d_oth, qts, gts, kts, os, dqs, dks, dvs, *per_head,
):
    half, wide = qo.shape
    heads = wide // 64
    blocks = 2 * half // block
    side = info[0]
    own_at = pl.multiple_of(side * half, half)
    oth_at = pl.multiple_of((1 - side) * half, half)
    qs, ks, vs, gs = [per_head[i * heads : (i + 1) * heads] for i in range(4)]
    for at, q_in, k_in, v_in, g_in, o_in in (
        (own_at, qo, ko, vo, go, oo),
        (oth_at, qr, kr, vr, gr, orr),
    ):
        rows = pl.ds(at, half)
        for refs, value in ((qs, q_in), (ks, k_in), (vs, v_in), (gs, g_in)):
            for i in range(heads // 2):
                pair = value[:, i * 128 : (i + 1) * 128]
                refs[2 * i][rows, :], refs[2 * i + 1][rows, :] = lane_halves(pair)
        for b in range(half // block):
            cols = pl.ds(pl.multiple_of(at + b * block, block), block)
            for ref, value in ((qts, q_in), (gts, g_in), (kts, k_in)):
                ref[:, cols] = value[b * block : (b + 1) * block, :].T
        os[rows, :] = o_in[...]
    dks[...] = jnp.zeros_like(dks)
    dvs[...] = jnp.zeros_like(dvs)

    diff = lax.broadcasted_iota(jnp.int32, (block, block), 1) - lax.broadcasted_iota(
        jnp.int32, (block, block), 0
    )
    factor = score_scale * log2e

    def per_rows(qb, carry):
        q_at = pl.multiple_of(qb * block, block)
        rows = pl.ds(q_at, block)
        product = gts[:, rows].astype(f32) * os[rows, :].T.astype(f32)
        inner = [jnp.sum(product[i * 64 : (i + 1) * 64], axis=0, keepdims=True) for i in range(heads)]
        lses = [lse_ref[0, i : i + 1, rows] for i in range(heads)]
        q_seg = seg_row[0:1, rows]

        def per_keys(kb, dq):
            k_at = pl.multiple_of(kb * block, block)
            keys = pl.ds(k_at, block)
            mask = (q_seg == seg_col[keys, :]) | (diff == k_at - q_at)
            dq_out, dk, dv = [], [], []
            for i in range(heads):
                pair = slice(i // 2 * 128, i // 2 * 128 + 128)
                s = dot_nn(ks[i][keys, :], qts[pair, rows]) * factor - lses[i]
                p = jnp.exp2(jnp.where(mask, s, low_score))
                dv.append(dot_nn(p.astype(bf16), gs[i][rows, :]))
                dp = dot_nn(vs[i][keys, :], gts[pair, rows])
                ds = (p * (dp - inner[i])).astype(bf16)
                dk.append(dot_nn(ds, qs[i][rows, :]))
                dq_out.append(dq[i] + dot_nn(kts[i * 64 : (i + 1) * 64, keys], ds))
            for i in range(0, heads, 2):
                pair = slice(i // 2 * 128, i // 2 * 128 + 128)
                dks[keys, pair] += dk[i] + dk[i + 1]
                dvs[keys, pair] += dv[i] + dv[i + 1]
            return tuple(dq_out)

        dq = lax.fori_loop(
            info[1 + qb], info[1 + blocks + qb], per_keys, (jnp.zeros((64, block), f32),) * heads
        )
        dqs[rows, :] = (jnp.concatenate(dq, axis=0) * score_scale).T.astype(bf16)
        return carry

    lax.fori_loop(0, blocks, per_rows, 0)
    for at, out in ((own_at, d_own), (oth_at, d_oth)):
        rows = pl.ds(at, half)
        out[:, :wide] = dqs[rows, :]
        out[:, wide : 2 * wide] = (dks[rows, :] * score_scale).astype(bf16)
        out[:, 2 * wide :] = dvs[rows, :].astype(bf16)


def attend_back(info, own, oth, g_own, g_oth, o_own, o_oth, lse, seg_row, seg_col):
    half = own.shape[0]
    rows = 2 * half
    groups = own.shape[1] // 768

    def part(which):
        return pl.BlockSpec((half, 256), lambda i, _: (0, i * 3 + which))

    col = pl.BlockSpec((half, 256), lambda i, _: (0, i))
    whole = lambda shape: pl.BlockSpec(shape, lambda i, _: (0,) * len(shape))
    shape = jax.ShapeDtypeStruct(own.shape, bf16)
    return pl.pallas_call(
        attend_back_kernel,
        grid_spec=pltpu.PrefetchScalarGridSpec(
            num_scalar_prefetch=1,
            grid=(groups,),
            in_specs=[part(0), part(1), part(2)] * 2
            + [col] * 4
            + [pl.BlockSpec((1, 8, rows), lambda i, _: (i, 0, 0))]
            + [whole((1, rows)), whole((rows, 1))],
            out_specs=[pl.BlockSpec((half, 768), lambda i, _: (0, i))] * 2,
            scratch_shapes=[pltpu.VMEM((256, rows), bf16)] * 3
            + [pltpu.VMEM((rows, 256), bf16)] * 2
            + [pltpu.VMEM((rows, 256), f32)] * 2
            + [pltpu.VMEM((rows, 128), bf16)] * 16,
        ),
        out_shape=(shape,) * 2,
        compiler_params=pltpu.CompilerParams(vmem_limit_bytes=60 * mib),
        cost_estimate=pl.CostEstimate(
            flops=int(groups * 10 * rows * rows * 256), bytes_accessed=int(own.size * 10), transcendentals=0
        ),
        name="attend_back",
    )(info, own, own, own, oth, oth, oth, g_own, g_oth, o_own, o_oth, lse, seg_row, seg_col)


def plan_gather(loads, bits, n_t, rows_load, row_gate, fused, later):
    tasks = {}
    for w, load in enumerate(loads):
        for s in range(n_t):
            last = None
            if s:
                last = (w, s, "z")
                tasks[last] = (None if s == 1 else (w, s - 1, "z"), "z", load)
            middle = list(range(1, bits))
            for k, bit in enumerate((middle if (w + s) % 2 == 0 else middle[::-1]) + [0]):
                if not (fused and w == later and k > 0):
                    tasks[(w, s, k)] = (last, bit, load << k)
                last = (w, s, k)
    tasks[("rows", 0, 0)] = ((row_gate, n_t - 1, "z"), "z", rows_load)
    tasks[("rows", 1, 0)] = (("rows", 0, 0), "z", rows_load)
    free, done, waiting = {}, {}, list(tasks)
    while waiting:
        ready = [
            (0.0 if tasks[t][0] is None else done[tasks[t][0]], i, t)
            for i, t in enumerate(waiting)
            if tasks[t][0] is None or tasks[t][0] in done
        ]
        start, _, task = min((max(r, free.get(tasks[t][1], 0.0)), i, t) for r, i, t in ready)
        _, link, load = tasks[task]
        done[task] = start + load / (150e3 if link == 0 else 44e3) + 3.0
        free[link] = done[task] - 3.0
        waiting.remove(task)
    order = sorted(done, key=lambda t: done[t])
    parents = {t: tasks[t][0] for t in order}
    steps = list(order)
    if fused:
        heavy = max(steps.index((0, s, bits - 1)) for s in range(n_t))
        small = max(steps.index((len(loads) - 1, s, bits - 1)) for s in range(n_t))
        at = max(heavy, small, steps.index(("rows", 0, 0)))
        steps.insert(at + 1, ("work", 0, 0))
        at = max(at + 1, steps.index(("rows", 1, 0)))
        steps.insert(at + 1, ("work", 1, 0))
    return parents, steps


def gather_kernel(n_dp, n_t, count, parents, steps, paired, fused, *refs):
    refs = list(refs)
    take = lambda n: [refs.pop(0) for _ in range(n)]
    (rows_ref,), own = take(1), take(count)
    (rows_out,), outs = take(1), take(count)
    if fused:
        x_out, a_out, near_out, far_out, wide_out, deep_out = take(6)
    send, recv, near = take(3)
    arrivals = [t for t in steps if t[0] != "work"]
    bits = n_dp.bit_length() - 1
    me, z = lax.axis_index("dp"), lax.axis_index("tensor")
    side = lax.rem(me, 2)
    base = me - side
    micro = z // 2
    number = {task: i for i, task in enumerate(arrivals)}
    greet(n_t, bits, me, z)
    flips = [bit_flip(me, bit) for bit in range(bits)]

    def slot(w, s, index, flip=0):
        cols = own[w].shape[1]
        at = s * cols
        if w in paired:
            whose = side if not flip else 1 - side
            at = pl.multiple_of(((s // 2 + whose) % 2 * 2 + s % 2) * cols, cols)
        return outs[w].at[index + (slice(None), pl.ds(at, cols))]

    def copy_of(task):
        w, s, k = task
        i = number[task]
        if k == "z":
            src = own[w] if s == 1 else slot(w, s - 1, (0,) * bits)
            dst = slot(w, s, (0,) * bits)
            where = (me, lax.rem(z + 1, n_t))
        else:
            middle = list(range(1, bits))
            order = (middle if (w + s) % 2 == 0 else middle[::-1]) + [0]
            bit = order[k]
            src_at, dst_at = [], []
            for axis in range(bits):
                if axis == bit:
                    src_at.append(0)
                    dst_at.append(1)
                else:
                    held = slice(None) if axis in order[:k] else 0
                    src_at.append(held)
                    dst_at.append(held)
            src = own[w] if (k == 0 and s == 0) else slot(w, s, tuple(src_at))
            dst = slot(w, s, tuple(dst_at), flip=bit == 0)
            where = (flips[bit], z)
        return pltpu.make_async_remote_copy(
            src_ref=src, dst_ref=dst, send_sem=send.at[i], recv_sem=recv.at[i],
            device_id=where, device_id_type=pl.DeviceIdType.MESH,
        )

    placed = []
    for w in range(count):
        placed.append(pltpu.make_async_copy(own[w], slot(w, 0, (0,) * bits), near.at[w]))
        placed[-1].start()

    place = lax.rem(z, 2)
    target_core = base + z // 2

    def rows_copy(m):
        i = [number[("rows", q, 0)] for q in range(2)]
        where = (target_core, 2 * m + side)
        mine = (side == z // 2) & (z == 2 * m + side)
        return i, where, mine

    def start_rows(turn):
        i = number[("rows", turn, 0)]
        for m in range(2):
            _, where, mine = rows_copy(m)
            now = lax.rem(place + m, 2) == turn

            @pl.when(now & mine)
            def _():
                pltpu.make_async_copy(rows_ref.at[m], rows_out.at[place], recv.at[i]).start()

            @pl.when(now & jnp.logical_not(mine))
            def _():
                pltpu.make_async_remote_copy(
                    src_ref=rows_ref.at[m], dst_ref=rows_out.at[place], send_sem=near.at[count + m],
                    recv_sem=recv.at[i], device_id=where, device_id_type=pl.DeviceIdType.MESH,
                ).start()

    if fused:
        w_buf, x_rows, x_buf, a_buf, q_buf, s_buf, pick, shift, gains, deep_buf, f_sem, fsend, frecv = refs
        quarter, width = x_rows.shape
        half = x_buf.shape[0]
        size = width // n_dp
        deep = w_buf.shape[1]
        lanes = s_buf.shape[-1] // n_t
        hd8 = fused // n_dp
        x_buf[2 * quarter :, :] = jnp.zeros((half - 2 * quarter, width), bf16)
        a_buf[2 * quarter :, :] = jnp.zeros((half - 2 * quarter, width), bf16)
        q_buf[2 * quarter :, :] = jnp.zeros((half - 2 * quarter, deep), bf16)

    def block_of(p):
        digits = sum(((p >> (bits - 1 - b)) & 1) << b for b in range(bits))
        spot = me
        for b in range(bits):
            if (digits >> b) & 1:
                spot = bit_flip(spot, b)
        return spot

    def prepare():
        pltpu.make_async_copy(outs[0].reshape(width, deep), w_buf, f_sem.at[0]).start()
        copy = pltpu.make_async_copy(outs[count - 1], s_buf, f_sem.at[1])
        copy.start()
        copy.wait()
        cells = [tuple((p >> (bits - 1 - b)) & 1 for b in range(bits)) for p in range(n_dp)]
        small = [s_buf[c].astype(f32) for c in cells]
        for p in range(n_dp):
            gains[:, p * size : (p + 1) * size] = small[p][0:8, :size]
            for s in range(n_t):
                at = pl.multiple_of(s * width + block_of(p) * size, size)
                deep_buf[:, pl.ds(at, size)] = jnp.broadcast_to(
                    small[p][6:7, s * lanes : s * lanes + size], (8, size)
                )
        n = lax.broadcasted_iota(jnp.int32, (lanes, 8 * 64), 1)
        i = lax.broadcasted_iota(jnp.int32, (lanes, 8 * 64), 0)
        source = n // 256 * (4 * hd8) + n % 256 // 64 * hd8 + n % hd8
        for p in range(n_dp):
            hit = (i == source) & (n % 64 // hd8 == block_of(p))
            pick[p * lanes : (p + 1) * lanes, :] = hit.astype(bf16)
        for s in range(n_t):
            line = jnp.concatenate([v[7:8, s * lanes : (s + 1) * lanes] for v in small], axis=1)
            line = jnp.broadcast_to(line, (8, n_dp * lanes)).astype(bf16)
            got = dot_nn(line, pick[...])
            at = pl.multiple_of(((s // 2 + side) % 2 * 2 + s % 2) * 768, 256)
            shift[:, pl.ds(at, 256)] = got[:, :256]
            shift[:, pl.ds(pl.multiple_of(at + 256, 256), 256)] = jnp.zeros((8, 256), f32)
            shift[:, pl.ds(pl.multiple_of(at + 512, 256), 256)] = got[:, 256:]
        pltpu.make_async_copy(outs[0].reshape(width, deep), w_buf, f_sem.at[0]).wait()

    def far_copy(turn):
        rows = pl.ds(pl.multiple_of(lax.rem(micro + turn, 2) * quarter, 16), quarter)
        return pltpu.make_async_remote_copy(
            src_ref=q_buf.at[rows, pl.ds(deep // 2, deep // 2)], dst_ref=far_out.at[rows, :],
            send_sem=fsend.at[turn], recv_sem=frecv.at[turn],
            device_id=(flips[0], z), device_id_type=pl.DeviceIdType.MESH,
        )

    def finals():
        pads = pl.ds(2 * quarter, half - 2 * quarter)
        return [
            pltpu.make_async_copy(x_buf, x_out, f_sem.at[3]),
            pltpu.make_async_copy(a_buf, a_out, f_sem.at[4]),
            pltpu.make_async_copy(gains, wide_out, f_sem.at[7]),
            pltpu.make_async_copy(deep_buf, deep_out, f_sem.at[8]),
            pltpu.make_async_copy(q_buf.at[:, pl.ds(0, deep // 2)], near_out, f_sem.at[5]),
            pltpu.make_async_copy(
                q_buf.at[pads, pl.ds(0, deep // 2)], far_out.at[pads, :], f_sem.at[6]
            ),
        ]

    def work(turn):
        q = lax.rem(micro + turn, 2)
        at = pl.multiple_of(q * quarter, 16)
        copy = pltpu.make_async_copy(rows_out.at[q], x_rows, f_sem.at[2])
        copy.start()
        if turn == 0:
            prepare()
        copy.wait()
        spots = [pl.multiple_of(block_of(p) * size, size) for p in range(n_dp)]

        def norm_rows(first, tall):
            src = pl.ds(pl.multiple_of(first, 16), tall)
            dst = pl.ds(pl.multiple_of(at + first, 16), tall)
            for p in range(n_dp):
                x_buf[dst, p * size : (p + 1) * size] = x_rows[src, pl.ds(spots[p], size)]
            hat, _ = norm_parts(x_buf[dst, :].astype(f32))
            a_buf[dst, :] = (hat * gains[0:1, :] + gains[1:2, :]).astype(bf16)

        def norm_block(r, carry):
            norm_rows(r * 80, 80)
            return carry

        lax.fori_loop(0, quarter // 80, norm_block, 0)
        if quarter % 80:
            norm_rows(quarter // 80 * 80, quarter % 80)
        rows = pl.ds(at, quarter)

        def column_block(n, carry):
            cols = pl.ds(pl.multiple_of(n * 256, 256), 256)
            value = dot_nn(a_buf[rows, :], w_buf[:, cols]) + shift[0:1, cols]
            q_buf[rows, cols] = value.astype(bf16)
            return carry

        lax.fori_loop(deep // 512, deep // 256, column_block, 0)
        far_copy(turn).start()
        lax.fori_loop(0, deep // 512, column_block, 0)
        if turn == 1:
            for copy in finals():
                copy.start()

    copies = {task: copy_of(task) for task in arrivals if task[0] != "rows"}
    for task in arrivals:
        if task[0] != "rows" and parents[task] is None:
            copies[task].start()
    landed = {w: False for w in range(count)}
    for task in steps:
        if task[0] == "work":
            work(task[1])
            continue
        if task[0] == "rows":
            q = lax.rem(micro + task[1], 2)
            pltpu.make_async_copy(rows_ref.at[0], rows_out.at[q], recv.at[number[task]]).wait()
        else:
            copies[task].wait_recv()
        for child in arrivals:
            if parents[child] == task and child[0] == "rows":
                start_rows(child[1])
            elif parents[child] == task:
                if child[1] == 0 and not landed[child[0]]:
                    placed[child[0]].wait()
                    landed[child[0]] = True
                copies[child].start()
    for w in range(count):
        if not landed[w]:
            placed[w].wait()
    for task in arrivals:
        if task[0] != "rows":
            copies[task].wait_send()
    for m in range(2):
        i, where, mine = rows_copy(m)

        @pl.when(jnp.logical_not(mine))
        def _():
            pltpu.make_async_remote_copy(
                src_ref=rows_ref.at[m], dst_ref=rows_out.at[0], send_sem=near.at[count + m],
                recv_sem=recv.at[i[0]], device_id=where, device_id_type=pl.DeviceIdType.MESH,
            ).wait_send()
    if fused:
        for copy in finals():
            copy.wait()
        for turn in range(2):
            far_copy(turn).wait()

def bit_flip(me, bit):
    span = 1 << bit
    return me + span - 2 * span * lax.rem(me // span, 2)


def gather_all(rows, own, n_dp, n_t, paired, half, head_size, later):
    bits = n_dp.bit_length() - 1
    quarter, width = rows.shape[1:]
    size = width // n_dp
    fused = head_size if size % 128 == 0 else 0
    parents, steps = plan_gather(
        [w.shape[0] * w.shape[1] * 2 for w in own], bits, n_t, rows[0].size * 2, 2, fused, later
    )
    count = len(own)
    arrivals = [t for t in steps if t[0] != "work"]
    hbm = pl.BlockSpec(memory_space=pl.ANY)
    shapes = [jax.ShapeDtypeStruct(rows.shape, bf16)]
    shapes += [
        jax.ShapeDtypeStruct((2,) * bits + (w.shape[0], n_t * w.shape[1]), w.dtype) for w in own
    ]
    scratch = [
        pltpu.SemaphoreType.DMA((len(arrivals),)),
        pltpu.SemaphoreType.DMA((len(arrivals),)),
        pltpu.SemaphoreType.DMA((count + 2,)),
    ]
    if fused:
        deep = n_t * own[0].shape[1]
        shapes += [jax.ShapeDtypeStruct((half, c), bf16) for c in (width, width, deep // 2, deep // 2)]
        shapes += [jax.ShapeDtypeStruct((8, c), f32) for c in (width, n_t * width)]
        scratch += [
            pltpu.VMEM((width, deep), bf16),
            pltpu.VMEM((quarter, width), bf16),
            pltpu.VMEM((half, width), bf16),
            pltpu.VMEM((half, width), bf16),
            pltpu.VMEM((half, deep), bf16),
            pltpu.VMEM((2,) * bits + (own[-1].shape[0], n_t * own[-1].shape[1]), bf16),
            pltpu.VMEM((n_dp * own[-1].shape[1], 512), bf16),
            pltpu.VMEM((8, deep), f32),
            pltpu.VMEM((8, width), f32),
            pltpu.VMEM((8, n_t * width), f32),
            pltpu.SemaphoreType.DMA((9,)),
            pltpu.SemaphoreType.DMA((2,)),
            pltpu.SemaphoreType.DMA((2,)),
        ]
    return pl.pallas_call(
        functools.partial(gather_kernel, n_dp, n_t, count, parents, steps, paired, fused),
        in_specs=[hbm] * (1 + count),
        out_specs=[hbm] * len(shapes),
        out_shape=tuple(shapes),
        scratch_shapes=scratch,
        compiler_params=pltpu.CompilerParams(
            collective_id=0, has_side_effects=True, vmem_limit_bytes=60 * mib
        ),
        cost_estimate=pl.CostEstimate(flops=0, bytes_accessed=300 * mib, transcendentals=0),
        name="gather_all",
    )(rows, *own)


def stage_bits(w, s, bits):
    middle = list(range(1, bits))
    return [0] + (middle if (w + s) % 2 == 0 else middle[::-1])


def plan_reduce(widths, size, bits, n_t, rows_load):
    turn = list(range(1, n_t)) + [0]
    last = len(widths)
    chunks = [(last, s) for s in turn]
    for s in turn:
        group = list(range(last))
        chunks += [(w, s) for w in (group[-1:] + group[:-1] if s == turn[0] else group)]
    ready, free, core, order = {}, {"z": rows_load / 44e3}, 0.0, []
    pending = {("make", w, s): 0.0 for w, s in chunks}
    rank = {c: i for i, c in enumerate(chunks)}
    arrived = {}
    while pending:
        def key(item):
            kind, w, s = item[0][0], item[0][1], item[0][2]
            begin = max(core, item[1])
            return (begin, kind == "make", rank[(w, s)])

        action, when = min(pending.items(), key=key)
        del pending[action]
        order.append(action)
        w, s = action[1], action[2]
        cols = 64 if w == last else widths[w]
        rows = 16 if w == last else size << (bits - 1)
        share = rows * cols / (512 * 1024)
        begin = max(core, when)
        core = begin + (4.5 * share + 2.0 if action[0] == "make" else 1.2 * share / (1 << action[3] if action[0] == "add" else 4) + 0.3)
        flow = stage_bits(w, s, bits)
        k = 0 if action[0] == "make" else action[3] + 1 if action[0] == "add" else None

        def send(link, load):
            begin = max(core, free.get(link, 0.0))
            free[link] = begin + load / (150e3 if link == 0 else 44e3)
            return free[link] + 5.0

        def to_z():
            if s != 0:
                nxt = turn[turn.index(s) + 1]
                arrived[(w, nxt)] = send("z", (rows >> (bits - 1)) * cols * 2)
                if (w, nxt) in ready:
                    pending[("z", w, nxt)] = arrived[(w, nxt)]

        if k is not None and k < bits:
            load = (rows >> k) * cols * 2
            pending[("add", w, s, k)] = send(flow[k], load)
        elif k is not None:
            ready[(w, s)] = core
            if s == turn[0]:
                to_z()
            elif (w, s) in arrived:
                pending[("z", w, s)] = arrived[(w, s)]
        else:
            to_z()
    return order


def greet(n_t, bits, me, z):
    side = lax.rem(me, 2)
    barrier = pltpu.get_barrier_semaphore()
    for dz in range(n_t):
        for other in range(2):
            if dz or other:
                where = (me - side + lax.rem(side + other, 2), lax.rem(z + dz, n_t))
                pl.semaphore_signal(barrier, inc=1, device_id=where, device_id_type=pl.DeviceIdType.MESH)
    for bit in range(1, bits):
        where = (bit_flip(me, bit), z)
        pl.semaphore_signal(barrier, inc=1, device_id=where, device_id_type=pl.DeviceIdType.MESH)
    pl.semaphore_wait(barrier, 2 * n_t - 1 + bits - 1)


def reduce_kernel(n_dp, n_t, plan, widths, paired, *refs):
    bits = n_dp.bit_length() - 1
    count = len(widths)
    refs = list(refs)
    take = lambda n: [refs.pop(0) for _ in range(n)]
    xs, gs, (small_in, rows_in) = take(count), take(count), take(2)
    outs, (small_out, rows_out) = take(count), take(2)
    kept, came, zcame = take(count + 1), take(count + 1), take(count + 1)
    later = [take(bits - 1) for _ in range(count + 1)]
    (away, away_small, x_buf, x_turn, g_buf) = take(5)
    (x_sem, g_sem, s_sem, r_sem, send, recv, zsend, zrecv) = take(8)
    me, z = lax.axis_index("dp"), lax.axis_index("tensor")
    turn = list(range(1, n_t)) + [0]
    blk = kept[0].shape[-2]
    tall = blk << (bits - 1)
    greet(n_t, bits, me, z)

    side = lax.rem(me, 2)
    micro, owner = z // 2, lax.rem(z, 2)

    def rows_to(q):
        where = (me - side + owner, 2 * side + q)
        mine = (owner == side) & (2 * side + q == z)
        return where, mine

    def rows_from(m):
        return (side == z // 2) & (2 * m + side == z)

    for q in range(2):
        where, mine = rows_to(q)
        for m in range(2):

            @pl.when((micro == m) & mine)
            def _():
                pltpu.make_async_copy(rows_in.at[q], rows_out.at[m], r_sem.at[2 + m]).start()

            @pl.when((micro == m) & jnp.logical_not(mine))
            def _():
                pltpu.make_async_remote_copy(
                    src_ref=rows_in.at[q], dst_ref=rows_out.at[m], send_sem=r_sem.at[q],
                    recv_sem=r_sem.at[2 + m], device_id=where, device_id_type=pl.DeviceIdType.MESH,
                ).start()

    made = [a for a in plan if a[0] == "make" and a[1] < count]

    def fetch(i):
        _, w, s = made[i]
        c = widths[w]
        at = s * c
        if w in paired:
            at = pl.multiple_of(((s // 2 + side) % 2 * 2 + s % 2) * c, c)
        return pltpu.make_async_copy(
            gs[w].at[:, pl.ds(at, c)], g_buf.at[i % 2, :, pl.ds(0, c)], g_sem.at[i % 2]
        )

    def fetch_x(w):
        return pltpu.make_async_copy(xs[w], x_buf, x_sem)

    def at_stage(w, s, k, taken):
        flow = stage_bits(w, s, bits)
        return tuple(
            0 if bit in flow[:k] else (taken if bit == flow[k] else slice(None)) for bit in range(1, bits)
        )

    def landing(w, s, k):
        ref = came[w] if k == 0 else later[w][k - 1]
        return ref.at[s]

    def copy_of(w, s, k):
        flow = stage_bits(w, s, bits)
        if k == 0:
            src = away_small.at[s] if w == count else away_view(w, s)
        else:
            src = kept[w].at[(s,) + at_stage(w, s, k, 1)]
        return pltpu.make_async_remote_copy(
            src_ref=src, dst_ref=landing(w, s, k), send_sem=send.at[w, s, k], recv_sem=recv.at[w, s, k],
            device_id=(bit_flip(me, flow[k]), z), device_id_type=pl.DeviceIdType.MESH,
        )

    def away_view(w, s):
        i = made.index(("make", w, s)) % 2
        return away.at[(i,) + (slice(None),) * bits + (pl.ds(0, widths[w]),)]

    def zcopy(w, s):
        nxt = turn[turn.index(s) + 1]
        return pltpu.make_async_remote_copy(
            src_ref=kept[w].at[(s,) + (0,) * (bits - 1)], dst_ref=zcame[w].at[nxt],
            send_sem=zsend.at[w, s], recv_sem=zrecv.at[w, nxt],
            device_id=(me, lax.rem(z + 1, n_t)), device_id_type=pl.DeviceIdType.MESH,
        )

    def finish(w, s, total):
        ref = small_out if w == count else outs[w]
        ref[...] = total

    fetch(0).start()
    fetch_x(made[0][1]).start()
    for action in plan:
        kind, w, s = action[:3]
        if kind == "make" and w == count:
            lanes = small_out.shape[-1]
            cols = pl.ds(s * lanes, lanes)
            for half, dst in ((1, away_small.at[s]), (0, kept[w].at[s])):
                src = small_in.at[(half,) + (slice(None),) * bits + (cols,)]
                pltpu.make_async_copy(src, dst, s_sem.at[half]).start()
            for half, dst in ((1, away_small.at[s]), (0, kept[w].at[s])):
                src = small_in.at[(half,) + (slice(None),) * bits + (cols,)]
                pltpu.make_async_copy(src, dst, s_sem.at[half]).wait()
            copy_of(w, s, 0).start()
        elif kind == "make":
            i = made.index(action)
            c = widths[w]
            if i == 0 or made[i - 1][1] != w:
                fetch_x(w).wait()
                for a in range(x_buf.shape[1] // 256):

                    def turn_block(b, carry, a=a):
                        rows = pl.ds(pl.multiple_of(b * 256, 256), 256)
                        x_turn[a * 256 : (a + 1) * 256, rows] = x_buf[rows, a * 256 : (a + 1) * 256].T
                        return carry

                    lax.fori_loop(0, x_buf.shape[0] // 256, turn_block, 0)
                follow = [m[1] for m in made[i:] if m[1] != w]
                if follow:
                    fetch_x(follow[0]).start()
            fetch(i).wait()
            if i + 1 < len(made):
                fetch(i + 1).start()
            if i >= 2:
                copy_of(*made[i - 2][1:], 0).wait_send()
            whole = (slice(None),) * bits

            def away_block(n, carry):
                cols = pl.ds(pl.multiple_of(n * 256, 256), 256)
                value = dot_nn(x_turn[tall:, :], g_buf[i % 2, :, cols]).astype(bf16)
                away[(i % 2,) + whole + (cols,)] = value.reshape((2,) * (bits - 1) + (blk, 256))
                return carry

            lax.fori_loop(0, c // 256, away_block, 0)
            copy_of(w, s, 0).start()

            def kept_block(n, carry):
                cols = pl.ds(pl.multiple_of(n * 256, 256), 256)
                value = dot_nn(x_turn[:tall, :], g_buf[i % 2, :, cols]).astype(bf16)
                kept[w][(s,) + whole + (cols,)] = value.reshape((2,) * (bits - 1) + (blk, 256))
                return carry

            lax.fori_loop(0, c // 256, kept_block, 0)
        elif kind == "add":
            k = action[3]
            copy_of(w, s, k).wait_recv()
            place = (s,) + (slice(None),) * (bits - 1) if k == 0 else (s,) + at_stage(w, s, k, 0)
            got = (came[w] if k == 0 else later[w][k - 1])[s]
            held = kept[w][place]
            kept[w][place] = (held.astype(f32) + got.astype(f32)).astype(held.dtype)
            if k + 1 < bits:
                copy_of(w, s, k + 1).start()
            elif s == turn[0]:
                zcopy(w, s).start()
        else:
            before = turn[turn.index(s) - 1]
            zcopy(w, before).wait_recv()
            place = (s,) + (0,) * (bits - 1)
            total = kept[w][place].astype(f32) + zcame[w][s].astype(f32)
            if s == turn[-1]:
                finish(w, s, total)
            else:
                kept[w][place] = total.astype(kept[w].dtype)
                zcopy(w, s).start()
    for w in range(count + 1):
        for s in turn:
            for k in range(bits):
                if k == 0 and w < count and made.index(("make", w, s)) < len(made) - 2:
                    continue
                copy_of(w, s, k).wait_send()
            if s != turn[-1]:
                zcopy(w, s).wait_send()
    for q in range(2):
        where, mine = rows_to(q)

        @pl.when(jnp.logical_not(mine))
        def _():
            pltpu.make_async_remote_copy(
                src_ref=rows_in.at[q], dst_ref=rows_out.at[0], send_sem=r_sem.at[q],
                recv_sem=r_sem.at[2], device_id=where, device_id_type=pl.DeviceIdType.MESH,
            ).wait_send()
    for m in range(2):
        pltpu.make_async_copy(rows_in.at[0], rows_out.at[m], r_sem.at[2 + m]).wait()


def reduce_all(xs, gs, small, rows, n_dp, n_t, paired):
    bits = n_dp.bit_length() - 1
    count = len(xs)
    width = xs[0].shape[1]
    size = width // n_dp
    widths = [g.shape[1] // n_t for g in gs]
    lanes = small.shape[-1] // n_t
    plan = plan_reduce(widths, size, bits, n_t, rows[0].size * 2)
    cells = (2,) * (bits - 1)
    shapes = [(size, c, bf16) for c in widths] + [(small.shape[-2], lanes, f32)]
    hbm, vmem = pl.BlockSpec(memory_space=pl.ANY), pl.BlockSpec(memory_space=pltpu.VMEM)
    scratch = [pltpu.VMEM((n_t,) + cells + (r, c), t) for r, c, t in shapes]
    scratch += [pltpu.VMEM((n_t,) + cells + (r, c), t) for r, c, t in shapes]
    scratch += [pltpu.VMEM((n_t, r, c), t) for r, c, t in shapes]
    for r, c, t in shapes:
        scratch += [pltpu.VMEM((n_t,) + (2,) * (bits - 1 - k) + (r, c), t) for k in range(1, bits)]
    scratch += [
        pltpu.VMEM((2,) + cells + (size, max(widths)), bf16),
        pltpu.VMEM((n_t,) + cells + (small.shape[-2], lanes), f32),
        pltpu.VMEM(xs[0].shape, bf16),
        pltpu.VMEM((width, xs[0].shape[0]), bf16),
        pltpu.VMEM((2, gs[0].shape[0], max(widths)), bf16),
        pltpu.SemaphoreType.DMA,
        pltpu.SemaphoreType.DMA((2,)),
        pltpu.SemaphoreType.DMA((2,)),
        pltpu.SemaphoreType.DMA((4,)),
        pltpu.SemaphoreType.DMA((count + 1, n_t, bits)),
        pltpu.SemaphoreType.DMA((count + 1, n_t, bits)),
        pltpu.SemaphoreType.DMA((count + 1, n_t)),
        pltpu.SemaphoreType.DMA((count + 1, n_t)),
    ]
    return pl.pallas_call(
        functools.partial(reduce_kernel, n_dp, n_t, plan, widths, paired),
        in_specs=[hbm] * (2 * count + 2),
        out_specs=[vmem] * (count + 1) + [hbm],
        out_shape=tuple(jax.ShapeDtypeStruct((size, c), f32) for c in widths)
        + (
            jax.ShapeDtypeStruct((small.shape[-2], lanes), f32),
            jax.ShapeDtypeStruct(rows.shape, rows.dtype),
        ),
        scratch_shapes=scratch,
        compiler_params=pltpu.CompilerParams(
            collective_id=1, has_side_effects=True, vmem_limit_bytes=60 * mib
        ),
        cost_estimate=pl.CostEstimate(
            flops=2 * xs[0].size * n_t * sum(widths), bytes_accessed=200 * mib, transcendentals=0
        ),
        name="reduce_all",
    )(*xs, *gs, small, rows)


def gelu_parts(v):
    bell = jnp.exp2(v * v * (-0.5 * log2e))
    t = 1.0 / (1.0 + jnp.abs(v) * (0.3275911 * 0.7071067811865476))
    poly = t * (
        0.254829592 * 0.5
        + t * (-0.284496736 * 0.5 + t * (1.421413741 * 0.5 + t * (-1.453152027 * 0.5 + t * (1.061405429 * 0.5))))
    )
    tail = poly * bell
    cdf = jnp.where(v < 0.0, tail, 1.0 - tail)
    return v * cdf, cdf + v * bell * 0.3989422804014327


def mlp_kernel(
    n_dp, n_t, o_own, o_oth, x_in, w_proj, w_fc1, w_fc2_in, cot, wide, deep_shift,
    heads_out, c_out, act_out, gpre_out, gy_out, gh_out, gattn_out, g_own, g_oth, y_a, y_b, gy_mid, w_fc2_parts,
    sums, deep_sums,
    heads, x_buf, h_buf, c_buf, act, slope, o_buf, gy, gc, wp, col_buf, row_buf, stage,
    col_sem, row_sem, load_sem, save_sem, out_sem, cot_send, cot_recv, swap_send, swap_recv,
    rest_send, rest_recv,
):
    bits = n_dp.bit_length() - 1
    me, z = lax.axis_index("dp"), lax.axis_index("tensor")
    side = lax.rem(me, 2)
    base = me - side
    micro, place = z // 2, lax.rem(z, 2)
    half, width = x_buf.shape
    quarter = stage.shape[0]
    size = width // n_dp
    deep = act.shape[1]
    mesh_id = pl.DeviceIdType.MESH
    partner = (bit_flip(me, 0), z)
    greet(n_t, bits, me, z)
    w_fc2 = w_fc2_parts.reshape(width, deep)

    def far_heads():
        return pltpu.make_async_remote_copy(
            src_ref=o_oth, dst_ref=heads.at[:, pl.ds(width // 2, width // 2)],
            send_sem=swap_send.at[0], recv_sem=swap_recv.at[0], device_id=partner, device_id_type=mesh_id,
        )

    far_heads().start()
    loads = [
        pltpu.make_async_copy(o_own, heads.at[:, pl.ds(0, width // 2)], load_sem.at[0]),
        pltpu.make_async_copy(x_in, x_buf, load_sem.at[1]),
        pltpu.make_async_copy(w_proj, wp, load_sem.at[2]),
    ]
    for copy in loads:
        copy.start()

    def rest(s, k):
        flow = stage_bits(2, s, bits)
        flow = flow[1:] + flow[:1]
        cols = pl.ds(s * width, width)
        src_at = tuple(0 if b == flow[k] or b not in flow[:k] else slice(None) for b in range(bits))
        dst_at = tuple(1 if b == flow[k] else a for b, a in enumerate(src_at))
        return pltpu.make_async_remote_copy(
            src_ref=w_fc2_parts.at[src_at + (slice(None), cols)],
            dst_ref=w_fc2_parts.at[dst_at + (slice(None), cols)],
            send_sem=rest_send.at[s, k], recv_sem=rest_recv.at[s, k],
            device_id=(bit_flip(me, flow[k]), z), device_id_type=mesh_id,
        )

    for s in range(n_t):
        rest(s, 1).start()

    def cot_copy(turn):
        m = lax.rem(place + turn, 2)
        where, mine = (base + z // 2, 2 * m + side), (side == z // 2) & (z == 2 * m + side)
        here = pltpu.make_async_copy(cot.at[m], gy_mid.at[turn], cot_recv.at[turn])
        there = pltpu.make_async_remote_copy(
            src_ref=cot.at[m], dst_ref=gy_mid.at[turn], send_sem=cot_send.at[turn],
            recv_sem=cot_recv.at[turn], device_id=where, device_id_type=mesh_id,
        )
        return here, there, mine

    for turn in range(2):
        here, there, mine = cot_copy(turn)

        @pl.when(mine)
        def _():
            here.start()

        @pl.when(jnp.logical_not(mine))
        def _():
            there.start()

    def cols_of(ref, n):
        slot = lax.rem(n, 2)
        return pltpu.make_async_copy(
            ref.at[:, pl.ds(pl.multiple_of(n * 1024, 1024), 1024)], col_buf.at[slot], col_sem.at[slot]
        )

    def rows_of(ref, n):
        slot = lax.rem(n, 2)
        return pltpu.make_async_copy(
            ref.at[pl.ds(pl.multiple_of(n * 256, 256), 256), :], row_buf.at[slot], row_sem.at[slot]
        )

    def stream(ref, fetch, count, use):
        def one(n, carry):
            fetch(ref, n).wait()

            @pl.when(n + 1 < count)
            def _():
                fetch(ref, n + 1).start()

            use(n, lax.rem(n, 2))
            return carry

        lax.fori_loop(0, count, one, 0)

    cols_of(w_fc1, 0).start()
    for copy in loads:
        copy.wait()
    far_heads().wait_recv()
    pltpu.make_async_copy(heads, heads_out, save_sem.at[0]).start()

    chunk = half // 1

    def by_rows(body):
        def one(r, carry):
            body(pl.ds(pl.multiple_of(r * chunk, chunk), chunk))
            return carry

        lax.fori_loop(0, half // chunk, one, 0)

    def proj_block(n, carry):
        cols = pl.ds(pl.multiple_of(n * 256, 256), 256)

        def body(rows):
            value = dot_nt(heads[rows, :], wp[cols, :]) + wide[2:3, cols]
            h_buf[rows, cols] = x_buf[rows, cols].astype(f32) + value

        by_rows(body)
        return carry

    lax.fori_loop(0, width // 256, proj_block, 0)

    def norm_block(r, carry):
        rows = pl.ds(pl.multiple_of(r * 128, 128), 128)
        hat, _ = norm_parts(h_buf[rows, :])
        c_buf[rows, :] = (hat * wide[3:4, :] + wide[4:5, :]).astype(bf16)
        return carry

    lax.fori_loop(0, half // 128, norm_block, 0)
    pltpu.make_async_copy(c_buf, c_out, save_sem.at[1]).start()

    def fc1_block(n, slot):
        cols = pl.ds(pl.multiple_of(n * 1024, 1024), 1024)

        def body(rows):
            value, grade = gelu_parts(dot_nn(c_buf[rows, :], col_buf[slot]) + deep_shift[0:1, cols])
            act[rows, cols] = value.astype(bf16)
            slope[rows, cols] = grade.astype(bf16)

        by_rows(body)

    pieces = deep // 1024
    sent = 0
    for n in range(pieces):
        cols_of(w_fc1, n).wait()
        if n + 1 < pieces:
            cols_of(w_fc1, n + 1).start()
        fc1_block(n, n % 2)
        ready = {1: n_t // 2, pieces - 1: n_t}.get(n, sent)
        for s in range(sent, ready):
            for k in range(2, bits):
                rest(s, k - 1).wait_recv()
                rest(s, k).start()
        sent = ready
    for s in range(n_t):
        rest(s, bits - 1).wait_recv()
    rows_of(w_fc2, 0).start()
    cols_of(w_fc2, 0).start()
    pltpu.make_async_copy(act, act_out, save_sem.at[2]).start()

    def spot(p):
        digits = sum(((p >> (bits - 1 - b)) & 1) << b for b in range(bits))
        at = me
        for b in range(bits):
            if (digits >> b) & 1:
                at = bit_flip(at, b)
        return pl.ds(pl.multiple_of(at * size, size), size)

    def fc2_block(n, slot):
        cols = pl.ds(pl.multiple_of(n * 256, 256), 256)

        def body(rows):
            value = dot_nt(act[rows, :], row_buf[slot]) + wide[5:6, cols]
            o_buf[rows, cols] = (h_buf[rows, cols] + value).astype(bf16)

        by_rows(body)

    stream(w_fc2, rows_of, width // 256, fc2_block)
    rows_of(w_fc1, 0).start()

    def unorder(r, carry):
        rows = pl.ds(pl.multiple_of(r * 16, 16), 16)
        line = o_buf[rows, :]
        for p in range(n_dp):
            x_buf[rows, spot(p)] = line[:, p * size : (p + 1) * size]
        return carry

    lax.fori_loop(0, half // 16, unorder, 0)

    for q in range(2):
        src = x_buf.at[pl.ds(q * quarter, quarter), :]
        for first in range(2):

            @pl.when(micro == first)
            def _():
                pltpu.make_async_copy(src, (y_a, y_b)[(q + first) % 2], out_sem.at[q]).start()

    gy[2 * quarter :, :] = jnp.zeros((half - 2 * quarter, width), bf16)
    for turn in range(2):
        cot_copy(turn)[0].wait()
        at = lax.rem(micro + turn, 2) * quarter
        copy = pltpu.make_async_copy(gy_mid.at[turn], stage, load_sem.at[0])
        copy.start()
        copy.wait()

        def reorder(r, carry):
            src = pl.ds(pl.multiple_of(r * 16, 16), 16)
            dst = pl.ds(pl.multiple_of(at + r * 16, 16), 16)
            for p in range(n_dp):
                gy[dst, p * size : (p + 1) * size] = stage[src, spot(p)]
            return carry

        lax.fori_loop(0, quarter // 16, reorder, 0)
    pltpu.make_async_copy(gy, gy_out, save_sem.at[3]).start()

    def gpre_block(n, slot):
        cols = pl.ds(pl.multiple_of(n * 1024, 1024), 1024)
        deep_sums[:, cols] = jnp.zeros((8, 1024), f32)

        def body(rows):
            value = dot_nn(gy[rows, :], col_buf[slot]) * slope[rows, cols].astype(f32)
            low = value.astype(bf16)
            slope[rows, cols] = low
            deep_sums[:, cols] += jnp.sum(low.astype(f32).reshape(chunk // 8, 8, 1024), axis=0)

        by_rows(body)

    stream(w_fc2, cols_of, deep // 1024, gpre_block)
    pltpu.make_async_copy(slope, gpre_out, save_sem.at[4]).start()

    def gc_block(n, slot):
        cols = pl.ds(pl.multiple_of(n * 256, 256), 256)

        def body(rows):
            gc[rows, cols] = dot_nt(slope[rows, :], row_buf[slot])

        by_rows(body)

    stream(w_fc1, rows_of, width // 256, gc_block)

    sums[...] = jnp.zeros_like(sums)

    def back_block(r, carry):
        rows = pl.ds(pl.multiple_of(r * 128, 128), 128)
        hat, inverse = norm_parts(h_buf[rows, :])
        g_c = gc[rows, :]
        g_y = gy[rows, :].astype(f32)
        g_h = g_y + norm_back(g_c * wide[3:4, :], hat, inverse)
        low = g_h.astype(bf16)
        gc[rows, :] = g_h
        o_buf[rows, :] = low
        for i, value in enumerate((low.astype(f32), g_c * hat, g_c, g_y)):
            sums[i] += jnp.sum(value.reshape(16, 8, width), axis=0)
        return carry

    lax.fori_loop(0, half // 128, back_block, 0)
    pltpu.make_async_copy(gc, gh_out, save_sem.at[5]).start()
    pltpu.make_async_copy(o_buf, gattn_out, save_sem.at[6]).start()

    pltpu.make_async_copy(heads, heads_out, save_sem.at[0]).wait()

    def gheads_block(n, carry):
        cols = pl.ds(pl.multiple_of(n * 256, 256), 256)

        def body(rows):
            heads[rows, cols] = dot_nn(o_buf[rows, :], wp[:, cols]).astype(bf16)

        by_rows(body)
        return carry

    lax.fori_loop(width // 512, width // 256, gheads_block, 0)
    far = pltpu.make_async_remote_copy(
        src_ref=heads.at[:, pl.ds(width // 2, width // 2)], dst_ref=g_oth,
        send_sem=swap_send.at[1], recv_sem=swap_recv.at[1], device_id=partner, device_id_type=mesh_id,
    )
    far.start()
    lax.fori_loop(0, width // 512, gheads_block, 0)
    near = pltpu.make_async_copy(heads.at[:, pl.ds(0, width // 2)], g_own, load_sem.at[1])
    near.start()

    pltpu.make_async_copy(c_buf, c_out, save_sem.at[1]).wait()
    pltpu.make_async_copy(act, act_out, save_sem.at[2]).wait()
    pltpu.make_async_copy(gy, gy_out, save_sem.at[3]).wait()
    pltpu.make_async_copy(slope, gpre_out, save_sem.at[4]).wait()
    pltpu.make_async_copy(gc, gh_out, save_sem.at[5]).wait()
    pltpu.make_async_copy(o_buf, gattn_out, save_sem.at[6]).wait()
    near.wait()
    far.wait()
    far_heads().wait_send()
    for turn in range(2):
        here, there, mine = cot_copy(turn)

        @pl.when(jnp.logical_not(mine))
        def _():
            there.wait_send()

    for s in range(n_t):
        for k in range(1, bits):
            rest(s, k).wait_send()
    for q in range(2):
        pltpu.make_async_copy(x_buf.at[pl.ds(q * quarter, quarter), :], y_a, out_sem.at[q]).wait()


def mlp(o_own, o_oth, x, w_proj, w_fc1, w_fc2, cot, wide, deep_shift, n_dp, n_t):
    half, width = x.shape
    deep = w_fc1.shape[1]
    quarter = cot.shape[1]
    hbm, vmem = pl.BlockSpec(memory_space=pl.ANY), pl.BlockSpec(memory_space=pltpu.VMEM)
    shape = jax.ShapeDtypeStruct
    row, tall = shape((half, width), bf16), shape((half, deep), bf16)
    dma = pltpu.SemaphoreType.DMA
    outs = pl.pallas_call(
        functools.partial(mlp_kernel, n_dp, n_t),
        in_specs=[hbm] * 7 + [vmem] * 2,
        out_specs=[hbm] * 13 + [vmem] * 2,
        input_output_aliases={5: 12},
        out_shape=(
            row, row, tall, tall, row, shape((half, width), f32), row,
            shape(o_own.shape, bf16), shape(o_own.shape, bf16), shape(cot.shape[1:], bf16),
            shape(cot.shape[1:], bf16), shape(cot.shape, bf16), shape(w_fc2.shape, bf16),
            shape((4, 8, width), f32), shape((8, deep), f32),
        ),
        scratch_shapes=[
            pltpu.VMEM((half, width), bf16),
            pltpu.VMEM((half, width), bf16),
            pltpu.VMEM((half, width), f32),
            pltpu.VMEM((half, width), bf16),
            pltpu.VMEM((half, deep), bf16),
            pltpu.VMEM((half, deep), bf16),
            pltpu.VMEM((half, width), bf16),
            pltpu.VMEM((half, width), bf16),
            pltpu.VMEM((half, width), f32),
            pltpu.VMEM((width, width), bf16),
            pltpu.VMEM((2, width, 1024), bf16),
            pltpu.VMEM((2, 256, deep), bf16),
            pltpu.VMEM((quarter, width), bf16),
            dma((2,)), dma((2,)), dma((3,)), dma((7,)), dma((2,)), dma((2,)), dma((2,)), dma((2,)),
            dma((2,)), dma((n_t, n_dp.bit_length() - 1)), dma((n_t, n_dp.bit_length() - 1)),
        ],
        compiler_params=pltpu.CompilerParams(
            collective_id=2, has_side_effects=True, vmem_limit_bytes=60 * mib
        ),
        cost_estimate=pl.CostEstimate(
            flops=2 * half * width * (4 * deep + 2 * width), bytes_accessed=90 * mib, transcendentals=0
        ),
        name="mlp",
    )(o_own, o_oth, x, w_proj, w_fc1, w_fc2, cot, wide, deep_shift)
    return outs


def ingest_kernel(order, a_ref, b_ref, o_ref):
    rows, width = a_ref.shape
    count = order.shape[0] - 1
    size = width // count
    first = order[count]
    for place in range(count):
        src = pl.ds(pl.multiple_of(order[place] * size, size), size)
        dst = slice(place * size, (place + 1) * size)

        @pl.when(first == 0)
        def _():
            o_ref[0:rows, dst] = a_ref[:, src]
            o_ref[rows : 2 * rows, dst] = b_ref[:, src]

        @pl.when(first != 0)
        def _():
            o_ref[0:rows, dst] = b_ref[:, src]
            o_ref[rows : 2 * rows, dst] = a_ref[:, src]

    o_ref[2 * rows :, :] = jnp.zeros((o_ref.shape[0] - 2 * rows, width), o_ref.dtype)


def ingest(order, first, a, b, padded):
    rows, width = a.shape
    count = order.shape[0]
    if width // count % 128:
        both = jnp.where(first == 0, jnp.concatenate([a, b]), jnp.concatenate([b, a]))
        both = jnp.take(both.reshape(2 * rows, count, -1), order, axis=1).reshape(2 * rows, width)
        return jnp.pad(both, ((0, padded - 2 * rows), (0, 0)))
    scalars = jnp.concatenate([order, first[None]]).astype(jnp.int32)
    return pl.pallas_call(
        ingest_kernel,
        grid_spec=pltpu.PrefetchScalarGridSpec(
            num_scalar_prefetch=1,
            grid=(1,),
            in_specs=[pl.BlockSpec((rows, width), lambda i, _: (0, 0))] * 2,
            out_specs=pl.BlockSpec((padded, width), lambda i, _: (0, 0)),
        ),
        out_shape=jax.ShapeDtypeStruct((padded, width), a.dtype),
        compiler_params=pltpu.CompilerParams(vmem_limit_bytes=20 * mib),
        name="ingest",
    )(scalars, a, b)


def egress_kernel(order, x_ref, a_ref, b_ref):
    rows, width = a_ref.shape
    count = order.shape[0] - 1
    size = width // count
    first = order[count]
    for place in range(count):
        dst = pl.ds(pl.multiple_of(order[place] * size, size), size)
        src = slice(place * size, (place + 1) * size)

        @pl.when(first == 0)
        def _():
            a_ref[:, dst] = x_ref[0:rows, src]
            b_ref[:, dst] = x_ref[rows : 2 * rows, src]

        @pl.when(first != 0)
        def _():
            b_ref[:, dst] = x_ref[0:rows, src]
            a_ref[:, dst] = x_ref[rows : 2 * rows, src]


def egress(order, inverse, first, x, rows):
    width = x.shape[1]
    count = order.shape[0]
    if width // count % 128:
        both = jnp.take(x.reshape(-1, count, width // count), inverse, axis=1).reshape(-1, width)
        top, low = both[:rows], both[rows : 2 * rows]
        return jnp.where(first == 0, top, low), jnp.where(first == 0, low, top)
    scalars = jnp.concatenate([order, first[None]]).astype(jnp.int32)
    return pl.pallas_call(
        egress_kernel,
        grid_spec=pltpu.PrefetchScalarGridSpec(
            num_scalar_prefetch=1,
            grid=(1,),
            in_specs=[pl.BlockSpec(x.shape, lambda i, _: (0, 0))],
            out_specs=[pl.BlockSpec((rows, width), lambda i, _: (0, 0))] * 2,
        ),
        out_shape=(jax.ShapeDtypeStruct((rows, width), x.dtype),) * 2,
        compiler_params=pltpu.CompilerParams(vmem_limit_bytes=20 * mib),
        name="egress",
    )(scalars, x)


def norm_parts(operand):
    centred = operand - jnp.mean(operand, axis=-1, keepdims=True)
    inverse = lax.rsqrt(jnp.mean(centred * centred, axis=-1, keepdims=True) + epsilon)
    return centred * inverse, inverse


def norm_back(scaled, normed, inverse):
    return inverse * (
        scaled
        - jnp.mean(scaled, axis=-1, keepdims=True)
        - normed * jnp.mean(scaled * normed, axis=-1, keepdims=True)
    )


def make_body(n_dp, n_t):
    bits = n_dp.bit_length() - 1
    reverse = [int(format(i, "b").zfill(bits)[::-1], 2) for i in range(n_dp)]
    axes = ("dp", "tensor")

    def at(dp, t):
        return dp * n_t + t

    go_a, go_b = [], []
    for dp in range(n_dp):
        c, base = dp % 2, dp - dp % 2
        for j in range(n_t):
            go_a.append((at(dp, j), at(base + j // 2, 2 * (j % 2) + c)))
            go_b.append((at(dp, j), at(base + j // 2, 2 * (1 - j % 2) + c)))
    back_a = [(d, s) for s, d in go_a]
    back_b = [(d, s) for s, d in go_b]
    ring = [(j, (j + 1) % n_t) for j in range(n_t)]

    def swap(value, bit):
        return lax.ppermute(value, "dp", [(i, i ^ (1 << bit)) for i in range(n_dp)])

    def step_z(value):
        return lax.ppermute(value, "tensor", ring)

    def body(
        tokens, segment_ids, pad_mask, cotangent, ln1_gain, ln1_bias, qkv_weight, qv_bias,
        proj_weight, proj_bias, ln2_gain, ln2_bias, fc1_weight, fc1_bias, fc2_weight, fc2_bias,
    ):
        me = lax.axis_index("dp")
        z = lax.axis_index("tensor")
        side = me % 2
        quarter, width = tokens.shape[2], tokens.shape[3]
        length = segment_ids.shape[2]
        half = -(-2 * quarter // block) * block
        size = width // n_dp
        micro = z // 2
        odd = z % 2
        order = jnp.stack([me ^ reverse[p] for p in range(n_dp)]).astype(jnp.int32)
        inverse = jnp.stack(
            [sum((((me ^ d) >> b) & 1) << (bits - 1 - b) for b in range(bits)) for d in range(n_dp)]
        ).astype(jnp.int32)

        def bring(array):
            a = lax.ppermute(lax.dynamic_index_in_dim(array[:, 0], odd, 0, False), axes, go_a)
            b = lax.ppermute(lax.dynamic_index_in_dim(array[:, 0], 1 - odd, 0, False), axes, go_b)
            return a, b

        def give(a, b):
            return lax.ppermute(a, axes, back_a), lax.ppermute(b, axes, back_b)

        lanes = max(128, size)

        def row_of(v):
            return jnp.pad(v.reshape(1, -1), ((0, 0), (0, lanes - v.size)))

        fields = [ln1_gain, ln1_bias, proj_bias, ln2_gain, ln2_bias, fc2_bias, fc1_bias, qv_bias]
        packed = jnp.concatenate([row_of(v) for v in fields] + [jnp.zeros((8, lanes), bf16)])
        rows_in, w_qkv, w_fc1, w_fc2, w_proj, small, *made = gather_all(
            tokens[:, 0],
            (qkv_weight.reshape(size, -1), fc1_weight, fc2_weight.T, proj_weight.T, packed),
            n_dp, n_t, (0, 3), half, qv_bias.shape[2] * n_dp, 2,
        )

        w_qkv, w_fc1, w_proj = [w.reshape(width, -1) for w in (w_qkv, w_fc1, w_proj)]
        heads_t, hd = qv_bias.shape[1], qv_bias.shape[2] * n_dp

        which = z % 2
        packed_ids = jnp.stack([segment_ids[:, 0], pad_mask[:, 0]])
        packed_oth = swap(packed_ids, 0)
        ids = jnp.where(which == side, packed_ids, packed_oth)
        ids = lax.dynamic_index_in_dim(ids, micro, 1, False)
        seg, live = ids[0], ids[1]
        gap = half - length // 2

        def stretch(v, fill):
            return jnp.pad(v.reshape(2, -1), ((0, 0), (0, gap)), constant_values=fill).reshape(-1)

        q_ids = stretch(seg, -1)
        k_ids = stretch(jnp.where(live == 1, seg, -2), -2)
        per_half = half // block
        first_pos = jnp.array([h * (length // 2) + b * block for h in range(2) for b in range(per_half)])
        last_pos = jnp.array(
            [min(h * (length // 2) + (b + 1) * block, (h + 1) * (length // 2)) - 1 for h in range(2) for b in range(per_half)]
        )
        lo = jnp.sum((seg[None, :] < seg[first_pos][:, None]).astype(jnp.int32), axis=1)
        hi = jnp.sum((seg[None, :] <= seg[last_pos][:, None]).astype(jnp.int32), axis=1) - 1
        place = lambda v: jnp.where(v >= length // 2, v + gap, v) // block
        info = jnp.concatenate([side[None], place(lo), place(hi) + 1]).astype(jnp.int32)

        if made:
            x_low, rows_one, own, oth, wide, deep_shift = made
            gain_one = wide[0]
            x = x_low.astype(f32)
            hat_one, inv_one = norm_parts(x)
        else:
            small = small.reshape(n_dp, packed.shape[0], n_t, lanes).astype(f32)
            gain_one, shift_one, proj_shift, gain_two, shift_two, fc2_shift = [
                small[:, i, 0, :size].reshape(-1) for i in range(6)
            ]
            ordered = jnp.take(small[:, 6:8], inverse, axis=0)
            fc1_shift = jnp.transpose(ordered[:, 0, :, :size], (1, 0, 2)).reshape(-1)
            w_fc2 = w_fc2.reshape(width, -1)
            x_low = ingest(order, jnp.int32(0), rows_in[0], rows_in[1], half)
            x = x_low.astype(f32)
            hat_one, inv_one = norm_parts(x)
            rows_one = (hat_one * gain_one + shift_one).astype(bf16)
            qv = ordered[:, 1, :, : qv_bias.size].reshape(n_dp, n_t, 2, heads_t, hd // n_dp)
            qv = jnp.transpose(qv, (1, 2, 3, 0, 4)).reshape(n_t, 2, heads_t * hd)
            shift = jnp.stack([qv[:, 0], jnp.zeros_like(qv[:, 0]), qv[:, 1]], axis=1).reshape(2, -1)
            shift = jnp.where(side == 0, shift, shift[::-1]).reshape(-1)
            near_cols = w_qkv.shape[1] // 2
            far = (dot_nn(rows_one, w_qkv[:, near_cols:]) + shift[near_cols:]).astype(bf16)
            oth = swap(far, 0)
            own = (dot_nn(rows_one, w_qkv[:, :near_cols]) + shift[:near_cols]).astype(bf16)
        if made:
            o_own, o_oth, lse = attend(info, own, oth, q_ids[None, :], k_ids[:, None])
            (
                heads, rows_two, act, g_pre, gy_low, g_hidden, g_attn, g_own, g_oth, y_a, y_b, _, _, sums, deep_sums,
            ) = mlp(
                o_own, o_oth, x_low, w_proj, w_fc1, w_fc2, cotangent[:, 0], wide, deep_shift, n_dp, n_t
            )
            proj_shift_grad, gain_two_grad, shift_two_grad, fc2_shift_grad = jnp.sum(sums, axis=1)
            fc1_shift_grad = jnp.sum(deep_sums, axis=0)
            parts = attend_back(
                info, own, oth, g_own, g_oth, o_own, o_oth, lse, q_ids[None, :], k_ids[:, None]
            )
            parts, (out_a, out_b) = lax.optimization_barrier((parts, give(y_a, y_b)))
            out = jnp.where(odd == 0, jnp.stack([out_a, out_b]), jnp.stack([out_b, out_a]))[:, None]
        else:
            own, oth, cot = lax.optimization_barrier((own, oth, cotangent))
            o_own, o_oth, lse = attend(info, own, oth, q_ids[None, :], k_ids[:, None])
            o_own, o_oth, lse, gy_a, gy_b = lax.optimization_barrier((o_own, o_oth, lse) + bring(cot))
            o_came = swap(o_oth, 0)
            heads = jnp.concatenate([o_own, o_came], axis=1)
            hidden = x + (dot_nt(heads, w_proj) + proj_shift)
            hat_two, inv_two = norm_parts(hidden)
            rows_two = (hat_two * gain_two + shift_two).astype(bf16)
            pre = dot_nn(rows_two, w_fc1) + fc1_shift
            cdf = 0.5 * (1.0 + lax.erf(pre * 0.7071067811865476))
            act = (pre * cdf).astype(bf16)
            slope = (cdf + pre * jnp.exp(-0.5 * pre * pre) * 0.3989422804014327).astype(bf16)
            y = hidden + (dot_nt(act, w_fc2) + fc2_shift)
            y_rows = egress(order, inverse, micro, y.astype(bf16), quarter)

            gy_low = ingest(order, micro, gy_a, gy_b, half)
            gy = gy_low.astype(f32)
            fc2_shift_grad = jnp.sum(gy, axis=0)
            g_pre = (dot_nn(gy_low, w_fc2) * slope.astype(f32)).astype(bf16)
            fc1_shift_grad = jnp.sum(g_pre, axis=0, dtype=f32)
            g_c = dot_nt(g_pre, w_fc1)
            gain_two_grad = jnp.sum(g_c * hat_two, axis=0)
            shift_two_grad = jnp.sum(g_c, axis=0)
            g_hidden = gy + norm_back(g_c * gain_two, hat_two, inv_two)
            g_attn = g_hidden.astype(bf16)
            proj_shift_grad = jnp.sum(g_attn, axis=0, dtype=f32)
            near_cols = w_proj.shape[1] // 2
            g_oth = swap(dot_nn(g_attn, w_proj[:, near_cols:]).astype(bf16), 0)
            g_own = dot_nn(g_attn, w_proj[:, :near_cols]).astype(bf16)
            own, y_rows = lax.optimization_barrier((own, y_rows))
            parts = attend_back(
                info, own, oth, g_own, g_oth, o_own, o_oth, lse, q_ids[None, :], k_ids[:, None]
            )
            parts, (out_a, out_b) = lax.optimization_barrier((parts, give(*y_rows)))
            out = jnp.where(odd == 0, jnp.stack([out_a, out_b]), jnp.stack([out_b, out_a]))[:, None]

        d_own, d_oth = parts
        d_qkv = jnp.concatenate([d_own, swap(d_oth, 0)], axis=1)
        qkv_sum = jnp.sum(d_qkv, axis=0, dtype=f32).reshape(2, n_t // 2, 3, -1)
        qkv_sum = jnp.where(side == 0, qkv_sum, qkv_sum[::-1]).reshape(n_t, 3, -1)
        g_a = dot_nt(d_qkv, w_qkv)
        gain_one_grad = jnp.sum(g_a * hat_one, axis=0)
        shift_one_grad = jnp.sum(g_a, axis=0)
        grad_rows = (g_hidden + norm_back(g_a * gain_one, hat_one, inv_one)).astype(bf16)
        grad_rows = jnp.stack(egress(order, inverse, jnp.int32(0), grad_rows, quarter))

        fields = [gain_one_grad, shift_one_grad, proj_shift_grad, gain_two_grad, shift_two_grad, fc2_shift_grad]
        wide_g = jnp.stack(fields).reshape(6, n_dp, 1, size)
        wide_g = jnp.transpose(jnp.broadcast_to(wide_g, (6, n_dp, n_t, size)), (1, 0, 2, 3))
        fc1_g = jnp.transpose(fc1_shift_grad.reshape(n_t, n_dp, 1, size), (1, 2, 0, 3))
        qv_g = jnp.stack([qkv_sum[:, 0], qkv_sum[:, 2]], axis=1).reshape(n_t, 2, heads_t, n_dp, -1)
        qv_g = jnp.transpose(qv_g, (3, 0, 1, 2, 4)).reshape(n_dp, 1, n_t, -1)
        pad = lambda v: jnp.pad(v, ((0, 0), (0, 0), (0, 0), (0, lanes - v.shape[-1])))
        hidden_g = jnp.take(jnp.concatenate([pad(fc1_g), pad(qv_g)], axis=1), order, axis=0)
        small_g = jnp.concatenate([pad(wide_g), hidden_g], axis=1)
        small_g = small_g.reshape((2,) * bits + (8, n_t * lanes))

        fc2_grad, fc1_grad, qkv_grad, proj_grad, small_sum, tokens_grad = reduce_all(
            (gy_low, rows_two, rows_one, g_attn), (act, g_pre, d_qkv, heads), small_g, grad_rows, n_dp, n_t, (2, 3)
        )
        wide_g = [small_sum[i, :size] for i in range(6)]
        fc1_g = small_sum[6:7, :size]
        qv_g = small_sum[7, : qv_bias.size].reshape(qv_bias.shape)
        return (
            out,
            tokens_grad[:, None],
            wide_g[0],
            wide_g[1],
            qkv_grad.reshape(qkv_weight.shape),
            qv_g,
            proj_grad.T,
            wide_g[2],
            wide_g[3],
            wide_g[4],
            fc1_grad,
            fc1_g,
            fc2_grad.T,
            wide_g[5],
        )

    return body


def solution(mesh):
    in_specs = (
        P(None, "dp", "tensor", None),
        P(None, "dp", None),
        P(None, "dp", None),
        P(None, "dp", "tensor", None),
        P("dp"),
        P("dp"),
        P("dp", None, "tensor"),
        P(None, "tensor", "dp"),
        P("tensor", "dp"),
        P("dp"),
        P("dp"),
        P("dp"),
        P("dp", "tensor"),
        P("tensor", "dp"),
        P("tensor", "dp"),
        P("dp"),
    )
    out_specs = (
        P(None, "dp", "tensor", None),
        P(None, "dp", "tensor", None),
        P("dp"),
        P("dp"),
        P("dp", None, "tensor"),
        P(None, "tensor", "dp"),
        P("tensor", "dp"),
        P("dp"),
        P("dp"),
        P("dp"),
        P("dp", "tensor"),
        P("tensor", "dp"),
        P("tensor", "dp"),
        P("dp"),
    )
    body = make_body(mesh.shape["dp"], mesh.shape["tensor"])
    return jax.shard_map(body, mesh=mesh, in_specs=in_specs, out_specs=out_specs, check_vma=False)
```

```python
import functools
import math

import jax
import jax.numpy as jnp
from jax import lax
from jax.experimental import pallas as pl
from jax.experimental.pallas import tpu as pltpu
from jax.sharding import PartitionSpec as P

bf16 = jnp.bfloat16
f32 = jnp.float32
epsilon = 1e-06
score_scale = 0.125
log2e = 1.4426950408889634
low_score = -1e30
block = 256
window = 384
stride = 128
mib = 1 << 20


def dot_nn(left, right):
    return lax.dot_general(left, right, (((1,), (0,)), ((), ())), preferred_element_type=f32)


def dot_nt(left, right):
    return lax.dot_general(left, right, (((1,), (1,)), ((), ())), preferred_element_type=f32)


def dot_tn(left, right):
    return lax.dot_general(left, right, (((0,), (0,)), ((), ())), preferred_element_type=f32)


def lane_halves(rows):
    lane = lax.broadcasted_iota(jnp.int32, rows.shape, 1)
    zero = jnp.zeros_like(rows)
    return jnp.where(lane < 64, rows, zero), jnp.where(lane < 64, zero, rows)


def attend_kernel(
    info, qo, ko, vo, qr, kr, vr, seg_row, seg_col, out_own, out_oth, lse_ref,
    qts, vts, os, *per_head,
):
    half, wide = qo.shape
    heads = wide // 64
    blocks = 2 * half // block
    side = info[0]
    own_at = pl.multiple_of(side * half, half)
    oth_at = pl.multiple_of((1 - side) * half, half)
    ks, ss = per_head[:heads], per_head[heads:]
    for at, q_in, k_in, v_in in ((own_at, qo, ko, vo), (oth_at, qr, kr, vr)):
        rows = pl.ds(at, half)
        for i in range(heads // 2):
            pair = k_in[:, i * 128 : (i + 1) * 128]
            ks[2 * i][rows, :], ks[2 * i + 1][rows, :] = lane_halves(pair)
        for b in range(half // block):
            cols = pl.ds(pl.multiple_of(at + b * block, block), block)
            vts[:, cols] = v_in[b * block : (b + 1) * block, :].T
            qts[:, cols] = q_in[b * block : (b + 1) * block, :].T

    for ref in ks:
        ref[2 * half :, :] = jnp.zeros((window, 128), bf16)
    vts[:, 2 * half :] = jnp.zeros((wide, window), bf16)
    diff = lax.broadcasted_iota(jnp.int32, (window, block), 1) - lax.broadcasted_iota(
        jnp.int32, (window, block), 0
    )
    factor = score_scale * log2e

    def per_rows(qb, carry):
        q_at = pl.multiple_of(qb * block, block)
        q_cols = pl.ds(q_at, block)
        q_seg = seg_row[0:1, q_cols]
        first, count = info[1 + qb], info[1 + blocks + qb]

        def scan(kb, tops):
            k_at = pl.multiple_of(first * stride + kb * window, stride)
            keys = pl.ds(k_at, window)
            mask = (q_seg == seg_col[keys, :]) | (diff == k_at - q_at)
            out = []
            for i in range(heads):
                q = qts[i // 2 * 128 : i // 2 * 128 + 128, q_cols]
                s = jnp.where(mask, dot_nn(ks[i][keys, :], q), low_score)
                ss[i][kb] = s
                out.append(jnp.maximum(tops[i], jnp.max(s.reshape(window // 8, 8, block), axis=0)))
            return tuple(out)

        start = jnp.full((8, block), low_score, f32)
        tops = lax.fori_loop(0, count, scan, (start,) * heads)
        tops = [jnp.max(top, axis=0, keepdims=True) * factor for top in tops]

        def mix(kb, state):
            keys = pl.ds(pl.multiple_of(first * stride + kb * window, stride), window)
            done = []
            for i in range(heads):
                p = jnp.exp2(ss[i][kb] * factor - tops[i])
                done.append(state[2 * i] + jnp.sum(p.reshape(window // 8, 8, block), axis=0))
                done.append(
                    state[2 * i + 1] + dot_nn(vts[i * 64 : (i + 1) * 64, keys], p.astype(bf16))
                )
            return tuple(done)

        zeros = (jnp.zeros((8, block), f32), jnp.zeros((64, block), f32))
        state = lax.fori_loop(0, count, mix, zeros * heads)
        mixed = []
        for i in range(heads):
            total = jnp.sum(state[2 * i], axis=0, keepdims=True)
            mixed.append(state[2 * i + 1] / total)
            lse_ref[0, i : i + 1, q_cols] = tops[i] + jnp.log2(total)
        os[q_cols, :] = jnp.concatenate(mixed, axis=0).T.astype(bf16)
        return carry

    lax.fori_loop(0, blocks, per_rows, 0)
    out_own[...] = os[pl.ds(own_at, half), :]
    out_oth[...] = os[pl.ds(oth_at, half), :]


def attend(info, own, oth, seg_row, seg_col):
    half = own.shape[0]
    rows = 2 * half
    groups = own.shape[1] // 768

    def part(which):
        return pl.BlockSpec((half, 256), lambda i, _: (0, i * 3 + which))

    whole = lambda shape: pl.BlockSpec(shape, lambda i, _: (0,) * len(shape))
    return pl.pallas_call(
        attend_kernel,
        grid_spec=pltpu.PrefetchScalarGridSpec(
            num_scalar_prefetch=1,
            grid=(groups,),
            in_specs=[part(0), part(1), part(2)] * 2 + [whole((1, rows)), whole((rows + window, 1))],
            out_specs=[
                pl.BlockSpec((half, 256), lambda i, _: (0, i)),
                pl.BlockSpec((half, 256), lambda i, _: (0, i)),
                pl.BlockSpec((1, 8, rows), lambda i, _: (i, 0, 0)),
            ],
            scratch_shapes=[pltpu.VMEM((256, rows), bf16), pltpu.VMEM((256, rows + window), bf16)]
            + [pltpu.VMEM((rows, 256), bf16)]
            + [pltpu.VMEM((rows + window, 128), bf16)] * 4
            + [pltpu.VMEM((-(-rows // window), window, block), f32)] * 4,
        ),
        out_shape=(
            jax.ShapeDtypeStruct((half, groups * 256), bf16),
            jax.ShapeDtypeStruct((half, groups * 256), bf16),
            jax.ShapeDtypeStruct((groups, 8, rows), f32),
        ),
        compiler_params=pltpu.CompilerParams(vmem_limit_bytes=60 * mib),
        cost_estimate=pl.CostEstimate(
            flops=int(groups * 4 * rows * rows * 256 * 1.5), bytes_accessed=int(own.size * 5), transcendentals=0
        ),
        name="attend",
    )(info, own, own, own, oth, oth, oth, seg_row, seg_col)


def attend_back_kernel(
    info, qo, ko, vo, qr, kr, vr, go, gr, oo, orr, lse_ref, seg_row, seg_col,
    d_own, d_oth, qts, gts, kts, os, dqs, dks, dvs, *per_head,
):
    half, wide = qo.shape
    heads = wide // 64
    blocks = 2 * half // block
    side = info[0]
    own_at = pl.multiple_of(side * half, half)
    oth_at = pl.multiple_of((1 - side) * half, half)
    ks, vs, qs, gs = [per_head[i * heads : (i + 1) * heads] for i in range(4)]
    for at, q_in, k_in, v_in, g_in, o_in in (
        (own_at, qo, ko, vo, go, oo),
        (oth_at, qr, kr, vr, gr, orr),
    ):
        rows = pl.ds(at, half)
        for refs, value in ((qs, q_in), (ks, k_in), (vs, v_in), (gs, g_in)):
            for i in range(heads // 2):
                pair = value[:, i * 128 : (i + 1) * 128]
                refs[2 * i][rows, :], refs[2 * i + 1][rows, :] = lane_halves(pair)
        for b in range(half // block):
            cols = pl.ds(pl.multiple_of(at + b * block, block), block)
            for ref, value in ((qts, q_in), (gts, g_in), (kts, k_in)):
                ref[:, cols] = value[b * block : (b + 1) * block, :].T
        os[rows, :] = o_in[...]
    dks[...] = jnp.zeros_like(dks)
    dvs[...] = jnp.zeros_like(dvs)

    for ref in ks + vs:
        ref[2 * half :, :] = jnp.zeros((window, 128), bf16)
    kts[:, 2 * half :] = jnp.zeros((wide, window), bf16)
    diff = lax.broadcasted_iota(jnp.int32, (window, block), 1) - lax.broadcasted_iota(
        jnp.int32, (window, block), 0
    )
    factor = score_scale * log2e

    def per_rows(qb, carry):
        q_at = pl.multiple_of(qb * block, block)
        rows = pl.ds(q_at, block)
        product = gts[:, rows].astype(f32) * os[rows, :].T.astype(f32)
        inner = [jnp.sum(product[i * 64 : (i + 1) * 64], axis=0, keepdims=True) for i in range(heads)]
        lses = [lse_ref[0, i : i + 1, rows] for i in range(heads)]
        q_seg = seg_row[0:1, rows]
        first, count = info[1 + qb], info[1 + blocks + qb]

        def per_keys(kb, dq):
            k_at = pl.multiple_of(first * stride + kb * window, stride)
            keys = pl.ds(k_at, window)
            mask = (q_seg == seg_col[keys, :]) | (diff == k_at - q_at)
            dq_out, dk, dv = [], [], []
            for i in range(heads):
                pair = slice(i // 2 * 128, i // 2 * 128 + 128)
                s = dot_nn(ks[i][keys, :], qts[pair, rows]) * factor - lses[i]
                p = jnp.exp2(jnp.where(mask, s, low_score))
                dv.append(dot_nn(p.astype(bf16), gs[i][rows, :]))
                dp = dot_nn(vs[i][keys, :], gts[pair, rows])
                ds = (p * (dp - inner[i])).astype(bf16)
                dk.append(dot_nn(ds, qs[i][rows, :]))
                dq_out.append(dq[i] + dot_nn(kts[i * 64 : (i + 1) * 64, keys], ds))
            for i in range(0, heads, 2):
                pair = slice(i // 2 * 128, i // 2 * 128 + 128)
                dks[keys, pair] += dk[i] + dk[i + 1]
                dvs[keys, pair] += dv[i] + dv[i + 1]
            return tuple(dq_out)

        dq = lax.fori_loop(
            0, count, per_keys, (jnp.zeros((64, block), f32),) * heads
        )
        dqs[rows, :] = (jnp.concatenate(dq, axis=0) * score_scale).T.astype(bf16)
        return carry

    lax.fori_loop(0, blocks, per_rows, 0)
    for at, out in ((own_at, d_own), (oth_at, d_oth)):
        rows = pl.ds(at, half)
        out[:, :wide] = dqs[rows, :]
        out[:, wide : 2 * wide] = (dks[rows, :] * score_scale).astype(bf16)
        out[:, 2 * wide :] = dvs[rows, :].astype(bf16)


def attend_back(info, own, oth, g_own, g_oth, o_own, o_oth, lse, seg_row, seg_col):
    half = own.shape[0]
    rows = 2 * half
    groups = own.shape[1] // 768

    def part(which):
        return pl.BlockSpec((half, 256), lambda i, _: (0, i * 3 + which))

    col = pl.BlockSpec((half, 256), lambda i, _: (0, i))
    whole = lambda shape: pl.BlockSpec(shape, lambda i, _: (0,) * len(shape))
    shape = jax.ShapeDtypeStruct(own.shape, bf16)
    return pl.pallas_call(
        attend_back_kernel,
        grid_spec=pltpu.PrefetchScalarGridSpec(
            num_scalar_prefetch=1,
            grid=(groups,),
            in_specs=[part(0), part(1), part(2)] * 2
            + [col] * 4
            + [pl.BlockSpec((1, 8, rows), lambda i, _: (i, 0, 0))]
            + [whole((1, rows)), whole((rows + window, 1))],
            out_specs=[pl.BlockSpec((half, 768), lambda i, _: (0, i))] * 2,
            scratch_shapes=[pltpu.VMEM((256, rows), bf16)] * 2
            + [pltpu.VMEM((256, rows + window), bf16)]
            + [pltpu.VMEM((rows, 256), bf16)] * 2
            + [pltpu.VMEM((rows + window, 256), f32)] * 2
            + [pltpu.VMEM((rows + window, 128), bf16)] * 8
            + [pltpu.VMEM((rows, 128), bf16)] * 8,
        ),
        out_shape=(shape,) * 2,
        compiler_params=pltpu.CompilerParams(vmem_limit_bytes=60 * mib),
        cost_estimate=pl.CostEstimate(
            flops=int(groups * 10 * rows * rows * 256), bytes_accessed=int(own.size * 10), transcendentals=0
        ),
        name="attend_back",
    )(info, own, own, own, oth, oth, oth, g_own, g_oth, o_own, o_oth, lse, seg_row, seg_col)


def plan_gather(loads, bits, n_t, rows_load, row_gate, fused, later):
    tasks = {}
    for w, load in enumerate(loads):
        for s in range(n_t):
            last = None
            if s:
                last = (w, s, "z")
                tasks[last] = (None if s == 1 else (w, s - 1, "z"), "z", load)
            middle = list(range(1, bits))
            for k, bit in enumerate((middle if (w + s) % 2 == 0 else middle[::-1]) + [0]):
                if not (fused and w == later and k > 0):
                    tasks[(w, s, k)] = (last, bit, load << k)
                last = (w, s, k)
    tasks[("rows", 0, 0)] = ((row_gate, n_t - 1, "z"), "z", rows_load)
    tasks[("rows", 1, 0)] = (("rows", 0, 0), "z", rows_load)
    free, done, waiting = {}, {}, list(tasks)
    while waiting:
        ready = [
            (0.0 if tasks[t][0] is None else done[tasks[t][0]], i, t)
            for i, t in enumerate(waiting)
            if tasks[t][0] is None or tasks[t][0] in done
        ]
        start, _, task = min((max(r, free.get(tasks[t][1], 0.0)), i, t) for r, i, t in ready)
        _, link, load = tasks[task]
        done[task] = start + load / (150e3 if link == 0 else 44e3) + 3.0
        free[link] = done[task] - 3.0
        waiting.remove(task)
    order = sorted(done, key=lambda t: done[t])
    parents = {t: tasks[t][0] for t in order}
    steps = list(order)
    if fused:
        heavy = max(steps.index((0, s, bits - 1)) for s in range(n_t))
        small = max(steps.index((len(loads) - 1, s, bits - 1)) for s in range(n_t))
        at = max(heavy, small, steps.index(("rows", 0, 0)))
        steps.insert(at + 1, ("work", 0, 0))
        at = max(at + 1, steps.index(("rows", 1, 0)))
        steps.insert(at + 1, ("work", 1, 0))
    return parents, steps


def gather_kernel(n_dp, n_t, count, parents, steps, paired, fused, *refs):
    refs = list(refs)
    take = lambda n: [refs.pop(0) for _ in range(n)]
    (rows_ref,), own = take(1), take(count)
    (rows_out,), outs = take(1), take(count)
    if fused:
        x_out, a_out, near_out, far_out, wide_out, deep_out = take(6)
    send, recv, near = take(3)
    arrivals = [t for t in steps if t[0] != "work"]
    bits = n_dp.bit_length() - 1
    me, z = lax.axis_index("dp"), lax.axis_index("tensor")
    side = lax.rem(me, 2)
    base = me - side
    micro = z // 2
    number = {task: i for i, task in enumerate(arrivals)}
    greet(n_t, bits, me, z)
    flips = [bit_flip(me, bit) for bit in range(bits)]

    def slot(w, s, index, flip=0):
        cols = own[w].shape[1]
        at = s * cols
        if w in paired:
            whose = side if not flip else 1 - side
            at = pl.multiple_of(((s // 2 + whose) % 2 * 2 + s % 2) * cols, cols)
        return outs[w].at[index + (slice(None), pl.ds(at, cols))]

    def copy_of(task):
        w, s, k = task
        i = number[task]
        if k == "z":
            src = own[w] if s == 1 else slot(w, s - 1, (0,) * bits)
            dst = slot(w, s, (0,) * bits)
            where = (me, lax.rem(z + 1, n_t))
        else:
            middle = list(range(1, bits))
            order = (middle if (w + s) % 2 == 0 else middle[::-1]) + [0]
            bit = order[k]
            src_at, dst_at = [], []
            for axis in range(bits):
                if axis == bit:
                    src_at.append(0)
                    dst_at.append(1)
                else:
                    held = slice(None) if axis in order[:k] else 0
                    src_at.append(held)
                    dst_at.append(held)
            src = own[w] if (k == 0 and s == 0) else slot(w, s, tuple(src_at))
            dst = slot(w, s, tuple(dst_at), flip=bit == 0)
            where = (flips[bit], z)
        return pltpu.make_async_remote_copy(
            src_ref=src, dst_ref=dst, send_sem=send.at[i], recv_sem=recv.at[i],
            device_id=where, device_id_type=pl.DeviceIdType.MESH,
        )

    placed = []
    for w in range(count):
        placed.append(pltpu.make_async_copy(own[w], slot(w, 0, (0,) * bits), near.at[w]))
        placed[-1].start()

    place = lax.rem(z, 2)
    target_core = base + z // 2

    def rows_copy(m):
        i = [number[("rows", q, 0)] for q in range(2)]
        where = (target_core, 2 * m + side)
        mine = (side == z // 2) & (z == 2 * m + side)
        return i, where, mine

    def start_rows(turn):
        i = number[("rows", turn, 0)]
        for m in range(2):
            _, where, mine = rows_copy(m)
            now = lax.rem(place + m, 2) == turn

            @pl.when(now & mine)
            def _():
                pltpu.make_async_copy(rows_ref.at[m], rows_out.at[place], recv.at[i]).start()

            @pl.when(now & jnp.logical_not(mine))
            def _():
                pltpu.make_async_remote_copy(
                    src_ref=rows_ref.at[m], dst_ref=rows_out.at[place], send_sem=near.at[count + m],
                    recv_sem=recv.at[i], device_id=where, device_id_type=pl.DeviceIdType.MESH,
                ).start()

    if fused:
        w_buf, x_rows, x_buf, a_buf, q_buf, s_buf, pick, shift, gains, deep_buf, f_sem, fsend, frecv = refs
        quarter, width = x_rows.shape
        half = x_buf.shape[0]
        size = width // n_dp
        deep = w_buf.shape[1]
        lanes = s_buf.shape[-1] // n_t
        hd8 = fused // n_dp
        x_buf[2 * quarter :, :] = jnp.zeros((half - 2 * quarter, width), bf16)
        a_buf[2 * quarter :, :] = jnp.zeros((half - 2 * quarter, width), bf16)
        q_buf[2 * quarter :, :] = jnp.zeros((half - 2 * quarter, deep), bf16)

    def block_of(p):
        digits = sum(((p >> (bits - 1 - b)) & 1) << b for b in range(bits))
        spot = me
        for b in range(bits):
            if (digits >> b) & 1:
                spot = bit_flip(spot, b)
        return spot

    def prepare():
        pltpu.make_async_copy(outs[0].reshape(width, deep), w_buf, f_sem.at[0]).start()
        copy = pltpu.make_async_copy(outs[count - 1], s_buf, f_sem.at[1])
        copy.start()
        copy.wait()
        cells = [tuple((p >> (bits - 1 - b)) & 1 for b in range(bits)) for p in range(n_dp)]
        small = [s_buf[c].astype(f32) for c in cells]
        for p in range(n_dp):
            gains[:, p * size : (p + 1) * size] = small[p][0:8, :size]
            for s in range(n_t):
                at = pl.multiple_of(s * width + block_of(p) * size, size)
                deep_buf[:, pl.ds(at, size)] = jnp.broadcast_to(
                    small[p][6:7, s * lanes : s * lanes + size], (8, size)
                )
        n = lax.broadcasted_iota(jnp.int32, (lanes, 8 * 64), 1)
        i = lax.broadcasted_iota(jnp.int32, (lanes, 8 * 64), 0)
        source = n // 256 * (4 * hd8) + n % 256 // 64 * hd8 + n % hd8
        for p in range(n_dp):
            hit = (i == source) & (n % 64 // hd8 == block_of(p))
            pick[p * lanes : (p + 1) * lanes, :] = hit.astype(bf16)
        for s in range(n_t):
            line = jnp.concatenate([v[7:8, s * lanes : (s + 1) * lanes] for v in small], axis=1)
            line = jnp.broadcast_to(line, (8, n_dp * lanes)).astype(bf16)
            got = dot_nn(line, pick[...])
            at = pl.multiple_of(((s // 2 + side) % 2 * 2 + s % 2) * 768, 256)
            shift[:, pl.ds(at, 256)] = got[:, :256]
            shift[:, pl.ds(pl.multiple_of(at + 256, 256), 256)] = jnp.zeros((8, 256), f32)
            shift[:, pl.ds(pl.multiple_of(at + 512, 256), 256)] = got[:, 256:]
        pltpu.make_async_copy(outs[0].reshape(width, deep), w_buf, f_sem.at[0]).wait()

    def far_copy(turn):
        rows = pl.ds(pl.multiple_of(lax.rem(micro + turn, 2) * quarter, 16), quarter)
        return pltpu.make_async_remote_copy(
            src_ref=q_buf.at[rows, pl.ds(deep // 2, deep // 2)], dst_ref=far_out.at[rows, :],
            send_sem=fsend.at[turn], recv_sem=frecv.at[turn],
            device_id=(flips[0], z), device_id_type=pl.DeviceIdType.MESH,
        )

    def finals():
        pads = pl.ds(2 * quarter, half - 2 * quarter)
        return [
            pltpu.make_async_copy(x_buf, x_out, f_sem.at[3]),
            pltpu.make_async_copy(a_buf, a_out, f_sem.at[4]),
            pltpu.make_async_copy(gains, wide_out, f_sem.at[7]),
            pltpu.make_async_copy(deep_buf, deep_out, f_sem.at[8]),
            pltpu.make_async_copy(q_buf.at[:, pl.ds(0, deep // 2)], near_out, f_sem.at[5]),
            pltpu.make_async_copy(
                q_buf.at[pads, pl.ds(0, deep // 2)], far_out.at[pads, :], f_sem.at[6]
            ),
        ]

    def work(turn):
        q = lax.rem(micro + turn, 2)
        at = pl.multiple_of(q * quarter, 16)
        copy = pltpu.make_async_copy(rows_out.at[q], x_rows, f_sem.at[2])
        copy.start()
        if turn == 0:
            prepare()
        copy.wait()
        spots = [pl.multiple_of(block_of(p) * size, size) for p in range(n_dp)]

        def norm_rows(first, tall):
            src = pl.ds(pl.multiple_of(first, 16), tall)
            dst = pl.ds(pl.multiple_of(at + first, 16), tall)
            for p in range(n_dp):
                x_buf[dst, p * size : (p + 1) * size] = x_rows[src, pl.ds(spots[p], size)]
            hat, _ = norm_parts(x_buf[dst, :].astype(f32))
            a_buf[dst, :] = (hat * gains[0:1, :] + gains[1:2, :]).astype(bf16)

        def norm_block(r, carry):
            norm_rows(r * 80, 80)
            return carry

        lax.fori_loop(0, quarter // 80, norm_block, 0)
        if quarter % 80:
            norm_rows(quarter // 80 * 80, quarter % 80)
        rows = pl.ds(at, quarter)

        def column_block(n, carry):
            cols = pl.ds(pl.multiple_of(n * 256, 256), 256)
            value = dot_nn(a_buf[rows, :], w_buf[:, cols]) + shift[0:1, cols]
            q_buf[rows, cols] = value.astype(bf16)
            return carry

        lax.fori_loop(deep // 512, deep // 256, column_block, 0)
        far_copy(turn).start()
        lax.fori_loop(0, deep // 512, column_block, 0)
        if turn == 1:
            for copy in finals():
                copy.start()

    copies = {task: copy_of(task) for task in arrivals if task[0] != "rows"}
    for task in arrivals:
        if task[0] != "rows" and parents[task] is None:
            copies[task].start()
    landed = {w: False for w in range(count)}
    for task in steps:
        if task[0] == "work":
            work(task[1])
            continue
        if task[0] == "rows":
            q = lax.rem(micro + task[1], 2)
            pltpu.make_async_copy(rows_ref.at[0], rows_out.at[q], recv.at[number[task]]).wait()
        else:
            copies[task].wait_recv()
        for child in arrivals:
            if parents[child] == task and child[0] == "rows":
                start_rows(child[1])
            elif parents[child] == task:
                if child[1] == 0 and not landed[child[0]]:
                    placed[child[0]].wait()
                    landed[child[0]] = True
                copies[child].start()
    for w in range(count):
        if not landed[w]:
            placed[w].wait()
    for task in arrivals:
        if task[0] != "rows":
            copies[task].wait_send()
    for m in range(2):
        i, where, mine = rows_copy(m)

        @pl.when(jnp.logical_not(mine))
        def _():
            pltpu.make_async_remote_copy(
                src_ref=rows_ref.at[m], dst_ref=rows_out.at[0], send_sem=near.at[count + m],
                recv_sem=recv.at[i[0]], device_id=where, device_id_type=pl.DeviceIdType.MESH,
            ).wait_send()
    if fused:
        for copy in finals():
            copy.wait()
        for turn in range(2):
            far_copy(turn).wait()

def bit_flip(me, bit):
    span = 1 << bit
    return me + span - 2 * span * lax.rem(me // span, 2)


def gather_all(rows, own, n_dp, n_t, paired, half, head_size, later):
    bits = n_dp.bit_length() - 1
    quarter, width = rows.shape[1:]
    size = width // n_dp
    fused = head_size if size % 128 == 0 else 0
    parents, steps = plan_gather(
        [w.shape[0] * w.shape[1] * 2 for w in own], bits, n_t, rows[0].size * 2, 2, fused, later
    )
    count = len(own)
    arrivals = [t for t in steps if t[0] != "work"]
    hbm = pl.BlockSpec(memory_space=pl.ANY)
    shapes = [jax.ShapeDtypeStruct(rows.shape, bf16)]
    shapes += [
        jax.ShapeDtypeStruct((2,) * bits + (w.shape[0], n_t * w.shape[1]), w.dtype) for w in own
    ]
    scratch = [
        pltpu.SemaphoreType.DMA((len(arrivals),)),
        pltpu.SemaphoreType.DMA((len(arrivals),)),
        pltpu.SemaphoreType.DMA((count + 2,)),
    ]
    if fused:
        deep = n_t * own[0].shape[1]
        shapes += [jax.ShapeDtypeStruct((half, c), bf16) for c in (width, width, deep // 2, deep // 2)]
        shapes += [jax.ShapeDtypeStruct((8, c), f32) for c in (width, n_t * width)]
        scratch += [
            pltpu.VMEM((width, deep), bf16),
            pltpu.VMEM((quarter, width), bf16),
            pltpu.VMEM((half, width), bf16),
            pltpu.VMEM((half, width), bf16),
            pltpu.VMEM((half, deep), bf16),
            pltpu.VMEM((2,) * bits + (own[-1].shape[0], n_t * own[-1].shape[1]), bf16),
            pltpu.VMEM((n_dp * own[-1].shape[1], 512), bf16),
            pltpu.VMEM((8, deep), f32),
            pltpu.VMEM((8, width), f32),
            pltpu.VMEM((8, n_t * width), f32),
            pltpu.SemaphoreType.DMA((9,)),
            pltpu.SemaphoreType.DMA((2,)),
            pltpu.SemaphoreType.DMA((2,)),
        ]
    return pl.pallas_call(
        functools.partial(gather_kernel, n_dp, n_t, count, parents, steps, paired, fused),
        in_specs=[hbm] * (1 + count),
        out_specs=[hbm] * len(shapes),
        out_shape=tuple(shapes),
        scratch_shapes=scratch,
        compiler_params=pltpu.CompilerParams(
            collective_id=0, has_side_effects=True, vmem_limit_bytes=60 * mib
        ),
        cost_estimate=pl.CostEstimate(flops=0, bytes_accessed=300 * mib, transcendentals=0),
        name="gather_all",
    )(rows, *own)


def stage_bits(w, s, bits):
    middle = list(range(1, bits))
    return [0] + (middle if (w + s) % 2 == 0 else middle[::-1])


def plan_reduce(widths, size, bits, n_t, rows_load):
    turn = list(range(1, n_t)) + [0]
    last = len(widths)
    chunks = [(last, s) for s in turn]
    for s in turn:
        group = list(range(last))
        chunks += [(w, s) for w in (group[-1:] + group[:-1] if s == turn[0] else group)]
    ready, free, core, order = {}, {"z": rows_load / 44e3}, 0.0, []
    pending = {("make", w, s): 0.0 for w, s in chunks}
    rank = {c: i for i, c in enumerate(chunks)}
    arrived = {}
    while pending:
        def key(item):
            kind, w, s = item[0][0], item[0][1], item[0][2]
            begin = max(core, item[1])
            return (begin, kind == "make", rank[(w, s)])

        action, when = min(pending.items(), key=key)
        del pending[action]
        order.append(action)
        w, s = action[1], action[2]
        cols = 64 if w == last else widths[w]
        rows = 16 if w == last else size << (bits - 1)
        share = rows * cols / (512 * 1024)
        begin = max(core, when)
        core = begin + (4.5 * share + 2.0 if action[0] == "make" else 1.2 * share / (1 << action[3] if action[0] == "add" else 4) + 0.3)
        flow = stage_bits(w, s, bits)
        k = 0 if action[0] == "make" else action[3] + 1 if action[0] == "add" else None

        def send(link, load):
            begin = max(core, free.get(link, 0.0))
            free[link] = begin + load / (150e3 if link == 0 else 44e3)
            return free[link] + 5.0

        def to_z():
            if s != 0:
                nxt = turn[turn.index(s) + 1]
                arrived[(w, nxt)] = send("z", (rows >> (bits - 1)) * cols * 2)
                if (w, nxt) in ready:
                    pending[("z", w, nxt)] = arrived[(w, nxt)]

        if k is not None and k < bits:
            load = (rows >> k) * cols * 2
            pending[("add", w, s, k)] = send(flow[k], load)
        elif k is not None:
            ready[(w, s)] = core
            if s == turn[0]:
                to_z()
            elif (w, s) in arrived:
                pending[("z", w, s)] = arrived[(w, s)]
        else:
            to_z()
    return order


def greet(n_t, bits, me, z):
    side = lax.rem(me, 2)
    barrier = pltpu.get_barrier_semaphore()
    for dz in range(n_t):
        for other in range(2):
            if dz or other:
                where = (me - side + lax.rem(side + other, 2), lax.rem(z + dz, n_t))
                pl.semaphore_signal(barrier, inc=1, device_id=where, device_id_type=pl.DeviceIdType.MESH)
    for bit in range(1, bits):
        where = (bit_flip(me, bit), z)
        pl.semaphore_signal(barrier, inc=1, device_id=where, device_id_type=pl.DeviceIdType.MESH)
    pl.semaphore_wait(barrier, 2 * n_t - 1 + bits - 1)


def reduce_kernel(n_dp, n_t, plan, widths, paired, *refs):
    bits = n_dp.bit_length() - 1
    count = len(widths)
    refs = list(refs)
    take = lambda n: [refs.pop(0) for _ in range(n)]
    xs, gs, (small_in, rows_in) = take(count), take(count), take(2)
    outs, (small_out, rows_out) = take(count), take(2)
    kept, came, zcame = take(count + 1), take(count + 1), take(count + 1)
    later = [take(bits - 1) for _ in range(count + 1)]
    (away, away_small, x_buf, x_turn, g_buf) = take(5)
    (x_sem, g_sem, s_sem, r_sem, send, recv, zsend, zrecv) = take(8)
    me, z = lax.axis_index("dp"), lax.axis_index("tensor")
    turn = list(range(1, n_t)) + [0]
    blk = kept[0].shape[-2]
    tall = blk << (bits - 1)
    greet(n_t, bits, me, z)

    side = lax.rem(me, 2)
    micro, owner = z // 2, lax.rem(z, 2)

    def rows_to(q):
        where = (me - side + owner, 2 * side + q)
        mine = (owner == side) & (2 * side + q == z)
        return where, mine

    def rows_from(m):
        return (side == z // 2) & (2 * m + side == z)

    for q in range(2):
        where, mine = rows_to(q)
        for m in range(2):

            @pl.when((micro == m) & mine)
            def _():
                pltpu.make_async_copy(rows_in.at[q], rows_out.at[m], r_sem.at[2 + m]).start()

            @pl.when((micro == m) & jnp.logical_not(mine))
            def _():
                pltpu.make_async_remote_copy(
                    src_ref=rows_in.at[q], dst_ref=rows_out.at[m], send_sem=r_sem.at[q],
                    recv_sem=r_sem.at[2 + m], device_id=where, device_id_type=pl.DeviceIdType.MESH,
                ).start()

    made = [a for a in plan if a[0] == "make" and a[1] < count]

    def fetch(i):
        _, w, s = made[i]
        c = widths[w]
        at = s * c
        if w in paired:
            at = pl.multiple_of(((s // 2 + side) % 2 * 2 + s % 2) * c, c)
        return pltpu.make_async_copy(
            gs[w].at[:, pl.ds(at, c)], g_buf.at[i % 2, :, pl.ds(0, c)], g_sem.at[i % 2]
        )

    def fetch_x(w):
        return pltpu.make_async_copy(xs[w], x_buf, x_sem)

    def at_stage(w, s, k, taken):
        flow = stage_bits(w, s, bits)
        return tuple(
            0 if bit in flow[:k] else (taken if bit == flow[k] else slice(None)) for bit in range(1, bits)
        )

    def landing(w, s, k):
        ref = came[w] if k == 0 else later[w][k - 1]
        return ref.at[s]

    def copy_of(w, s, k):
        flow = stage_bits(w, s, bits)
        if k == 0:
            src = away_small.at[s] if w == count else away_view(w, s)
        else:
            src = kept[w].at[(s,) + at_stage(w, s, k, 1)]
        return pltpu.make_async_remote_copy(
            src_ref=src, dst_ref=landing(w, s, k), send_sem=send.at[w, s, k], recv_sem=recv.at[w, s, k],
            device_id=(bit_flip(me, flow[k]), z), device_id_type=pl.DeviceIdType.MESH,
        )

    def away_view(w, s):
        i = made.index(("make", w, s)) % 2
        return away.at[(i,) + (slice(None),) * bits + (pl.ds(0, widths[w]),)]

    def zcopy(w, s):
        nxt = turn[turn.index(s) + 1]
        return pltpu.make_async_remote_copy(
            src_ref=kept[w].at[(s,) + (0,) * (bits - 1)], dst_ref=zcame[w].at[nxt],
            send_sem=zsend.at[w, s], recv_sem=zrecv.at[w, nxt],
            device_id=(me, lax.rem(z + 1, n_t)), device_id_type=pl.DeviceIdType.MESH,
        )

    def finish(w, s, total):
        ref = small_out if w == count else outs[w]
        ref[...] = total

    fetch(0).start()
    fetch_x(made[0][1]).start()
    for action in plan:
        kind, w, s = action[:3]
        if kind == "make" and w == count:
            lanes = small_out.shape[-1]
            cols = pl.ds(s * lanes, lanes)
            for half, dst in ((1, away_small.at[s]), (0, kept[w].at[s])):
                src = small_in.at[(half,) + (slice(None),) * bits + (cols,)]
                pltpu.make_async_copy(src, dst, s_sem.at[half]).start()
            for half, dst in ((1, away_small.at[s]), (0, kept[w].at[s])):
                src = small_in.at[(half,) + (slice(None),) * bits + (cols,)]
                pltpu.make_async_copy(src, dst, s_sem.at[half]).wait()
            copy_of(w, s, 0).start()
        elif kind == "make":
            i = made.index(action)
            c = widths[w]
            if i == 0 or made[i - 1][1] != w:
                fetch_x(w).wait()
                for a in range(x_buf.shape[1] // 256):

                    def turn_block(b, carry, a=a):
                        rows = pl.ds(pl.multiple_of(b * 256, 256), 256)
                        x_turn[a * 256 : (a + 1) * 256, rows] = x_buf[rows, a * 256 : (a + 1) * 256].T
                        return carry

                    lax.fori_loop(0, x_buf.shape[0] // 256, turn_block, 0)
                follow = [m[1] for m in made[i:] if m[1] != w]
                if follow:
                    fetch_x(follow[0]).start()
            fetch(i).wait()
            if i + 1 < len(made):
                fetch(i + 1).start()
            if i >= 2:
                copy_of(*made[i - 2][1:], 0).wait_send()
            whole = (slice(None),) * bits

            def away_block(n, carry):
                cols = pl.ds(pl.multiple_of(n * 256, 256), 256)
                value = dot_nn(x_turn[tall:, :], g_buf[i % 2, :, cols]).astype(bf16)
                away[(i % 2,) + whole + (cols,)] = value.reshape((2,) * (bits - 1) + (blk, 256))
                return carry

            lax.fori_loop(0, c // 256, away_block, 0)
            copy_of(w, s, 0).start()

            def kept_block(n, carry):
                cols = pl.ds(pl.multiple_of(n * 256, 256), 256)
                value = dot_nn(x_turn[:tall, :], g_buf[i % 2, :, cols]).astype(bf16)
                kept[w][(s,) + whole + (cols,)] = value.reshape((2,) * (bits - 1) + (blk, 256))
                return carry

            lax.fori_loop(0, c // 256, kept_block, 0)
        elif kind == "add":
            k = action[3]
            copy_of(w, s, k).wait_recv()
            place = (s,) + (slice(None),) * (bits - 1) if k == 0 else (s,) + at_stage(w, s, k, 0)
            got = (came[w] if k == 0 else later[w][k - 1])[s]
            held = kept[w][place]
            kept[w][place] = (held.astype(f32) + got.astype(f32)).astype(held.dtype)
            if k + 1 < bits:
                copy_of(w, s, k + 1).start()
            elif s == turn[0]:
                zcopy(w, s).start()
        else:
            before = turn[turn.index(s) - 1]
            zcopy(w, before).wait_recv()
            place = (s,) + (0,) * (bits - 1)
            total = kept[w][place].astype(f32) + zcame[w][s].astype(f32)
            if s == turn[-1]:
                finish(w, s, total)
            else:
                kept[w][place] = total.astype(kept[w].dtype)
                zcopy(w, s).start()
    for w in range(count + 1):
        for s in turn:
            for k in range(bits):
                if k == 0 and w < count and made.index(("make", w, s)) < len(made) - 2:
                    continue
                copy_of(w, s, k).wait_send()
            if s != turn[-1]:
                zcopy(w, s).wait_send()
    for q in range(2):
        where, mine = rows_to(q)

        @pl.when(jnp.logical_not(mine))
        def _():
            pltpu.make_async_remote_copy(
                src_ref=rows_in.at[q], dst_ref=rows_out.at[0], send_sem=r_sem.at[q],
                recv_sem=r_sem.at[2], device_id=where, device_id_type=pl.DeviceIdType.MESH,
            ).wait_send()
    for m in range(2):
        pltpu.make_async_copy(rows_in.at[0], rows_out.at[m], r_sem.at[2 + m]).wait()


def reduce_all(xs, gs, small, rows, n_dp, n_t, paired):
    bits = n_dp.bit_length() - 1
    count = len(xs)
    width = xs[0].shape[1]
    size = width // n_dp
    widths = [g.shape[1] // n_t for g in gs]
    lanes = small.shape[-1] // n_t
    plan = plan_reduce(widths, size, bits, n_t, rows[0].size * 2)
    cells = (2,) * (bits - 1)
    shapes = [(size, c, bf16) for c in widths] + [(small.shape[-2], lanes, f32)]
    hbm, vmem = pl.BlockSpec(memory_space=pl.ANY), pl.BlockSpec(memory_space=pltpu.VMEM)
    scratch = [pltpu.VMEM((n_t,) + cells + (r, c), t) for r, c, t in shapes]
    scratch += [pltpu.VMEM((n_t,) + cells + (r, c), t) for r, c, t in shapes]
    scratch += [pltpu.VMEM((n_t, r, c), t) for r, c, t in shapes]
    for r, c, t in shapes:
        scratch += [pltpu.VMEM((n_t,) + (2,) * (bits - 1 - k) + (r, c), t) for k in range(1, bits)]
    scratch += [
        pltpu.VMEM((2,) + cells + (size, max(widths)), bf16),
        pltpu.VMEM((n_t,) + cells + (small.shape[-2], lanes), f32),
        pltpu.VMEM(xs[0].shape, bf16),
        pltpu.VMEM((width, xs[0].shape[0]), bf16),
        pltpu.VMEM((2, gs[0].shape[0], max(widths)), bf16),
        pltpu.SemaphoreType.DMA,
        pltpu.SemaphoreType.DMA((2,)),
        pltpu.SemaphoreType.DMA((2,)),
        pltpu.SemaphoreType.DMA((4,)),
        pltpu.SemaphoreType.DMA((count + 1, n_t, bits)),
        pltpu.SemaphoreType.DMA((count + 1, n_t, bits)),
        pltpu.SemaphoreType.DMA((count + 1, n_t)),
        pltpu.SemaphoreType.DMA((count + 1, n_t)),
    ]
    return pl.pallas_call(
        functools.partial(reduce_kernel, n_dp, n_t, plan, widths, paired),
        in_specs=[hbm] * (2 * count + 2),
        out_specs=[vmem] * (count + 1) + [hbm],
        out_shape=tuple(jax.ShapeDtypeStruct((size, c), f32) for c in widths)
        + (
            jax.ShapeDtypeStruct((small.shape[-2], lanes), f32),
            jax.ShapeDtypeStruct(rows.shape, rows.dtype),
        ),
        scratch_shapes=scratch,
        compiler_params=pltpu.CompilerParams(
            collective_id=1, has_side_effects=True, vmem_limit_bytes=60 * mib
        ),
        cost_estimate=pl.CostEstimate(
            flops=2 * xs[0].size * n_t * sum(widths), bytes_accessed=200 * mib, transcendentals=0
        ),
        name="reduce_all",
    )(*xs, *gs, small, rows)


def gelu_parts(v):
    bell = jnp.exp2(v * v * (-0.5 * log2e))
    t = 1.0 / (1.0 + jnp.abs(v) * (0.3275911 * 0.7071067811865476))
    poly = t * (
        0.254829592 * 0.5
        + t * (-0.284496736 * 0.5 + t * (1.421413741 * 0.5 + t * (-1.453152027 * 0.5 + t * (1.061405429 * 0.5))))
    )
    tail = poly * bell
    cdf = jnp.where(v < 0.0, tail, 1.0 - tail)
    return v * cdf, cdf + v * bell * 0.3989422804014327


def mlp_kernel(
    n_dp, n_t, o_own, o_oth, x_in, w_proj, w_fc1, w_fc2_in, cot, wide, deep_shift,
    heads_out, c_out, act_out, gpre_out, gy_out, gh_out, gattn_out, g_own, g_oth, y_a, y_b, gy_mid, w_fc2_parts,
    sums, deep_sums,
    heads, x_buf, h_buf, c_buf, act, slope, o_buf, gy, gc, wp, col_buf, row_buf, stage,
    col_sem, row_sem, load_sem, save_sem, out_sem, cot_send, cot_recv, swap_send, swap_recv,
    rest_send, rest_recv,
):
    bits = n_dp.bit_length() - 1
    me, z = lax.axis_index("dp"), lax.axis_index("tensor")
    side = lax.rem(me, 2)
    base = me - side
    micro, place = z // 2, lax.rem(z, 2)
    half, width = x_buf.shape
    quarter = stage.shape[0]
    size = width // n_dp
    deep = act.shape[1]
    mesh_id = pl.DeviceIdType.MESH
    partner = (bit_flip(me, 0), z)
    greet(n_t, bits, me, z)
    w_fc2 = w_fc2_parts.reshape(width, deep)

    def far_heads():
        return pltpu.make_async_remote_copy(
            src_ref=o_oth, dst_ref=heads.at[:, pl.ds(width // 2, width // 2)],
            send_sem=swap_send.at[0], recv_sem=swap_recv.at[0], device_id=partner, device_id_type=mesh_id,
        )

    far_heads().start()
    loads = [
        pltpu.make_async_copy(o_own, heads.at[:, pl.ds(0, width // 2)], load_sem.at[0]),
        pltpu.make_async_copy(x_in, x_buf, load_sem.at[1]),
        pltpu.make_async_copy(w_proj, wp, load_sem.at[2]),
    ]
    for copy in loads:
        copy.start()

    def rest(s, k):
        flow = stage_bits(2, s, bits)
        flow = flow[1:] + flow[:1]
        cols = pl.ds(s * width, width)
        src_at = tuple(0 if b == flow[k] or b not in flow[:k] else slice(None) for b in range(bits))
        dst_at = tuple(1 if b == flow[k] else a for b, a in enumerate(src_at))
        return pltpu.make_async_remote_copy(
            src_ref=w_fc2_parts.at[src_at + (slice(None), cols)],
            dst_ref=w_fc2_parts.at[dst_at + (slice(None), cols)],
            send_sem=rest_send.at[s, k], recv_sem=rest_recv.at[s, k],
            device_id=(bit_flip(me, flow[k]), z), device_id_type=mesh_id,
        )

    for s in range(n_t):
        rest(s, 1).start()

    def cot_copy(turn):
        m = lax.rem(place + turn, 2)
        where, mine = (base + z // 2, 2 * m + side), (side == z // 2) & (z == 2 * m + side)
        here = pltpu.make_async_copy(cot.at[m], gy_mid.at[turn], cot_recv.at[turn])
        there = pltpu.make_async_remote_copy(
            src_ref=cot.at[m], dst_ref=gy_mid.at[turn], send_sem=cot_send.at[turn],
            recv_sem=cot_recv.at[turn], device_id=where, device_id_type=mesh_id,
        )
        return here, there, mine

    for turn in range(2):
        here, there, mine = cot_copy(turn)

        @pl.when(mine)
        def _():
            here.start()

        @pl.when(jnp.logical_not(mine))
        def _():
            there.start()

    def cols_of(ref, n):
        slot = lax.rem(n, 2)
        return pltpu.make_async_copy(
            ref.at[:, pl.ds(pl.multiple_of(n * 1024, 1024), 1024)], col_buf.at[slot], col_sem.at[slot]
        )

    def rows_of(ref, n):
        slot = lax.rem(n, 2)
        return pltpu.make_async_copy(
            ref.at[pl.ds(pl.multiple_of(n * 256, 256), 256), :], row_buf.at[slot], row_sem.at[slot]
        )

    def stream(ref, fetch, count, use):
        def one(n, carry):
            fetch(ref, n).wait()

            @pl.when(n + 1 < count)
            def _():
                fetch(ref, n + 1).start()

            use(n, lax.rem(n, 2))
            return carry

        lax.fori_loop(0, count, one, 0)

    cols_of(w_fc1, 0).start()
    for copy in loads:
        copy.wait()
    far_heads().wait_recv()
    pltpu.make_async_copy(heads, heads_out, save_sem.at[0]).start()

    chunk = half // 1

    def by_rows(body):
        def one(r, carry):
            body(pl.ds(pl.multiple_of(r * chunk, chunk), chunk))
            return carry

        lax.fori_loop(0, half // chunk, one, 0)

    def proj_block(n, carry):
        cols = pl.ds(pl.multiple_of(n * 256, 256), 256)

        def body(rows):
            value = dot_nt(heads[rows, :], wp[cols, :]) + wide[2:3, cols]
            h_buf[rows, cols] = x_buf[rows, cols].astype(f32) + value

        by_rows(body)
        return carry

    lax.fori_loop(0, width // 256, proj_block, 0)

    def norm_block(r, carry):
        rows = pl.ds(pl.multiple_of(r * 128, 128), 128)
        hat, _ = norm_parts(h_buf[rows, :])
        c_buf[rows, :] = (hat * wide[3:4, :] + wide[4:5, :]).astype(bf16)
        return carry

    lax.fori_loop(0, half // 128, norm_block, 0)
    pltpu.make_async_copy(c_buf, c_out, save_sem.at[1]).start()

    def fc1_block(n, slot):
        cols = pl.ds(pl.multiple_of(n * 1024, 1024), 1024)

        def body(rows):
            value, grade = gelu_parts(dot_nn(c_buf[rows, :], col_buf[slot]) + deep_shift[0:1, cols])
            act[rows, cols] = value.astype(bf16)
            slope[rows, cols] = grade.astype(bf16)

        by_rows(body)

    pieces = deep // 1024
    sent = 0
    for n in range(pieces):
        cols_of(w_fc1, n).wait()
        if n + 1 < pieces:
            cols_of(w_fc1, n + 1).start()
        fc1_block(n, n % 2)
        ready = {1: n_t // 2, pieces - 1: n_t}.get(n, sent)
        for s in range(sent, ready):
            for k in range(2, bits):
                rest(s, k - 1).wait_recv()
                rest(s, k).start()
        sent = ready
    for s in range(n_t):
        rest(s, bits - 1).wait_recv()
    rows_of(w_fc2, 0).start()
    cols_of(w_fc2, 0).start()
    pltpu.make_async_copy(act, act_out, save_sem.at[2]).start()

    def spot(p):
        digits = sum(((p >> (bits - 1 - b)) & 1) << b for b in range(bits))
        at = me
        for b in range(bits):
            if (digits >> b) & 1:
                at = bit_flip(at, b)
        return pl.ds(pl.multiple_of(at * size, size), size)

    def fc2_block(n, slot):
        cols = pl.ds(pl.multiple_of(n * 256, 256), 256)

        def body(rows):
            value = dot_nt(act[rows, :], row_buf[slot]) + wide[5:6, cols]
            o_buf[rows, cols] = (h_buf[rows, cols] + value).astype(bf16)

        by_rows(body)

    stream(w_fc2, rows_of, width // 256, fc2_block)
    rows_of(w_fc1, 0).start()

    def unorder(r, carry):
        rows = pl.ds(pl.multiple_of(r * 16, 16), 16)
        line = o_buf[rows, :]
        for p in range(n_dp):
            x_buf[rows, spot(p)] = line[:, p * size : (p + 1) * size]
        return carry

    lax.fori_loop(0, half // 16, unorder, 0)

    for q in range(2):
        src = x_buf.at[pl.ds(q * quarter, quarter), :]
        for first in range(2):

            @pl.when(micro == first)
            def _():
                pltpu.make_async_copy(src, (y_a, y_b)[(q + first) % 2], out_sem.at[q]).start()

    gy[2 * quarter :, :] = jnp.zeros((half - 2 * quarter, width), bf16)
    for turn in range(2):
        cot_copy(turn)[0].wait()
        at = lax.rem(micro + turn, 2) * quarter
        copy = pltpu.make_async_copy(gy_mid.at[turn], stage, load_sem.at[0])
        copy.start()
        copy.wait()

        def reorder(r, carry):
            src = pl.ds(pl.multiple_of(r * 16, 16), 16)
            dst = pl.ds(pl.multiple_of(at + r * 16, 16), 16)
            for p in range(n_dp):
                gy[dst, p * size : (p + 1) * size] = stage[src, spot(p)]
            return carry

        lax.fori_loop(0, quarter // 16, reorder, 0)
    pltpu.make_async_copy(gy, gy_out, save_sem.at[3]).start()

    def gpre_block(n, slot):
        cols = pl.ds(pl.multiple_of(n * 1024, 1024), 1024)
        deep_sums[:, cols] = jnp.zeros((8, 1024), f32)

        def body(rows):
            value = dot_nn(gy[rows, :], col_buf[slot]) * slope[rows, cols].astype(f32)
            low = value.astype(bf16)
            slope[rows, cols] = low
            deep_sums[:, cols] += jnp.sum(low.astype(f32).reshape(chunk // 8, 8, 1024), axis=0)

        by_rows(body)

    stream(w_fc2, cols_of, deep // 1024, gpre_block)
    pltpu.make_async_copy(slope, gpre_out, save_sem.at[4]).start()

    def gc_block(n, slot):
        cols = pl.ds(pl.multiple_of(n * 256, 256), 256)

        def body(rows):
            gc[rows, cols] = dot_nt(slope[rows, :], row_buf[slot])

        by_rows(body)

    stream(w_fc1, rows_of, width // 256, gc_block)

    sums[...] = jnp.zeros_like(sums)

    def back_block(r, carry):
        rows = pl.ds(pl.multiple_of(r * 128, 128), 128)
        hat, inverse = norm_parts(h_buf[rows, :])
        g_c = gc[rows, :]
        g_y = gy[rows, :].astype(f32)
        g_h = g_y + norm_back(g_c * wide[3:4, :], hat, inverse)
        low = g_h.astype(bf16)
        gc[rows, :] = g_h
        o_buf[rows, :] = low
        for i, value in enumerate((low.astype(f32), g_c * hat, g_c, g_y)):
            sums[i] += jnp.sum(value.reshape(16, 8, width), axis=0)
        return carry

    lax.fori_loop(0, half // 128, back_block, 0)
    pltpu.make_async_copy(gc, gh_out, save_sem.at[5]).start()
    pltpu.make_async_copy(o_buf, gattn_out, save_sem.at[6]).start()

    pltpu.make_async_copy(heads, heads_out, save_sem.at[0]).wait()

    def gheads_block(n, carry):
        cols = pl.ds(pl.multiple_of(n * 256, 256), 256)

        def body(rows):
            heads[rows, cols] = dot_nn(o_buf[rows, :], wp[:, cols]).astype(bf16)

        by_rows(body)
        return carry

    lax.fori_loop(width // 512, width // 256, gheads_block, 0)
    far = pltpu.make_async_remote_copy(
        src_ref=heads.at[:, pl.ds(width // 2, width // 2)], dst_ref=g_oth,
        send_sem=swap_send.at[1], recv_sem=swap_recv.at[1], device_id=partner, device_id_type=mesh_id,
    )
    far.start()
    lax.fori_loop(0, width // 512, gheads_block, 0)
    near = pltpu.make_async_copy(heads.at[:, pl.ds(0, width // 2)], g_own, load_sem.at[1])
    near.start()

    pltpu.make_async_copy(c_buf, c_out, save_sem.at[1]).wait()
    pltpu.make_async_copy(act, act_out, save_sem.at[2]).wait()
    pltpu.make_async_copy(gy, gy_out, save_sem.at[3]).wait()
    pltpu.make_async_copy(slope, gpre_out, save_sem.at[4]).wait()
    pltpu.make_async_copy(gc, gh_out, save_sem.at[5]).wait()
    pltpu.make_async_copy(o_buf, gattn_out, save_sem.at[6]).wait()
    near.wait()
    far.wait()
    far_heads().wait_send()
    for turn in range(2):
        here, there, mine = cot_copy(turn)

        @pl.when(jnp.logical_not(mine))
        def _():
            there.wait_send()

    for s in range(n_t):
        for k in range(1, bits):
            rest(s, k).wait_send()
    for q in range(2):
        pltpu.make_async_copy(x_buf.at[pl.ds(q * quarter, quarter), :], y_a, out_sem.at[q]).wait()


def mlp(o_own, o_oth, x, w_proj, w_fc1, w_fc2, cot, wide, deep_shift, n_dp, n_t):
    half, width = x.shape
    deep = w_fc1.shape[1]
    quarter = cot.shape[1]
    hbm, vmem = pl.BlockSpec(memory_space=pl.ANY), pl.BlockSpec(memory_space=pltpu.VMEM)
    shape = jax.ShapeDtypeStruct
    row, tall = shape((half, width), bf16), shape((half, deep), bf16)
    dma = pltpu.SemaphoreType.DMA
    outs = pl.pallas_call(
        functools.partial(mlp_kernel, n_dp, n_t),
        in_specs=[hbm] * 7 + [vmem] * 2,
        out_specs=[hbm] * 13 + [vmem] * 2,
        input_output_aliases={5: 12},
        out_shape=(
            row, row, tall, tall, row, shape((half, width), f32), row,
            shape(o_own.shape, bf16), shape(o_own.shape, bf16), shape(cot.shape[1:], bf16),
            shape(cot.shape[1:], bf16), shape(cot.shape, bf16), shape(w_fc2.shape, bf16),
            shape((4, 8, width), f32), shape((8, deep), f32),
        ),
        scratch_shapes=[
            pltpu.VMEM((half, width), bf16),
            pltpu.VMEM((half, width), bf16),
            pltpu.VMEM((half, width), f32),
            pltpu.VMEM((half, width), bf16),
            pltpu.VMEM((half, deep), bf16),
            pltpu.VMEM((half, deep), bf16),
            pltpu.VMEM((half, width), bf16),
            pltpu.VMEM((half, width), bf16),
            pltpu.VMEM((half, width), f32),
            pltpu.VMEM((width, width), bf16),
            pltpu.VMEM((2, width, 1024), bf16),
            pltpu.VMEM((2, 256, deep), bf16),
            pltpu.VMEM((quarter, width), bf16),
            dma((2,)), dma((2,)), dma((3,)), dma((7,)), dma((2,)), dma((2,)), dma((2,)), dma((2,)),
            dma((2,)), dma((n_t, n_dp.bit_length() - 1)), dma((n_t, n_dp.bit_length() - 1)),
        ],
        compiler_params=pltpu.CompilerParams(
            collective_id=2, has_side_effects=True, vmem_limit_bytes=60 * mib
        ),
        cost_estimate=pl.CostEstimate(
            flops=2 * half * width * (4 * deep + 2 * width), bytes_accessed=90 * mib, transcendentals=0
        ),
        name="mlp",
    )(o_own, o_oth, x, w_proj, w_fc1, w_fc2, cot, wide, deep_shift)
    return outs


def ingest_kernel(order, a_ref, b_ref, o_ref):
    rows, width = a_ref.shape
    count = order.shape[0] - 1
    size = width // count
    first = order[count]
    for place in range(count):
        src = pl.ds(pl.multiple_of(order[place] * size, size), size)
        dst = slice(place * size, (place + 1) * size)

        @pl.when(first == 0)
        def _():
            o_ref[0:rows, dst] = a_ref[:, src]
            o_ref[rows : 2 * rows, dst] = b_ref[:, src]

        @pl.when(first != 0)
        def _():
            o_ref[0:rows, dst] = b_ref[:, src]
            o_ref[rows : 2 * rows, dst] = a_ref[:, src]

    o_ref[2 * rows :, :] = jnp.zeros((o_ref.shape[0] - 2 * rows, width), o_ref.dtype)


def ingest(order, first, a, b, padded):
    rows, width = a.shape
    count = order.shape[0]
    if width // count % 128:
        both = jnp.where(first == 0, jnp.concatenate([a, b]), jnp.concatenate([b, a]))
        both = jnp.take(both.reshape(2 * rows, count, -1), order, axis=1).reshape(2 * rows, width)
        return jnp.pad(both, ((0, padded - 2 * rows), (0, 0)))
    scalars = jnp.concatenate([order, first[None]]).astype(jnp.int32)
    return pl.pallas_call(
        ingest_kernel,
        grid_spec=pltpu.PrefetchScalarGridSpec(
            num_scalar_prefetch=1,
            grid=(1,),
            in_specs=[pl.BlockSpec((rows, width), lambda i, _: (0, 0))] * 2,
            out_specs=pl.BlockSpec((padded, width), lambda i, _: (0, 0)),
        ),
        out_shape=jax.ShapeDtypeStruct((padded, width), a.dtype),
        compiler_params=pltpu.CompilerParams(vmem_limit_bytes=20 * mib),
        name="ingest",
    )(scalars, a, b)


def egress_kernel(order, x_ref, a_ref, b_ref):
    rows, width = a_ref.shape
    count = order.shape[0] - 1
    size = width // count
    first = order[count]
    for place in range(count):
        dst = pl.ds(pl.multiple_of(order[place] * size, size), size)
        src = slice(place * size, (place + 1) * size)

        @pl.when(first == 0)
        def _():
            a_ref[:, dst] = x_ref[0:rows, src]
            b_ref[:, dst] = x_ref[rows : 2 * rows, src]

        @pl.when(first != 0)
        def _():
            b_ref[:, dst] = x_ref[0:rows, src]
            a_ref[:, dst] = x_ref[rows : 2 * rows, src]


def egress(order, inverse, first, x, rows):
    width = x.shape[1]
    count = order.shape[0]
    if width // count % 128:
        both = jnp.take(x.reshape(-1, count, width // count), inverse, axis=1).reshape(-1, width)
        top, low = both[:rows], both[rows : 2 * rows]
        return jnp.where(first == 0, top, low), jnp.where(first == 0, low, top)
    scalars = jnp.concatenate([order, first[None]]).astype(jnp.int32)
    return pl.pallas_call(
        egress_kernel,
        grid_spec=pltpu.PrefetchScalarGridSpec(
            num_scalar_prefetch=1,
            grid=(1,),
            in_specs=[pl.BlockSpec(x.shape, lambda i, _: (0, 0))],
            out_specs=[pl.BlockSpec((rows, width), lambda i, _: (0, 0))] * 2,
        ),
        out_shape=(jax.ShapeDtypeStruct((rows, width), x.dtype),) * 2,
        compiler_params=pltpu.CompilerParams(vmem_limit_bytes=20 * mib),
        name="egress",
    )(scalars, x)


def norm_parts(operand):
    centred = operand - jnp.mean(operand, axis=-1, keepdims=True)
    inverse = lax.rsqrt(jnp.mean(centred * centred, axis=-1, keepdims=True) + epsilon)
    return centred * inverse, inverse


def norm_back(scaled, normed, inverse):
    return inverse * (
        scaled
        - jnp.mean(scaled, axis=-1, keepdims=True)
        - normed * jnp.mean(scaled * normed, axis=-1, keepdims=True)
    )


def make_body(n_dp, n_t):
    bits = n_dp.bit_length() - 1
    reverse = [int(format(i, "b").zfill(bits)[::-1], 2) for i in range(n_dp)]
    axes = ("dp", "tensor")

    def at(dp, t):
        return dp * n_t + t

    go_a, go_b = [], []
    for dp in range(n_dp):
        c, base = dp % 2, dp - dp % 2
        for j in range(n_t):
            go_a.append((at(dp, j), at(base + j // 2, 2 * (j % 2) + c)))
            go_b.append((at(dp, j), at(base + j // 2, 2 * (1 - j % 2) + c)))
    back_a = [(d, s) for s, d in go_a]
    back_b = [(d, s) for s, d in go_b]
    ring = [(j, (j + 1) % n_t) for j in range(n_t)]

    def swap(value, bit):
        return lax.ppermute(value, "dp", [(i, i ^ (1 << bit)) for i in range(n_dp)])

    def step_z(value):
        return lax.ppermute(value, "tensor", ring)

    def body(
        tokens, segment_ids, pad_mask, cotangent, ln1_gain, ln1_bias, qkv_weight, qv_bias,
        proj_weight, proj_bias, ln2_gain, ln2_bias, fc1_weight, fc1_bias, fc2_weight, fc2_bias,
    ):
        me = lax.axis_index("dp")
        z = lax.axis_index("tensor")
        side = me % 2
        quarter, width = tokens.shape[2], tokens.shape[3]
        length = segment_ids.shape[2]
        half = -(-2 * quarter // block) * block
        size = width // n_dp
        micro = z // 2
        odd = z % 2
        order = jnp.stack([me ^ reverse[p] for p in range(n_dp)]).astype(jnp.int32)
        inverse = jnp.stack(
            [sum((((me ^ d) >> b) & 1) << (bits - 1 - b) for b in range(bits)) for d in range(n_dp)]
        ).astype(jnp.int32)

        def bring(array):
            a = lax.ppermute(lax.dynamic_index_in_dim(array[:, 0], odd, 0, False), axes, go_a)
            b = lax.ppermute(lax.dynamic_index_in_dim(array[:, 0], 1 - odd, 0, False), axes, go_b)
            return a, b

        def give(a, b):
            return lax.ppermute(a, axes, back_a), lax.ppermute(b, axes, back_b)

        lanes = max(128, size)

        def row_of(v):
            return jnp.pad(v.reshape(1, -1), ((0, 0), (0, lanes - v.size)))

        fields = [ln1_gain, ln1_bias, proj_bias, ln2_gain, ln2_bias, fc2_bias, fc1_bias, qv_bias]
        packed = jnp.concatenate([row_of(v) for v in fields] + [jnp.zeros((8, lanes), bf16)])
        rows_in, w_qkv, w_fc1, w_fc2, w_proj, small, *made = gather_all(
            tokens[:, 0],
            (qkv_weight.reshape(size, -1), fc1_weight, fc2_weight.T, proj_weight.T, packed),
            n_dp, n_t, (0, 3), half, qv_bias.shape[2] * n_dp, 2,
        )

        w_qkv, w_fc1, w_proj = [w.reshape(width, -1) for w in (w_qkv, w_fc1, w_proj)]
        heads_t, hd = qv_bias.shape[1], qv_bias.shape[2] * n_dp

        which = z % 2
        packed_ids = jnp.stack([segment_ids[:, 0], pad_mask[:, 0]])
        packed_oth = swap(packed_ids, 0)
        ids = jnp.where(which == side, packed_ids, packed_oth)
        ids = lax.dynamic_index_in_dim(ids, micro, 1, False)
        seg, live = ids[0], ids[1]
        gap = half - length // 2

        def stretch(v, fill):
            return jnp.pad(v.reshape(2, -1), ((0, 0), (0, gap)), constant_values=fill).reshape(-1)

        q_ids = stretch(seg, -1)
        k_ids = stretch(jnp.where(live == 1, seg, -2), -2)
        per_half = half // block
        first_pos = jnp.array([h * (length // 2) + b * block for h in range(2) for b in range(per_half)])
        last_pos = jnp.array(
            [min(h * (length // 2) + (b + 1) * block, (h + 1) * (length // 2)) - 1 for h in range(2) for b in range(per_half)]
        )
        lo = jnp.sum((seg[None, :] < seg[first_pos][:, None]).astype(jnp.int32), axis=1)
        hi = jnp.sum((seg[None, :] <= seg[last_pos][:, None]).astype(jnp.int32), axis=1) - 1
        place = lambda v: jnp.where(v >= length // 2, v + gap, v)
        start = place(lo) // stride
        count = (place(hi) - start * stride) // window + 1
        info = jnp.concatenate([side[None], start, count]).astype(jnp.int32)
        k_ids = jnp.pad(k_ids, (0, window), constant_values=-2)

        if made:
            x_low, rows_one, own, oth, wide, deep_shift = made
            gain_one = wide[0]
            x = x_low.astype(f32)
            hat_one, inv_one = norm_parts(x)
        else:
            small = small.reshape(n_dp, packed.shape[0], n_t, lanes).astype(f32)
            gain_one, shift_one, proj_shift, gain_two, shift_two, fc2_shift = [
                small[:, i, 0, :size].reshape(-1) for i in range(6)
            ]
            ordered = jnp.take(small[:, 6:8], inverse, axis=0)
            fc1_shift = jnp.transpose(ordered[:, 0, :, :size], (1, 0, 2)).reshape(-1)
            w_fc2 = w_fc2.reshape(width, -1)
            x_low = ingest(order, jnp.int32(0), rows_in[0], rows_in[1], half)
            x = x_low.astype(f32)
            hat_one, inv_one = norm_parts(x)
            rows_one = (hat_one * gain_one + shift_one).astype(bf16)
            qv = ordered[:, 1, :, : qv_bias.size].reshape(n_dp, n_t, 2, heads_t, hd // n_dp)
            qv = jnp.transpose(qv, (1, 2, 3, 0, 4)).reshape(n_t, 2, heads_t * hd)
            shift = jnp.stack([qv[:, 0], jnp.zeros_like(qv[:, 0]), qv[:, 1]], axis=1).reshape(2, -1)
            shift = jnp.where(side == 0, shift, shift[::-1]).reshape(-1)
            near_cols = w_qkv.shape[1] // 2
            far = (dot_nn(rows_one, w_qkv[:, near_cols:]) + shift[near_cols:]).astype(bf16)
            oth = swap(far, 0)
            own = (dot_nn(rows_one, w_qkv[:, :near_cols]) + shift[:near_cols]).astype(bf16)
        if made:
            o_own, o_oth, lse = attend(info, own, oth, q_ids[None, :], k_ids[:, None])
            (
                heads, rows_two, act, g_pre, gy_low, g_hidden, g_attn, g_own, g_oth, y_a, y_b, _, _, sums, deep_sums,
            ) = mlp(
                o_own, o_oth, x_low, w_proj, w_fc1, w_fc2, cotangent[:, 0], wide, deep_shift, n_dp, n_t
            )
            proj_shift_grad, gain_two_grad, shift_two_grad, fc2_shift_grad = jnp.sum(sums, axis=1)
            fc1_shift_grad = jnp.sum(deep_sums, axis=0)
            parts = attend_back(
                info, own, oth, g_own, g_oth, o_own, o_oth, lse, q_ids[None, :], k_ids[:, None]
            )
            parts, (out_a, out_b) = lax.optimization_barrier((parts, give(y_a, y_b)))
            out = jnp.where(odd == 0, jnp.stack([out_a, out_b]), jnp.stack([out_b, out_a]))[:, None]
        else:
            own, oth, cot = lax.optimization_barrier((own, oth, cotangent))
            o_own, o_oth, lse = attend(info, own, oth, q_ids[None, :], k_ids[:, None])
            o_own, o_oth, lse, gy_a, gy_b = lax.optimization_barrier((o_own, o_oth, lse) + bring(cot))
            o_came = swap(o_oth, 0)
            heads = jnp.concatenate([o_own, o_came], axis=1)
            hidden = x + (dot_nt(heads, w_proj) + proj_shift)
            hat_two, inv_two = norm_parts(hidden)
            rows_two = (hat_two * gain_two + shift_two).astype(bf16)
            pre = dot_nn(rows_two, w_fc1) + fc1_shift
            cdf = 0.5 * (1.0 + lax.erf(pre * 0.7071067811865476))
            act = (pre * cdf).astype(bf16)
            slope = (cdf + pre * jnp.exp(-0.5 * pre * pre) * 0.3989422804014327).astype(bf16)
            y = hidden + (dot_nt(act, w_fc2) + fc2_shift)
            y_rows = egress(order, inverse, micro, y.astype(bf16), quarter)

            gy_low = ingest(order, micro, gy_a, gy_b, half)
            gy = gy_low.astype(f32)
            fc2_shift_grad = jnp.sum(gy, axis=0)
            g_pre = (dot_nn(gy_low, w_fc2) * slope.astype(f32)).astype(bf16)
            fc1_shift_grad = jnp.sum(g_pre, axis=0, dtype=f32)
            g_c = dot_nt(g_pre, w_fc1)
            gain_two_grad = jnp.sum(g_c * hat_two, axis=0)
            shift_two_grad = jnp.sum(g_c, axis=0)
            g_hidden = gy + norm_back(g_c * gain_two, hat_two, inv_two)
            g_attn = g_hidden.astype(bf16)
            proj_shift_grad = jnp.sum(g_attn, axis=0, dtype=f32)
            near_cols = w_proj.shape[1] // 2
            g_oth = swap(dot_nn(g_attn, w_proj[:, near_cols:]).astype(bf16), 0)
            g_own = dot_nn(g_attn, w_proj[:, :near_cols]).astype(bf16)
            own, y_rows = lax.optimization_barrier((own, y_rows))
            parts = attend_back(
                info, own, oth, g_own, g_oth, o_own, o_oth, lse, q_ids[None, :], k_ids[:, None]
            )
            parts, (out_a, out_b) = lax.optimization_barrier((parts, give(*y_rows)))
            out = jnp.where(odd == 0, jnp.stack([out_a, out_b]), jnp.stack([out_b, out_a]))[:, None]

        d_own, d_oth = parts
        d_qkv = jnp.concatenate([d_own, swap(d_oth, 0)], axis=1)
        qkv_sum = jnp.sum(d_qkv, axis=0, dtype=f32).reshape(2, n_t // 2, 3, -1)
        qkv_sum = jnp.where(side == 0, qkv_sum, qkv_sum[::-1]).reshape(n_t, 3, -1)
        g_a = dot_nt(d_qkv, w_qkv)
        gain_one_grad = jnp.sum(g_a * hat_one, axis=0)
        shift_one_grad = jnp.sum(g_a, axis=0)
        grad_rows = (g_hidden + norm_back(g_a * gain_one, hat_one, inv_one)).astype(bf16)
        grad_rows = jnp.stack(egress(order, inverse, jnp.int32(0), grad_rows, quarter))

        fields = [gain_one_grad, shift_one_grad, proj_shift_grad, gain_two_grad, shift_two_grad, fc2_shift_grad]
        wide_g = jnp.stack(fields).reshape(6, n_dp, 1, size)
        wide_g = jnp.transpose(jnp.broadcast_to(wide_g, (6, n_dp, n_t, size)), (1, 0, 2, 3))
        fc1_g = jnp.transpose(fc1_shift_grad.reshape(n_t, n_dp, 1, size), (1, 2, 0, 3))
        qv_g = jnp.stack([qkv_sum[:, 0], qkv_sum[:, 2]], axis=1).reshape(n_t, 2, heads_t, n_dp, -1)
        qv_g = jnp.transpose(qv_g, (3, 0, 1, 2, 4)).reshape(n_dp, 1, n_t, -1)
        pad = lambda v: jnp.pad(v, ((0, 0), (0, 0), (0, 0), (0, lanes - v.shape[-1])))
        hidden_g = jnp.take(jnp.concatenate([pad(fc1_g), pad(qv_g)], axis=1), order, axis=0)
        small_g = jnp.concatenate([pad(wide_g), hidden_g], axis=1)
        small_g = small_g.reshape((2,) * bits + (8, n_t * lanes))

        fc2_grad, fc1_grad, qkv_grad, proj_grad, small_sum, tokens_grad = reduce_all(
            (gy_low, rows_two, rows_one, g_attn), (act, g_pre, d_qkv, heads), small_g, grad_rows, n_dp, n_t, (2, 3)
        )
        wide_g = [small_sum[i, :size] for i in range(6)]
        fc1_g = small_sum[6:7, :size]
        qv_g = small_sum[7, : qv_bias.size].reshape(qv_bias.shape)
        return (
            out,
            tokens_grad[:, None],
            wide_g[0],
            wide_g[1],
            qkv_grad.reshape(qkv_weight.shape),
            qv_g,
            proj_grad.T,
            wide_g[2],
            wide_g[3],
            wide_g[4],
            fc1_grad,
            fc1_g,
            fc2_grad.T,
            wide_g[5],
        )

    return body


def solution(mesh):
    in_specs = (
        P(None, "dp", "tensor", None),
        P(None, "dp", None),
        P(None, "dp", None),
        P(None, "dp", "tensor", None),
        P("dp"),
        P("dp"),
        P("dp", None, "tensor"),
        P(None, "tensor", "dp"),
        P("tensor", "dp"),
        P("dp"),
        P("dp"),
        P("dp"),
        P("dp", "tensor"),
        P("tensor", "dp"),
        P("tensor", "dp"),
        P("dp"),
    )
    out_specs = (
        P(None, "dp", "tensor", None),
        P(None, "dp", "tensor", None),
        P("dp"),
        P("dp"),
        P("dp", None, "tensor"),
        P(None, "tensor", "dp"),
        P("tensor", "dp"),
        P("dp"),
        P("dp"),
        P("dp"),
        P("dp", "tensor"),
        P("tensor", "dp"),
        P("tensor", "dp"),
        P("dp"),
    )
    body = make_body(mesh.shape["dp"], mesh.shape["tensor"])
    return jax.shard_map(body, mesh=mesh, in_specs=in_specs, out_specs=out_specs, check_vma=False)
```

```python
import functools
import math

import jax
import jax.numpy as jnp
from jax import lax
from jax.experimental import pallas as pl
from jax.experimental.pallas import tpu as pltpu
from jax.sharding import PartitionSpec as P

bf16 = jnp.bfloat16
f32 = jnp.float32
epsilon = 1e-06
score_scale = 0.125
log2e = 1.4426950408889634
low_score = -1e30
block = 256
window = 384
stride = 128
mib = 1 << 20


def dot_nn(left, right):
    return lax.dot_general(left, right, (((1,), (0,)), ((), ())), preferred_element_type=f32)


def dot_nt(left, right):
    return lax.dot_general(left, right, (((1,), (1,)), ((), ())), preferred_element_type=f32)


def dot_tn(left, right):
    return lax.dot_general(left, right, (((0,), (0,)), ((), ())), preferred_element_type=f32)


def lane_halves(rows):
    lane = lax.broadcasted_iota(jnp.int32, rows.shape, 1)
    zero = jnp.zeros_like(rows)
    return jnp.where(lane < 64, rows, zero), jnp.where(lane < 64, zero, rows)


def attend_kernel(
    info, qo, ko, vo, qr, kr, vr, seg_row, seg_col, out_own, out_oth, lse_ref,
    qts, vts, os, *per_head,
):
    half, wide = qo.shape
    heads = wide // 64
    blocks = 2 * half // block
    side = info[0]
    own_at = pl.multiple_of(side * half, half)
    oth_at = pl.multiple_of((1 - side) * half, half)
    ks, ss = per_head[:heads], per_head[heads:]
    for at, q_in, k_in, v_in in ((own_at, qo, ko, vo), (oth_at, qr, kr, vr)):
        rows = pl.ds(at, half)
        for i in range(heads // 2):
            pair = k_in[:, i * 128 : (i + 1) * 128]
            ks[2 * i][rows, :], ks[2 * i + 1][rows, :] = lane_halves(pair)
        for b in range(half // block):
            cols = pl.ds(pl.multiple_of(at + b * block, block), block)
            vts[:, cols] = v_in[b * block : (b + 1) * block, :].T
            qts[:, cols] = q_in[b * block : (b + 1) * block, :].T

    for ref in ks:
        ref[2 * half :, :] = jnp.zeros((window, 128), bf16)
    vts[:, 2 * half :] = jnp.zeros((wide, window), bf16)
    diff = lax.broadcasted_iota(jnp.int32, (window, block), 1) - lax.broadcasted_iota(
        jnp.int32, (window, block), 0
    )
    factor = score_scale * log2e

    def per_rows(qb, carry):
        q_at = pl.multiple_of(qb * block, block)
        q_cols = pl.ds(q_at, block)
        q_seg = seg_row[0:1, q_cols]
        first, count = info[1 + qb], info[1 + blocks + qb]

        def scan(kb, tops):
            k_at = pl.multiple_of(first * stride + kb * window, stride)
            keys = pl.ds(k_at, window)
            mask = (q_seg == seg_col[keys, :]) | (diff == k_at - q_at)
            out = []
            for i in range(heads):
                q = qts[i // 2 * 128 : i // 2 * 128 + 128, q_cols]
                s = jnp.where(mask, dot_nn(ks[i][keys, :], q), low_score)
                ss[i][kb] = s
                out.append(jnp.maximum(tops[i], jnp.max(s.reshape(window // 8, 8, block), axis=0)))
            return tuple(out)

        start = jnp.full((8, block), low_score, f32)
        tops = lax.fori_loop(0, count, scan, (start,) * heads)
        tops = [jnp.max(top, axis=0, keepdims=True) * factor for top in tops]

        def mix(kb, state):
            keys = pl.ds(pl.multiple_of(first * stride + kb * window, stride), window)
            done = []
            for i in range(heads):
                p = jnp.exp2(ss[i][kb] * factor - tops[i])
                done.append(state[2 * i] + jnp.sum(p.reshape(window // 8, 8, block), axis=0))
                done.append(
                    state[2 * i + 1] + dot_nn(vts[i * 64 : (i + 1) * 64, keys], p.astype(bf16))
                )
            return tuple(done)

        zeros = (jnp.zeros((8, block), f32), jnp.zeros((64, block), f32))
        state = lax.fori_loop(0, count, mix, zeros * heads)
        mixed = []
        for i in range(heads):
            total = jnp.sum(state[2 * i], axis=0, keepdims=True)
            mixed.append(state[2 * i + 1] / total)
            lse_ref[0, i : i + 1, q_cols] = tops[i] + jnp.log2(total)
        os[q_cols, :] = jnp.concatenate(mixed, axis=0).T.astype(bf16)
        return carry

    lax.fori_loop(0, blocks, per_rows, 0)
    out_own[...] = os[pl.ds(own_at, half), :]
    out_oth[...] = os[pl.ds(oth_at, half), :]


def attend(info, own, oth, seg_row, seg_col):
    half = own.shape[0]
    rows = 2 * half
    groups = own.shape[1] // 768

    def part(which):
        return pl.BlockSpec((half, 256), lambda i, _: (0, i * 3 + which))

    whole = lambda shape: pl.BlockSpec(shape, lambda i, _: (0,) * len(shape))
    return pl.pallas_call(
        attend_kernel,
        grid_spec=pltpu.PrefetchScalarGridSpec(
            num_scalar_prefetch=1,
            grid=(groups,),
            in_specs=[part(0), part(1), part(2)] * 2 + [whole((1, rows)), whole((rows + window, 1))],
            out_specs=[
                pl.BlockSpec((half, 256), lambda i, _: (0, i)),
                pl.BlockSpec((half, 256), lambda i, _: (0, i)),
                pl.BlockSpec((1, 8, rows), lambda i, _: (i, 0, 0)),
            ],
            scratch_shapes=[pltpu.VMEM((256, rows), bf16), pltpu.VMEM((256, rows + window), bf16)]
            + [pltpu.VMEM((rows, 256), bf16)]
            + [pltpu.VMEM((rows + window, 128), bf16)] * 4
            + [pltpu.VMEM((-(-rows // window), window, block), f32)] * 4,
        ),
        out_shape=(
            jax.ShapeDtypeStruct((half, groups * 256), bf16),
            jax.ShapeDtypeStruct((half, groups * 256), bf16),
            jax.ShapeDtypeStruct((groups, 8, rows), f32),
        ),
        compiler_params=pltpu.CompilerParams(vmem_limit_bytes=60 * mib),
        cost_estimate=pl.CostEstimate(
            flops=int(groups * 4 * rows * rows * 256 * 1.5), bytes_accessed=int(own.size * 5), transcendentals=0
        ),
        name="attend",
    )(info, own, own, own, oth, oth, oth, seg_row, seg_col)


def attend_back_kernel(
    info, qo, ko, vo, qr, kr, vr, go, gr, oo, orr, lse_ref, seg_row, seg_col,
    d_own, d_oth, qts, gts, kts, os, dqs, dks, dvs, *per_head,
):
    half, wide = qo.shape
    heads = wide // 64
    blocks = 2 * half // block
    side = info[0]
    own_at = pl.multiple_of(side * half, half)
    oth_at = pl.multiple_of((1 - side) * half, half)
    ks, vs, qs, gs = [per_head[i * heads : (i + 1) * heads] for i in range(4)]
    for at, q_in, k_in, v_in, g_in, o_in in (
        (own_at, qo, ko, vo, go, oo),
        (oth_at, qr, kr, vr, gr, orr),
    ):
        rows = pl.ds(at, half)
        for refs, value in ((qs, q_in), (ks, k_in), (vs, v_in), (gs, g_in)):
            for i in range(heads // 2):
                pair = value[:, i * 128 : (i + 1) * 128]
                refs[2 * i][rows, :], refs[2 * i + 1][rows, :] = lane_halves(pair)
        for b in range(half // block):
            cols = pl.ds(pl.multiple_of(at + b * block, block), block)
            for ref, value in ((qts, q_in), (gts, g_in), (kts, k_in)):
                ref[:, cols] = value[b * block : (b + 1) * block, :].T
        os[rows, :] = o_in[...]
    dks[...] = jnp.zeros_like(dks)
    dvs[...] = jnp.zeros_like(dvs)

    for ref in ks + vs:
        ref[2 * half :, :] = jnp.zeros((window, 128), bf16)
    kts[:, 2 * half :] = jnp.zeros((wide, window), bf16)
    diff = lax.broadcasted_iota(jnp.int32, (window, block), 1) - lax.broadcasted_iota(
        jnp.int32, (window, block), 0
    )
    factor = score_scale * log2e

    def per_rows(qb, carry):
        q_at = pl.multiple_of(qb * block, block)
        rows = pl.ds(q_at, block)
        product = gts[:, rows].astype(f32) * os[rows, :].T.astype(f32)
        inner = [jnp.sum(product[i * 64 : (i + 1) * 64], axis=0, keepdims=True) for i in range(heads)]
        lses = [lse_ref[0, i : i + 1, rows] for i in range(heads)]
        q_seg = seg_row[0:1, rows]
        first, count = info[1 + qb], info[1 + blocks + qb]

        def per_keys(kb, dq):
            k_at = pl.multiple_of(first * stride + kb * window, stride)
            keys = pl.ds(k_at, window)
            mask = (q_seg == seg_col[keys, :]) | (diff == k_at - q_at)
            dq_out, dk, dv = [], [], []
            for i in range(heads):
                pair = slice(i // 2 * 128, i // 2 * 128 + 128)
                s = dot_nn(ks[i][keys, :], qts[pair, rows]) * factor - lses[i]
                p = jnp.exp2(jnp.where(mask, s, low_score))
                dv.append(dot_nn(p.astype(bf16), gs[i][rows, :]))
                dp = dot_nn(vs[i][keys, :], gts[pair, rows])
                ds = (p * (dp - inner[i])).astype(bf16)
                dk.append(dot_nn(ds, qs[i][rows, :]))
                dq_out.append(dq[i] + dot_nn(kts[i * 64 : (i + 1) * 64, keys], ds))
            for i in range(0, heads, 2):
                pair = slice(i // 2 * 128, i // 2 * 128 + 128)
                dks[keys, pair] += dk[i] + dk[i + 1]
                dvs[keys, pair] += dv[i] + dv[i + 1]
            return tuple(dq_out)

        dq = lax.fori_loop(
            0, count, per_keys, (jnp.zeros((64, block), f32),) * heads
        )
        dqs[rows, :] = (jnp.concatenate(dq, axis=0) * score_scale).T.astype(bf16)
        return carry

    lax.fori_loop(0, blocks, per_rows, 0)
    for at, out in ((own_at, d_own), (oth_at, d_oth)):
        rows = pl.ds(at, half)
        out[:, :wide] = dqs[rows, :]
        out[:, wide : 2 * wide] = (dks[rows, :] * score_scale).astype(bf16)
        out[:, 2 * wide :] = dvs[rows, :].astype(bf16)


def attend_back(info, own, oth, g_own, g_oth, o_own, o_oth, lse, seg_row, seg_col):
    half = own.shape[0]
    rows = 2 * half
    groups = own.shape[1] // 768

    def part(which):
        return pl.BlockSpec((half, 256), lambda i, _: (0, i * 3 + which))

    col = pl.BlockSpec((half, 256), lambda i, _: (0, i))
    whole = lambda shape: pl.BlockSpec(shape, lambda i, _: (0,) * len(shape))
    shape = jax.ShapeDtypeStruct(own.shape, bf16)
    return pl.pallas_call(
        attend_back_kernel,
        grid_spec=pltpu.PrefetchScalarGridSpec(
            num_scalar_prefetch=1,
            grid=(groups,),
            in_specs=[part(0), part(1), part(2)] * 2
            + [col] * 4
            + [pl.BlockSpec((1, 8, rows), lambda i, _: (i, 0, 0))]
            + [whole((1, rows)), whole((rows + window, 1))],
            out_specs=[pl.BlockSpec((half, 768), lambda i, _: (0, i))] * 2,
            scratch_shapes=[pltpu.VMEM((256, rows), bf16)] * 2
            + [pltpu.VMEM((256, rows + window), bf16)]
            + [pltpu.VMEM((rows, 256), bf16)] * 2
            + [pltpu.VMEM((rows + window, 256), f32)] * 2
            + [pltpu.VMEM((rows + window, 128), bf16)] * 8
            + [pltpu.VMEM((rows, 128), bf16)] * 8,
        ),
        out_shape=(shape,) * 2,
        compiler_params=pltpu.CompilerParams(vmem_limit_bytes=60 * mib),
        cost_estimate=pl.CostEstimate(
            flops=int(groups * 10 * rows * rows * 256), bytes_accessed=int(own.size * 10), transcendentals=0
        ),
        name="attend_back",
    )(info, own, own, own, oth, oth, oth, g_own, g_oth, o_own, o_oth, lse, seg_row, seg_col)


def plan_gather(loads, bits, n_t, rows_load, row_gate, fused, later):
    tasks = {}
    for w, load in enumerate(loads):
        for s in range(n_t):
            last = None
            if s:
                last = (w, s, "z")
                tasks[last] = (None if s == 1 else (w, s - 1, "z"), "z", load)
            middle = list(range(1, bits))
            for k, bit in enumerate((middle if (w + s) % 2 == 0 else middle[::-1]) + [0]):
                if not (fused and w == later and k > 0):
                    tasks[(w, s, k)] = (last, bit, load << k)
                last = (w, s, k)
    tasks[("rows", 0, 0)] = ((row_gate, n_t - 1, "z"), "z", rows_load)
    tasks[("rows", 1, 0)] = (("rows", 0, 0), "z", rows_load)
    free, done, waiting = {}, {}, list(tasks)
    while waiting:
        ready = [
            (0.0 if tasks[t][0] is None else done[tasks[t][0]], i, t)
            for i, t in enumerate(waiting)
            if tasks[t][0] is None or tasks[t][0] in done
        ]
        start, _, task = min((max(r, free.get(tasks[t][1], 0.0)), i, t) for r, i, t in ready)
        _, link, load = tasks[task]
        done[task] = start + load / (150e3 if link == 0 else 44e3) + 3.0
        free[link] = done[task] - 3.0
        waiting.remove(task)
    order = sorted(done, key=lambda t: done[t])
    parents = {t: tasks[t][0] for t in order}
    steps = list(order)
    if fused:
        heavy = max(steps.index((0, s, bits - 1)) for s in range(n_t))
        small = max(steps.index((len(loads) - 1, s, bits - 1)) for s in range(n_t))
        at = max(heavy, small, steps.index(("rows", 0, 0)))
        steps.insert(at + 1, ("work", 0, 0))
        at = max(at + 1, steps.index(("rows", 1, 0)))
        steps.insert(at + 1, ("work", 1, 0))
    return parents, steps


def gather_kernel(n_dp, n_t, count, parents, steps, paired, fused, *refs):
    refs = list(refs)
    take = lambda n: [refs.pop(0) for _ in range(n)]
    (rows_ref,), own = take(1), take(count)
    (rows_out,), outs = take(1), take(count)
    if fused:
        x_out, a_out, near_out, far_out, wide_out, deep_out = take(6)
    send, recv, near = take(3)
    arrivals = [t for t in steps if t[0] != "work"]
    bits = n_dp.bit_length() - 1
    me, z = lax.axis_index("dp"), lax.axis_index("tensor")
    side = lax.rem(me, 2)
    base = me - side
    micro = z // 2
    number = {task: i for i, task in enumerate(arrivals)}
    greet(n_t, bits, me, z)
    flips = [bit_flip(me, bit) for bit in range(bits)]

    def slot(w, s, index, flip=0):
        cols = own[w].shape[1]
        at = s * cols
        if w in paired:
            whose = side if not flip else 1 - side
            at = pl.multiple_of(((s // 2 + whose) % 2 * 2 + s % 2) * cols, cols)
        return outs[w].at[index + (slice(None), pl.ds(at, cols))]

    def copy_of(task):
        w, s, k = task
        i = number[task]
        if k == "z":
            src = own[w] if s == 1 else slot(w, s - 1, (0,) * bits)
            dst = slot(w, s, (0,) * bits)
            where = (me, lax.rem(z + 1, n_t))
        else:
            middle = list(range(1, bits))
            order = (middle if (w + s) % 2 == 0 else middle[::-1]) + [0]
            bit = order[k]
            src_at, dst_at = [], []
            for axis in range(bits):
                if axis == bit:
                    src_at.append(0)
                    dst_at.append(1)
                else:
                    held = slice(None) if axis in order[:k] else 0
                    src_at.append(held)
                    dst_at.append(held)
            src = own[w] if (k == 0 and s == 0) else slot(w, s, tuple(src_at))
            dst = slot(w, s, tuple(dst_at), flip=bit == 0)
            where = (flips[bit], z)
        return pltpu.make_async_remote_copy(
            src_ref=src, dst_ref=dst, send_sem=send.at[i], recv_sem=recv.at[i],
            device_id=where, device_id_type=pl.DeviceIdType.MESH,
        )

    placed = []
    for w in range(count):
        placed.append(pltpu.make_async_copy(own[w], slot(w, 0, (0,) * bits), near.at[w]))
        placed[-1].start()

    place = lax.rem(z, 2)
    target_core = base + z // 2

    def rows_copy(m):
        i = [number[("rows", q, 0)] for q in range(2)]
        where = (target_core, 2 * m + side)
        mine = (side == z // 2) & (z == 2 * m + side)
        return i, where, mine

    def start_rows(turn):
        i = number[("rows", turn, 0)]
        for m in range(2):
            _, where, mine = rows_copy(m)
            now = lax.rem(place + m, 2) == turn

            @pl.when(now & mine)
            def _():
                pltpu.make_async_copy(rows_ref.at[m], rows_out.at[place], recv.at[i]).start()

            @pl.when(now & jnp.logical_not(mine))
            def _():
                pltpu.make_async_remote_copy(
                    src_ref=rows_ref.at[m], dst_ref=rows_out.at[place], send_sem=near.at[count + m],
                    recv_sem=recv.at[i], device_id=where, device_id_type=pl.DeviceIdType.MESH,
                ).start()

    if fused:
        w_buf, x_rows, x_buf, a_buf, q_buf, s_buf, pick, shift, gains, deep_buf, f_sem, fsend, frecv = refs
        quarter, width = x_rows.shape
        half = x_buf.shape[0]
        size = width // n_dp
        deep = w_buf.shape[1]
        lanes = s_buf.shape[-1] // n_t
        hd8 = fused // n_dp
        x_buf[2 * quarter :, :] = jnp.zeros((half - 2 * quarter, width), bf16)
        a_buf[2 * quarter :, :] = jnp.zeros((half - 2 * quarter, width), bf16)
        q_buf[2 * quarter :, :] = jnp.zeros((half - 2 * quarter, deep), bf16)

    def block_of(p):
        digits = sum(((p >> (bits - 1 - b)) & 1) << b for b in range(bits))
        spot = me
        for b in range(bits):
            if (digits >> b) & 1:
                spot = bit_flip(spot, b)
        return spot

    def prepare():
        pltpu.make_async_copy(outs[0].reshape(width, deep), w_buf, f_sem.at[0]).start()
        copy = pltpu.make_async_copy(outs[count - 1], s_buf, f_sem.at[1])
        copy.start()
        copy.wait()
        cells = [tuple((p >> (bits - 1 - b)) & 1 for b in range(bits)) for p in range(n_dp)]
        small = [s_buf[c].astype(f32) for c in cells]
        for p in range(n_dp):
            gains[:, p * size : (p + 1) * size] = small[p][0:8, :size]
            for s in range(n_t):
                at = pl.multiple_of(s * width + block_of(p) * size, size)
                deep_buf[:, pl.ds(at, size)] = jnp.broadcast_to(
                    small[p][6:7, s * lanes : s * lanes + size], (8, size)
                )
        n = lax.broadcasted_iota(jnp.int32, (lanes, 8 * 64), 1)
        i = lax.broadcasted_iota(jnp.int32, (lanes, 8 * 64), 0)
        source = n // 256 * (4 * hd8) + n % 256 // 64 * hd8 + n % hd8
        for p in range(n_dp):
            hit = (i == source) & (n % 64 // hd8 == block_of(p))
            pick[p * lanes : (p + 1) * lanes, :] = hit.astype(bf16)
        for s in range(n_t):
            line = jnp.concatenate([v[7:8, s * lanes : (s + 1) * lanes] for v in small], axis=1)
            line = jnp.broadcast_to(line, (8, n_dp * lanes)).astype(bf16)
            got = dot_nn(line, pick[...])
            at = pl.multiple_of(((s // 2 + side) % 2 * 2 + s % 2) * 768, 256)
            shift[:, pl.ds(at, 256)] = got[:, :256]
            shift[:, pl.ds(pl.multiple_of(at + 256, 256), 256)] = jnp.zeros((8, 256), f32)
            shift[:, pl.ds(pl.multiple_of(at + 512, 256), 256)] = got[:, 256:]
        pltpu.make_async_copy(outs[0].reshape(width, deep), w_buf, f_sem.at[0]).wait()

    def far_copy(turn):
        rows = pl.ds(pl.multiple_of(lax.rem(micro + turn, 2) * quarter, 16), quarter)
        return pltpu.make_async_remote_copy(
            src_ref=q_buf.at[rows, pl.ds(deep // 2, deep // 2)], dst_ref=far_out.at[rows, :],
            send_sem=fsend.at[turn], recv_sem=frecv.at[turn],
            device_id=(flips[0], z), device_id_type=pl.DeviceIdType.MESH,
        )

    def finals():
        pads = pl.ds(2 * quarter, half - 2 * quarter)
        return [
            pltpu.make_async_copy(x_buf, x_out, f_sem.at[3]),
            pltpu.make_async_copy(a_buf, a_out, f_sem.at[4]),
            pltpu.make_async_copy(gains, wide_out, f_sem.at[7]),
            pltpu.make_async_copy(deep_buf, deep_out, f_sem.at[8]),
            pltpu.make_async_copy(q_buf.at[:, pl.ds(0, deep // 2)], near_out, f_sem.at[5]),
            pltpu.make_async_copy(
                q_buf.at[pads, pl.ds(0, deep // 2)], far_out.at[pads, :], f_sem.at[6]
            ),
        ]

    def work(turn):
        q = lax.rem(micro + turn, 2)
        at = pl.multiple_of(q * quarter, 16)
        copy = pltpu.make_async_copy(rows_out.at[q], x_rows, f_sem.at[2])
        copy.start()
        if turn == 0:
            prepare()
        copy.wait()
        spots = [pl.multiple_of(block_of(p) * size, size) for p in range(n_dp)]

        def norm_rows(first, tall):
            src = pl.ds(pl.multiple_of(first, 16), tall)
            dst = pl.ds(pl.multiple_of(at + first, 16), tall)
            for p in range(n_dp):
                x_buf[dst, p * size : (p + 1) * size] = x_rows[src, pl.ds(spots[p], size)]
            hat, _ = norm_parts(x_buf[dst, :].astype(f32))
            a_buf[dst, :] = (hat * gains[0:1, :] + gains[1:2, :]).astype(bf16)

        def norm_block(r, carry):
            norm_rows(r * 80, 80)
            return carry

        lax.fori_loop(0, quarter // 80, norm_block, 0)
        if quarter % 80:
            norm_rows(quarter // 80 * 80, quarter % 80)
        rows = pl.ds(at, quarter)

        def column_block(n, carry):
            cols = pl.ds(pl.multiple_of(n * 256, 256), 256)
            value = dot_nn(a_buf[rows, :], w_buf[:, cols]) + shift[0:1, cols]
            q_buf[rows, cols] = value.astype(bf16)
            return carry

        lax.fori_loop(deep // 512, deep // 256, column_block, 0)
        far_copy(turn).start()
        lax.fori_loop(0, deep // 512, column_block, 0)
        if turn == 1:
            for copy in finals():
                copy.start()

    copies = {task: copy_of(task) for task in arrivals if task[0] != "rows"}
    for task in arrivals:
        if task[0] != "rows" and parents[task] is None:
            copies[task].start()
    landed = {w: False for w in range(count)}
    for task in steps:
        if task[0] == "work":
            work(task[1])
            continue
        if task[0] == "rows":
            q = lax.rem(micro + task[1], 2)
            pltpu.make_async_copy(rows_ref.at[0], rows_out.at[q], recv.at[number[task]]).wait()
        else:
            copies[task].wait_recv()
        for child in arrivals:
            if parents[child] == task and child[0] == "rows":
                start_rows(child[1])
            elif parents[child] == task:
                if child[1] == 0 and not landed[child[0]]:
                    placed[child[0]].wait()
                    landed[child[0]] = True
                copies[child].start()
    for w in range(count):
        if not landed[w]:
            placed[w].wait()
    for task in arrivals:
        if task[0] != "rows":
            copies[task].wait_send()
    for m in range(2):
        i, where, mine = rows_copy(m)

        @pl.when(jnp.logical_not(mine))
        def _():
            pltpu.make_async_remote_copy(
                src_ref=rows_ref.at[m], dst_ref=rows_out.at[0], send_sem=near.at[count + m],
                recv_sem=recv.at[i[0]], device_id=where, device_id_type=pl.DeviceIdType.MESH,
            ).wait_send()
    if fused:
        for copy in finals():
            copy.wait()
        for turn in range(2):
            far_copy(turn).wait()

def bit_flip(me, bit):
    span = 1 << bit
    return me + span - 2 * span * lax.rem(me // span, 2)


def gather_all(rows, own, n_dp, n_t, paired, half, head_size, later):
    bits = n_dp.bit_length() - 1
    quarter, width = rows.shape[1:]
    size = width // n_dp
    fused = head_size if size % 128 == 0 else 0
    parents, steps = plan_gather(
        [w.shape[0] * w.shape[1] * 2 for w in own], bits, n_t, rows[0].size * 2, 2, fused, later
    )
    count = len(own)
    arrivals = [t for t in steps if t[0] != "work"]
    hbm = pl.BlockSpec(memory_space=pl.ANY)
    shapes = [jax.ShapeDtypeStruct(rows.shape, bf16)]
    shapes += [
        jax.ShapeDtypeStruct((2,) * bits + (w.shape[0], n_t * w.shape[1]), w.dtype) for w in own
    ]
    scratch = [
        pltpu.SemaphoreType.DMA((len(arrivals),)),
        pltpu.SemaphoreType.DMA((len(arrivals),)),
        pltpu.SemaphoreType.DMA((count + 2,)),
    ]
    if fused:
        deep = n_t * own[0].shape[1]
        shapes += [jax.ShapeDtypeStruct((half, c), bf16) for c in (width, width, deep // 2, deep // 2)]
        shapes += [jax.ShapeDtypeStruct((8, c), f32) for c in (width, n_t * width)]
        scratch += [
            pltpu.VMEM((width, deep), bf16),
            pltpu.VMEM((quarter, width), bf16),
            pltpu.VMEM((half, width), bf16),
            pltpu.VMEM((half, width), bf16),
            pltpu.VMEM((half, deep), bf16),
            pltpu.VMEM((2,) * bits + (own[-1].shape[0], n_t * own[-1].shape[1]), bf16),
            pltpu.VMEM((n_dp * own[-1].shape[1], 512), bf16),
            pltpu.VMEM((8, deep), f32),
            pltpu.VMEM((8, width), f32),
            pltpu.VMEM((8, n_t * width), f32),
            pltpu.SemaphoreType.DMA((9,)),
            pltpu.SemaphoreType.DMA((2,)),
            pltpu.SemaphoreType.DMA((2,)),
        ]
    return pl.pallas_call(
        functools.partial(gather_kernel, n_dp, n_t, count, parents, steps, paired, fused),
        in_specs=[hbm] * (1 + count),
        out_specs=[hbm] * len(shapes),
        out_shape=tuple(shapes),
        scratch_shapes=scratch,
        compiler_params=pltpu.CompilerParams(
            collective_id=0, has_side_effects=True, vmem_limit_bytes=60 * mib
        ),
        cost_estimate=pl.CostEstimate(flops=0, bytes_accessed=300 * mib, transcendentals=0),
        name="gather_all",
    )(rows, *own)


def stage_bits(w, s, bits):
    middle = list(range(1, bits))
    return [0] + (middle if (w + s) % 2 == 0 else middle[::-1])


def plan_reduce(widths, size, bits, n_t, rows_load):
    turn = list(range(1, n_t)) + [0]
    last = len(widths)
    chunks = [(last, s) for s in turn]
    for s in turn:
        group = list(range(last))
        chunks += [(w, s) for w in (group[-1:] + group[:-1] if s == turn[0] else group)]
    ready, free, core, order = {}, {"z": rows_load / 44e3}, 0.0, []
    pending = {("make", w, s): 0.0 for w, s in chunks}
    rank = {c: i for i, c in enumerate(chunks)}
    arrived = {}
    while pending:
        def key(item):
            kind, w, s = item[0][0], item[0][1], item[0][2]
            begin = max(core, item[1])
            return (begin, kind == "make", rank[(w, s)])

        action, when = min(pending.items(), key=key)
        del pending[action]
        order.append(action)
        w, s = action[1], action[2]
        cols = 64 if w == last else widths[w]
        rows = 16 if w == last else size << (bits - 1)
        share = rows * cols / (512 * 1024)
        begin = max(core, when)
        core = begin + (4.5 * share + 2.0 if action[0] == "make" else 1.2 * share / (1 << action[3] if action[0] == "add" else 4) + 0.3)
        flow = stage_bits(w, s, bits)
        k = 0 if action[0] == "make" else action[3] + 1 if action[0] == "add" else None

        def send(link, load):
            begin = max(core, free.get(link, 0.0))
            free[link] = begin + load / (150e3 if link == 0 else 44e3)
            return free[link] + 5.0

        def to_z():
            if s != 0:
                nxt = turn[turn.index(s) + 1]
                arrived[(w, nxt)] = send("z", (rows >> (bits - 1)) * cols * 2)
                if (w, nxt) in ready:
                    pending[("z", w, nxt)] = arrived[(w, nxt)]

        if k is not None and k < bits:
            load = (rows >> k) * cols * 2
            pending[("add", w, s, k)] = send(flow[k], load)
        elif k is not None:
            ready[(w, s)] = core
            if s == turn[0]:
                to_z()
            elif (w, s) in arrived:
                pending[("z", w, s)] = arrived[(w, s)]
        else:
            to_z()
    return order


def greet(n_t, bits, me, z):
    side = lax.rem(me, 2)
    barrier = pltpu.get_barrier_semaphore()
    for dz in range(n_t):
        for other in range(2):
            if dz or other:
                where = (me - side + lax.rem(side + other, 2), lax.rem(z + dz, n_t))
                pl.semaphore_signal(barrier, inc=1, device_id=where, device_id_type=pl.DeviceIdType.MESH)
    for bit in range(1, bits):
        where = (bit_flip(me, bit), z)
        pl.semaphore_signal(barrier, inc=1, device_id=where, device_id_type=pl.DeviceIdType.MESH)
    pl.semaphore_wait(barrier, 2 * n_t - 1 + bits - 1)


def reduce_kernel(n_dp, n_t, plan, widths, paired, *refs):
    bits = n_dp.bit_length() - 1
    count = len(widths)
    refs = list(refs)
    take = lambda n: [refs.pop(0) for _ in range(n)]
    xs, gs, (small_in, rows_in) = take(count), take(count), take(2)
    outs, (small_out, rows_out) = take(count), take(2)
    kept, came, zcame = take(count + 1), take(count + 1), take(count + 1)
    later = [take(bits - 1) for _ in range(count + 1)]
    (away, away_small, x_buf, x_turn, g_buf) = take(5)
    (x_sem, g_sem, s_sem, r_sem, send, recv, zsend, zrecv) = take(8)
    me, z = lax.axis_index("dp"), lax.axis_index("tensor")
    turn = list(range(1, n_t)) + [0]
    blk = kept[0].shape[-2]
    tall = blk << (bits - 1)
    greet(n_t, bits, me, z)

    side = lax.rem(me, 2)
    micro, owner = z // 2, lax.rem(z, 2)

    def rows_to(q):
        where = (me - side + owner, 2 * side + q)
        mine = (owner == side) & (2 * side + q == z)
        return where, mine

    def rows_from(m):
        return (side == z // 2) & (2 * m + side == z)

    for q in range(2):
        where, mine = rows_to(q)
        for m in range(2):

            @pl.when((micro == m) & mine)
            def _():
                pltpu.make_async_copy(rows_in.at[q], rows_out.at[m], r_sem.at[2 + m]).start()

            @pl.when((micro == m) & jnp.logical_not(mine))
            def _():
                pltpu.make_async_remote_copy(
                    src_ref=rows_in.at[q], dst_ref=rows_out.at[m], send_sem=r_sem.at[q],
                    recv_sem=r_sem.at[2 + m], device_id=where, device_id_type=pl.DeviceIdType.MESH,
                ).start()

    made = [a for a in plan if a[0] == "make" and a[1] < count]

    def fetch(i):
        _, w, s = made[i]
        c = widths[w]
        at = s * c
        if w in paired:
            at = pl.multiple_of(((s // 2 + side) % 2 * 2 + s % 2) * c, c)
        return pltpu.make_async_copy(
            gs[w].at[:, pl.ds(at, c)], g_buf.at[i % 2, :, pl.ds(0, c)], g_sem.at[i % 2]
        )

    def fetch_x(w):
        return pltpu.make_async_copy(xs[w], x_buf, x_sem)

    def at_stage(w, s, k, taken):
        flow = stage_bits(w, s, bits)
        return tuple(
            0 if bit in flow[:k] else (taken if bit == flow[k] else slice(None)) for bit in range(1, bits)
        )

    def landing(w, s, k):
        ref = came[w] if k == 0 else later[w][k - 1]
        return ref.at[s]

    def copy_of(w, s, k):
        flow = stage_bits(w, s, bits)
        if k == 0:
            src = away_small.at[s] if w == count else away_view(w, s)
        else:
            src = kept[w].at[(s,) + at_stage(w, s, k, 1)]
        return pltpu.make_async_remote_copy(
            src_ref=src, dst_ref=landing(w, s, k), send_sem=send.at[w, s, k], recv_sem=recv.at[w, s, k],
            device_id=(bit_flip(me, flow[k]), z), device_id_type=pl.DeviceIdType.MESH,
        )

    def away_view(w, s):
        i = made.index(("make", w, s)) % 2
        return away.at[(i,) + (slice(None),) * bits + (pl.ds(0, widths[w]),)]

    def zcopy(w, s):
        nxt = turn[turn.index(s) + 1]
        return pltpu.make_async_remote_copy(
            src_ref=kept[w].at[(s,) + (0,) * (bits - 1)], dst_ref=zcame[w].at[nxt],
            send_sem=zsend.at[w, s], recv_sem=zrecv.at[w, nxt],
            device_id=(me, lax.rem(z + 1, n_t)), device_id_type=pl.DeviceIdType.MESH,
        )

    def finish(w, s, total):
        ref = small_out if w == count else outs[w]
        ref[...] = total if total.shape == ref.shape else total.T

    fetch(0).start()
    fetch_x(made[0][1]).start()
    for action in plan:
        kind, w, s = action[:3]
        if kind == "make" and w == count:
            lanes = small_out.shape[-1]
            cols = pl.ds(s * lanes, lanes)
            for half, dst in ((1, away_small.at[s]), (0, kept[w].at[s])):
                src = small_in.at[(half,) + (slice(None),) * bits + (cols,)]
                pltpu.make_async_copy(src, dst, s_sem.at[half]).start()
            for half, dst in ((1, away_small.at[s]), (0, kept[w].at[s])):
                src = small_in.at[(half,) + (slice(None),) * bits + (cols,)]
                pltpu.make_async_copy(src, dst, s_sem.at[half]).wait()
            copy_of(w, s, 0).start()
        elif kind == "make":
            i = made.index(action)
            c = widths[w]
            if i == 0 or made[i - 1][1] != w:
                fetch_x(w).wait()
                for a in range(x_buf.shape[1] // 256):

                    def turn_block(b, carry, a=a):
                        rows = pl.ds(pl.multiple_of(b * 256, 256), 256)
                        x_turn[a * 256 : (a + 1) * 256, rows] = x_buf[rows, a * 256 : (a + 1) * 256].T
                        return carry

                    lax.fori_loop(0, x_buf.shape[0] // 256, turn_block, 0)
                follow = [m[1] for m in made[i:] if m[1] != w]
                if follow:
                    fetch_x(follow[0]).start()
            fetch(i).wait()
            if i + 1 < len(made):
                fetch(i + 1).start()
            if i >= 2:
                copy_of(*made[i - 2][1:], 0).wait_send()
            whole = (slice(None),) * bits

            def away_block(n, carry):
                cols = pl.ds(pl.multiple_of(n * 256, 256), 256)
                value = dot_nn(x_turn[tall:, :], g_buf[i % 2, :, cols]).astype(bf16)
                away[(i % 2,) + whole + (cols,)] = value.reshape((2,) * (bits - 1) + (blk, 256))
                return carry

            lax.fori_loop(0, c // 256, away_block, 0)
            copy_of(w, s, 0).start()

            def kept_block(n, carry):
                cols = pl.ds(pl.multiple_of(n * 256, 256), 256)
                value = dot_nn(x_turn[:tall, :], g_buf[i % 2, :, cols]).astype(bf16)
                kept[w][(s,) + whole + (cols,)] = value.reshape((2,) * (bits - 1) + (blk, 256))
                return carry

            lax.fori_loop(0, c // 256, kept_block, 0)
        elif kind == "add":
            k = action[3]
            copy_of(w, s, k).wait_recv()
            place = (s,) + (slice(None),) * (bits - 1) if k == 0 else (s,) + at_stage(w, s, k, 0)
            got = (came[w] if k == 0 else later[w][k - 1])[s]
            held = kept[w][place]
            kept[w][place] = (held.astype(f32) + got.astype(f32)).astype(held.dtype)
            if k + 1 < bits:
                copy_of(w, s, k + 1).start()
            elif s == turn[0]:
                zcopy(w, s).start()
        else:
            before = turn[turn.index(s) - 1]
            zcopy(w, before).wait_recv()
            place = (s,) + (0,) * (bits - 1)
            total = kept[w][place].astype(f32) + zcame[w][s].astype(f32)
            if s == turn[-1]:
                finish(w, s, total)
            else:
                kept[w][place] = total.astype(kept[w].dtype)
                zcopy(w, s).start()
    for w in range(count + 1):
        for s in turn:
            for k in range(bits):
                if k == 0 and w < count and made.index(("make", w, s)) < len(made) - 2:
                    continue
                copy_of(w, s, k).wait_send()
            if s != turn[-1]:
                zcopy(w, s).wait_send()
    for q in range(2):
        where, mine = rows_to(q)

        @pl.when(jnp.logical_not(mine))
        def _():
            pltpu.make_async_remote_copy(
                src_ref=rows_in.at[q], dst_ref=rows_out.at[0], send_sem=r_sem.at[q],
                recv_sem=r_sem.at[2], device_id=where, device_id_type=pl.DeviceIdType.MESH,
            ).wait_send()
    for m in range(2):
        pltpu.make_async_copy(rows_in.at[0], rows_out.at[m], r_sem.at[2 + m]).wait()


def reduce_all(xs, gs, small, rows, n_dp, n_t, paired):
    bits = n_dp.bit_length() - 1
    turned = (0, 3) if xs[0].shape[1] // n_dp % 128 == 0 else ()
    count = len(xs)
    width = xs[0].shape[1]
    size = width // n_dp
    widths = [g.shape[1] // n_t for g in gs]
    lanes = small.shape[-1] // n_t
    plan = plan_reduce(widths, size, bits, n_t, rows[0].size * 2)
    cells = (2,) * (bits - 1)
    shapes = [(size, c, bf16) for c in widths] + [(small.shape[-2], lanes, f32)]
    hbm, vmem = pl.BlockSpec(memory_space=pl.ANY), pl.BlockSpec(memory_space=pltpu.VMEM)
    scratch = [pltpu.VMEM((n_t,) + cells + (r, c), t) for r, c, t in shapes]
    scratch += [pltpu.VMEM((n_t,) + cells + (r, c), t) for r, c, t in shapes]
    scratch += [pltpu.VMEM((n_t, r, c), t) for r, c, t in shapes]
    for r, c, t in shapes:
        scratch += [pltpu.VMEM((n_t,) + (2,) * (bits - 1 - k) + (r, c), t) for k in range(1, bits)]
    scratch += [
        pltpu.VMEM((2,) + cells + (size, max(widths)), bf16),
        pltpu.VMEM((n_t,) + cells + (small.shape[-2], lanes), f32),
        pltpu.VMEM(xs[0].shape, bf16),
        pltpu.VMEM((width, xs[0].shape[0]), bf16),
        pltpu.VMEM((2, gs[0].shape[0], max(widths)), bf16),
        pltpu.SemaphoreType.DMA,
        pltpu.SemaphoreType.DMA((2,)),
        pltpu.SemaphoreType.DMA((2,)),
        pltpu.SemaphoreType.DMA((4,)),
        pltpu.SemaphoreType.DMA((count + 1, n_t, bits)),
        pltpu.SemaphoreType.DMA((count + 1, n_t, bits)),
        pltpu.SemaphoreType.DMA((count + 1, n_t)),
        pltpu.SemaphoreType.DMA((count + 1, n_t)),
    ]
    return pl.pallas_call(
        functools.partial(reduce_kernel, n_dp, n_t, plan, widths, paired),
        in_specs=[hbm] * (2 * count + 2),
        out_specs=[vmem] * (count + 1) + [hbm],
        out_shape=tuple(
            jax.ShapeDtypeStruct((c, size) if w in turned else (size, c), f32) for w, c in enumerate(widths)
        )
        + (
            jax.ShapeDtypeStruct((small.shape[-2], lanes), f32),
            jax.ShapeDtypeStruct(rows.shape, rows.dtype),
        ),
        scratch_shapes=scratch,
        compiler_params=pltpu.CompilerParams(
            collective_id=1, has_side_effects=True, vmem_limit_bytes=60 * mib
        ),
        cost_estimate=pl.CostEstimate(
            flops=2 * xs[0].size * n_t * sum(widths), bytes_accessed=200 * mib, transcendentals=0
        ),
        name="reduce_all",
    )(*xs, *gs, small, rows)


def gelu_parts(v):
    bell = jnp.exp2(v * v * (-0.5 * log2e))
    t = 1.0 / (1.0 + jnp.abs(v) * (0.3275911 * 0.7071067811865476))
    poly = t * (
        0.254829592 * 0.5
        + t * (-0.284496736 * 0.5 + t * (1.421413741 * 0.5 + t * (-1.453152027 * 0.5 + t * (1.061405429 * 0.5))))
    )
    tail = poly * bell
    cdf = jnp.where(v < 0.0, tail, 1.0 - tail)
    return v * cdf, cdf + v * bell * 0.3989422804014327


def mlp_kernel(
    n_dp, n_t, o_own, o_oth, x_in, w_proj, w_fc1, w_fc2_in, cot, wide, deep_shift,
    heads_out, c_out, act_out, gpre_out, gy_out, gh_out, gattn_out, g_own, g_oth, y_a, y_b, gy_mid, w_fc2_parts,
    sums, deep_sums,
    heads, x_buf, h_buf, c_buf, act, slope, o_buf, gy, gc, wp, col_buf, row_buf, stage,
    col_sem, row_sem, load_sem, save_sem, out_sem, cot_send, cot_recv, swap_send, swap_recv,
    rest_send, rest_recv,
):
    bits = n_dp.bit_length() - 1
    me, z = lax.axis_index("dp"), lax.axis_index("tensor")
    side = lax.rem(me, 2)
    base = me - side
    micro, place = z // 2, lax.rem(z, 2)
    half, width = x_buf.shape
    quarter = stage.shape[0]
    size = width // n_dp
    deep = act.shape[1]
    mesh_id = pl.DeviceIdType.MESH
    partner = (bit_flip(me, 0), z)
    greet(n_t, bits, me, z)
    w_fc2 = w_fc2_parts.reshape(width, deep)

    def far_heads():
        return pltpu.make_async_remote_copy(
            src_ref=o_oth, dst_ref=heads.at[:, pl.ds(width // 2, width // 2)],
            send_sem=swap_send.at[0], recv_sem=swap_recv.at[0], device_id=partner, device_id_type=mesh_id,
        )

    far_heads().start()
    loads = [
        pltpu.make_async_copy(o_own, heads.at[:, pl.ds(0, width // 2)], load_sem.at[0]),
        pltpu.make_async_copy(x_in, x_buf, load_sem.at[1]),
        pltpu.make_async_copy(w_proj, wp, load_sem.at[2]),
    ]
    for copy in loads:
        copy.start()

    def rest(s, k):
        flow = stage_bits(2, s, bits)
        flow = flow[1:] + flow[:1]
        cols = pl.ds(s * width, width)
        src_at = tuple(0 if b == flow[k] or b not in flow[:k] else slice(None) for b in range(bits))
        dst_at = tuple(1 if b == flow[k] else a for b, a in enumerate(src_at))
        return pltpu.make_async_remote_copy(
            src_ref=w_fc2_parts.at[src_at + (slice(None), cols)],
            dst_ref=w_fc2_parts.at[dst_at + (slice(None), cols)],
            send_sem=rest_send.at[s, k], recv_sem=rest_recv.at[s, k],
            device_id=(bit_flip(me, flow[k]), z), device_id_type=mesh_id,
        )

    for s in range(n_t):
        rest(s, 1).start()

    def cot_copy(turn):
        m = lax.rem(place + turn, 2)
        where, mine = (base + z // 2, 2 * m + side), (side == z // 2) & (z == 2 * m + side)
        here = pltpu.make_async_copy(cot.at[m], gy_mid.at[turn], cot_recv.at[turn])
        there = pltpu.make_async_remote_copy(
            src_ref=cot.at[m], dst_ref=gy_mid.at[turn], send_sem=cot_send.at[turn],
            recv_sem=cot_recv.at[turn], device_id=where, device_id_type=mesh_id,
        )
        return here, there, mine

    for turn in range(2):
        here, there, mine = cot_copy(turn)

        @pl.when(mine)
        def _():
            here.start()

        @pl.when(jnp.logical_not(mine))
        def _():
            there.start()

    def cols_of(ref, n):
        slot = lax.rem(n, 2)
        return pltpu.make_async_copy(
            ref.at[:, pl.ds(pl.multiple_of(n * 1024, 1024), 1024)], col_buf.at[slot], col_sem.at[slot]
        )

    def rows_of(ref, n):
        slot = lax.rem(n, 2)
        return pltpu.make_async_copy(
            ref.at[pl.ds(pl.multiple_of(n * 256, 256), 256), :], row_buf.at[slot], row_sem.at[slot]
        )

    def stream(ref, fetch, count, use):
        def one(n, carry):
            fetch(ref, n).wait()

            @pl.when(n + 1 < count)
            def _():
                fetch(ref, n + 1).start()

            use(n, lax.rem(n, 2))
            return carry

        lax.fori_loop(0, count, one, 0)

    cols_of(w_fc1, 0).start()
    for copy in loads:
        copy.wait()
    far_heads().wait_recv()
    pltpu.make_async_copy(heads, heads_out, save_sem.at[0]).start()

    chunk = half // 1

    def by_rows(body):
        def one(r, carry):
            body(pl.ds(pl.multiple_of(r * chunk, chunk), chunk))
            return carry

        lax.fori_loop(0, half // chunk, one, 0)

    def proj_block(n, carry):
        cols = pl.ds(pl.multiple_of(n * 256, 256), 256)

        def body(rows):
            value = dot_nt(heads[rows, :], wp[cols, :]) + wide[2:3, cols]
            h_buf[rows, cols] = x_buf[rows, cols].astype(f32) + value

        by_rows(body)
        return carry

    lax.fori_loop(0, width // 256, proj_block, 0)

    def norm_block(r, carry):
        rows = pl.ds(pl.multiple_of(r * 128, 128), 128)
        hat, _ = norm_parts(h_buf[rows, :])
        c_buf[rows, :] = (hat * wide[3:4, :] + wide[4:5, :]).astype(bf16)
        return carry

    lax.fori_loop(0, half // 128, norm_block, 0)
    pltpu.make_async_copy(c_buf, c_out, save_sem.at[1]).start()

    def fc1_block(n, slot):
        cols = pl.ds(pl.multiple_of(n * 1024, 1024), 1024)

        def body(rows):
            value, grade = gelu_parts(dot_nn(c_buf[rows, :], col_buf[slot]) + deep_shift[0:1, cols])
            act[rows, cols] = value.astype(bf16)
            slope[rows, cols] = grade.astype(bf16)

        by_rows(body)

    pieces = deep // 1024
    sent = 0
    for n in range(pieces):
        cols_of(w_fc1, n).wait()
        if n + 1 < pieces:
            cols_of(w_fc1, n + 1).start()
        fc1_block(n, n % 2)
        ready = {1: n_t // 2, pieces - 1: n_t}.get(n, sent)
        for s in range(sent, ready):
            for k in range(2, bits):
                rest(s, k - 1).wait_recv()
                rest(s, k).start()
        sent = ready
    for s in range(n_t):
        rest(s, bits - 1).wait_recv()
    rows_of(w_fc2, 0).start()
    cols_of(w_fc2, 0).start()
    pltpu.make_async_copy(act, act_out, save_sem.at[2]).start()

    def spot(p):
        digits = sum(((p >> (bits - 1 - b)) & 1) << b for b in range(bits))
        at = me
        for b in range(bits):
            if (digits >> b) & 1:
                at = bit_flip(at, b)
        return pl.ds(pl.multiple_of(at * size, size), size)

    def fc2_block(n, slot):
        cols = pl.ds(pl.multiple_of(n * 256, 256), 256)

        def body(rows):
            value = dot_nt(act[rows, :], row_buf[slot]) + wide[5:6, cols]
            o_buf[rows, cols] = (h_buf[rows, cols] + value).astype(bf16)

        by_rows(body)

    stream(w_fc2, rows_of, width // 256, fc2_block)
    rows_of(w_fc1, 0).start()

    def unorder(r, carry):
        rows = pl.ds(pl.multiple_of(r * 16, 16), 16)
        line = o_buf[rows, :]
        for p in range(n_dp):
            x_buf[rows, spot(p)] = line[:, p * size : (p + 1) * size]
        return carry

    lax.fori_loop(0, half // 16, unorder, 0)

    for q in range(2):
        src = x_buf.at[pl.ds(q * quarter, quarter), :]
        for first in range(2):

            @pl.when(micro == first)
            def _():
                pltpu.make_async_copy(src, (y_a, y_b)[(q + first) % 2], out_sem.at[q]).start()

    gy[2 * quarter :, :] = jnp.zeros((half - 2 * quarter, width), bf16)
    for turn in range(2):
        cot_copy(turn)[0].wait()
        at = lax.rem(micro + turn, 2) * quarter
        copy = pltpu.make_async_copy(gy_mid.at[turn], stage, load_sem.at[0])
        copy.start()
        copy.wait()

        def reorder(r, carry):
            src = pl.ds(pl.multiple_of(r * 16, 16), 16)
            dst = pl.ds(pl.multiple_of(at + r * 16, 16), 16)
            for p in range(n_dp):
                gy[dst, p * size : (p + 1) * size] = stage[src, spot(p)]
            return carry

        lax.fori_loop(0, quarter // 16, reorder, 0)
    pltpu.make_async_copy(gy, gy_out, save_sem.at[3]).start()

    def gpre_block(n, slot):
        cols = pl.ds(pl.multiple_of(n * 1024, 1024), 1024)
        deep_sums[:, cols] = jnp.zeros((8, 1024), f32)

        def body(rows):
            value = dot_nn(gy[rows, :], col_buf[slot]) * slope[rows, cols].astype(f32)
            low = value.astype(bf16)
            slope[rows, cols] = low
            deep_sums[:, cols] += jnp.sum(low.astype(f32).reshape(chunk // 8, 8, 1024), axis=0)

        by_rows(body)

    stream(w_fc2, cols_of, deep // 1024, gpre_block)
    pltpu.make_async_copy(slope, gpre_out, save_sem.at[4]).start()

    def gc_block(n, slot):
        cols = pl.ds(pl.multiple_of(n * 256, 256), 256)

        def body(rows):
            gc[rows, cols] = dot_nt(slope[rows, :], row_buf[slot])

        by_rows(body)

    stream(w_fc1, rows_of, width // 256, gc_block)

    sums[...] = jnp.zeros_like(sums)

    def back_block(r, carry):
        rows = pl.ds(pl.multiple_of(r * 128, 128), 128)
        hat, inverse = norm_parts(h_buf[rows, :])
        g_c = gc[rows, :]
        g_y = gy[rows, :].astype(f32)
        g_h = g_y + norm_back(g_c * wide[3:4, :], hat, inverse)
        low = g_h.astype(bf16)
        gc[rows, :] = g_h
        o_buf[rows, :] = low
        for i, value in enumerate((low.astype(f32), g_c * hat, g_c, g_y)):
            sums[i] += jnp.sum(value.reshape(16, 8, width), axis=0)
        return carry

    lax.fori_loop(0, half // 128, back_block, 0)
    pltpu.make_async_copy(gc, gh_out, save_sem.at[5]).start()
    pltpu.make_async_copy(o_buf, gattn_out, save_sem.at[6]).start()

    pltpu.make_async_copy(heads, heads_out, save_sem.at[0]).wait()

    def gheads_block(n, carry):
        cols = pl.ds(pl.multiple_of(n * 256, 256), 256)

        def body(rows):
            heads[rows, cols] = dot_nn(o_buf[rows, :], wp[:, cols]).astype(bf16)

        by_rows(body)
        return carry

    lax.fori_loop(width // 512, width // 256, gheads_block, 0)
    far = pltpu.make_async_remote_copy(
        src_ref=heads.at[:, pl.ds(width // 2, width // 2)], dst_ref=g_oth,
        send_sem=swap_send.at[1], recv_sem=swap_recv.at[1], device_id=partner, device_id_type=mesh_id,
    )
    far.start()
    lax.fori_loop(0, width // 512, gheads_block, 0)
    near = pltpu.make_async_copy(heads.at[:, pl.ds(0, width // 2)], g_own, load_sem.at[1])
    near.start()

    pltpu.make_async_copy(c_buf, c_out, save_sem.at[1]).wait()
    pltpu.make_async_copy(act, act_out, save_sem.at[2]).wait()
    pltpu.make_async_copy(gy, gy_out, save_sem.at[3]).wait()
    pltpu.make_async_copy(slope, gpre_out, save_sem.at[4]).wait()
    pltpu.make_async_copy(gc, gh_out, save_sem.at[5]).wait()
    pltpu.make_async_copy(o_buf, gattn_out, save_sem.at[6]).wait()
    near.wait()
    far.wait()
    far_heads().wait_send()
    for turn in range(2):
        here, there, mine = cot_copy(turn)

        @pl.when(jnp.logical_not(mine))
        def _():
            there.wait_send()

    for s in range(n_t):
        for k in range(1, bits):
            rest(s, k).wait_send()
    for q in range(2):
        pltpu.make_async_copy(x_buf.at[pl.ds(q * quarter, quarter), :], y_a, out_sem.at[q]).wait()


def mlp(o_own, o_oth, x, w_proj, w_fc1, w_fc2, cot, wide, deep_shift, n_dp, n_t):
    half, width = x.shape
    deep = w_fc1.shape[1]
    quarter = cot.shape[1]
    hbm, vmem = pl.BlockSpec(memory_space=pl.ANY), pl.BlockSpec(memory_space=pltpu.VMEM)
    shape = jax.ShapeDtypeStruct
    row, tall = shape((half, width), bf16), shape((half, deep), bf16)
    dma = pltpu.SemaphoreType.DMA
    outs = pl.pallas_call(
        functools.partial(mlp_kernel, n_dp, n_t),
        in_specs=[hbm] * 7 + [vmem] * 2,
        out_specs=[hbm] * 13 + [vmem] * 2,
        input_output_aliases={5: 12},
        out_shape=(
            row, row, tall, tall, row, shape((half, width), f32), row,
            shape(o_own.shape, bf16), shape(o_own.shape, bf16), shape(cot.shape[1:], bf16),
            shape(cot.shape[1:], bf16), shape(cot.shape, bf16), shape(w_fc2.shape, bf16),
            shape((4, 8, width), f32), shape((8, deep), f32),
        ),
        scratch_shapes=[
            pltpu.VMEM((half, width), bf16),
            pltpu.VMEM((half, width), bf16),
            pltpu.VMEM((half, width), f32),
            pltpu.VMEM((half, width), bf16),
            pltpu.VMEM((half, deep), bf16),
            pltpu.VMEM((half, deep), bf16),
            pltpu.VMEM((half, width), bf16),
            pltpu.VMEM((half, width), bf16),
            pltpu.VMEM((half, width), f32),
            pltpu.VMEM((width, width), bf16),
            pltpu.VMEM((2, width, 1024), bf16),
            pltpu.VMEM((2, 256, deep), bf16),
            pltpu.VMEM((quarter, width), bf16),
            dma((2,)), dma((2,)), dma((3,)), dma((7,)), dma((2,)), dma((2,)), dma((2,)), dma((2,)),
            dma((2,)), dma((n_t, n_dp.bit_length() - 1)), dma((n_t, n_dp.bit_length() - 1)),
        ],
        compiler_params=pltpu.CompilerParams(
            collective_id=2, has_side_effects=True, vmem_limit_bytes=60 * mib
        ),
        cost_estimate=pl.CostEstimate(
            flops=2 * half * width * (4 * deep + 2 * width), bytes_accessed=90 * mib, transcendentals=0
        ),
        name="mlp",
    )(o_own, o_oth, x, w_proj, w_fc1, w_fc2, cot, wide, deep_shift)
    return outs


def ingest_kernel(order, a_ref, b_ref, o_ref):
    rows, width = a_ref.shape
    count = order.shape[0] - 1
    size = width // count
    first = order[count]
    for place in range(count):
        src = pl.ds(pl.multiple_of(order[place] * size, size), size)
        dst = slice(place * size, (place + 1) * size)

        @pl.when(first == 0)
        def _():
            o_ref[0:rows, dst] = a_ref[:, src]
            o_ref[rows : 2 * rows, dst] = b_ref[:, src]

        @pl.when(first != 0)
        def _():
            o_ref[0:rows, dst] = b_ref[:, src]
            o_ref[rows : 2 * rows, dst] = a_ref[:, src]

    o_ref[2 * rows :, :] = jnp.zeros((o_ref.shape[0] - 2 * rows, width), o_ref.dtype)


def ingest(order, first, a, b, padded):
    rows, width = a.shape
    count = order.shape[0]
    if width // count % 128:
        both = jnp.where(first == 0, jnp.concatenate([a, b]), jnp.concatenate([b, a]))
        both = jnp.take(both.reshape(2 * rows, count, -1), order, axis=1).reshape(2 * rows, width)
        return jnp.pad(both, ((0, padded - 2 * rows), (0, 0)))
    scalars = jnp.concatenate([order, first[None]]).astype(jnp.int32)
    return pl.pallas_call(
        ingest_kernel,
        grid_spec=pltpu.PrefetchScalarGridSpec(
            num_scalar_prefetch=1,
            grid=(1,),
            in_specs=[pl.BlockSpec((rows, width), lambda i, _: (0, 0))] * 2,
            out_specs=pl.BlockSpec((padded, width), lambda i, _: (0, 0)),
        ),
        out_shape=jax.ShapeDtypeStruct((padded, width), a.dtype),
        compiler_params=pltpu.CompilerParams(vmem_limit_bytes=20 * mib),
        name="ingest",
    )(scalars, a, b)


def egress_kernel(order, x_ref, a_ref, b_ref):
    rows, width = a_ref.shape
    count = order.shape[0] - 1
    size = width // count
    first = order[count]
    for place in range(count):
        dst = pl.ds(pl.multiple_of(order[place] * size, size), size)
        src = slice(place * size, (place + 1) * size)

        @pl.when(first == 0)
        def _():
            a_ref[:, dst] = x_ref[0:rows, src]
            b_ref[:, dst] = x_ref[rows : 2 * rows, src]

        @pl.when(first != 0)
        def _():
            b_ref[:, dst] = x_ref[0:rows, src]
            a_ref[:, dst] = x_ref[rows : 2 * rows, src]


def egress(order, inverse, first, x, rows):
    width = x.shape[1]
    count = order.shape[0]
    if width // count % 128:
        both = jnp.take(x.reshape(-1, count, width // count), inverse, axis=1).reshape(-1, width)
        top, low = both[:rows], both[rows : 2 * rows]
        return jnp.where(first == 0, top, low), jnp.where(first == 0, low, top)
    scalars = jnp.concatenate([order, first[None]]).astype(jnp.int32)
    return pl.pallas_call(
        egress_kernel,
        grid_spec=pltpu.PrefetchScalarGridSpec(
            num_scalar_prefetch=1,
            grid=(1,),
            in_specs=[pl.BlockSpec(x.shape, lambda i, _: (0, 0))],
            out_specs=[pl.BlockSpec((rows, width), lambda i, _: (0, 0))] * 2,
        ),
        out_shape=(jax.ShapeDtypeStruct((rows, width), x.dtype),) * 2,
        compiler_params=pltpu.CompilerParams(vmem_limit_bytes=20 * mib),
        name="egress",
    )(scalars, x)


def norm_parts(operand):
    centred = operand - jnp.mean(operand, axis=-1, keepdims=True)
    inverse = lax.rsqrt(jnp.mean(centred * centred, axis=-1, keepdims=True) + epsilon)
    return centred * inverse, inverse


def norm_back(scaled, normed, inverse):
    return inverse * (
        scaled
        - jnp.mean(scaled, axis=-1, keepdims=True)
        - normed * jnp.mean(scaled * normed, axis=-1, keepdims=True)
    )


def make_body(n_dp, n_t):
    bits = n_dp.bit_length() - 1
    reverse = [int(format(i, "b").zfill(bits)[::-1], 2) for i in range(n_dp)]
    axes = ("dp", "tensor")

    def at(dp, t):
        return dp * n_t + t

    go_a, go_b = [], []
    for dp in range(n_dp):
        c, base = dp % 2, dp - dp % 2
        for j in range(n_t):
            go_a.append((at(dp, j), at(base + j // 2, 2 * (j % 2) + c)))
            go_b.append((at(dp, j), at(base + j // 2, 2 * (1 - j % 2) + c)))
    back_a = [(d, s) for s, d in go_a]
    back_b = [(d, s) for s, d in go_b]
    ring = [(j, (j + 1) % n_t) for j in range(n_t)]

    def swap(value, bit):
        return lax.ppermute(value, "dp", [(i, i ^ (1 << bit)) for i in range(n_dp)])

    def step_z(value):
        return lax.ppermute(value, "tensor", ring)

    def body(
        tokens, segment_ids, pad_mask, cotangent, ln1_gain, ln1_bias, qkv_weight, qv_bias,
        proj_weight, proj_bias, ln2_gain, ln2_bias, fc1_weight, fc1_bias, fc2_weight, fc2_bias,
    ):
        me = lax.axis_index("dp")
        z = lax.axis_index("tensor")
        side = me % 2
        quarter, width = tokens.shape[2], tokens.shape[3]
        length = segment_ids.shape[2]
        half = -(-2 * quarter // block) * block
        size = width // n_dp
        micro = z // 2
        odd = z % 2
        order = jnp.stack([me ^ reverse[p] for p in range(n_dp)]).astype(jnp.int32)
        inverse = jnp.stack(
            [sum((((me ^ d) >> b) & 1) << (bits - 1 - b) for b in range(bits)) for d in range(n_dp)]
        ).astype(jnp.int32)

        def bring(array):
            a = lax.ppermute(lax.dynamic_index_in_dim(array[:, 0], odd, 0, False), axes, go_a)
            b = lax.ppermute(lax.dynamic_index_in_dim(array[:, 0], 1 - odd, 0, False), axes, go_b)
            return a, b

        def give(a, b):
            return lax.ppermute(a, axes, back_a), lax.ppermute(b, axes, back_b)

        lanes = max(128, size)

        def row_of(v):
            return jnp.pad(v.reshape(1, -1), ((0, 0), (0, lanes - v.size)))

        fields = [ln1_gain, ln1_bias, proj_bias, ln2_gain, ln2_bias, fc2_bias, fc1_bias, qv_bias]
        packed = jnp.concatenate([row_of(v) for v in fields] + [jnp.zeros((8, lanes), bf16)])
        rows_in, w_qkv, w_fc1, w_fc2, w_proj, small, *made = gather_all(
            tokens[:, 0],
            (qkv_weight.reshape(size, -1), fc1_weight, fc2_weight.T, proj_weight.T, packed),
            n_dp, n_t, (0, 3), half, qv_bias.shape[2] * n_dp, 2,
        )

        w_qkv, w_fc1, w_proj = [w.reshape(width, -1) for w in (w_qkv, w_fc1, w_proj)]
        heads_t, hd = qv_bias.shape[1], qv_bias.shape[2] * n_dp

        which = z % 2
        packed_ids = jnp.stack([segment_ids[:, 0], pad_mask[:, 0]])
        packed_oth = swap(packed_ids, 0)
        ids = jnp.where(which == side, packed_ids, packed_oth)
        ids = lax.dynamic_index_in_dim(ids, micro, 1, False)
        seg, live = ids[0], ids[1]
        gap = half - length // 2

        def stretch(v, fill):
            return jnp.pad(v.reshape(2, -1), ((0, 0), (0, gap)), constant_values=fill).reshape(-1)

        q_ids = stretch(seg, -1)
        k_ids = stretch(jnp.where(live == 1, seg, -2), -2)
        per_half = half // block
        first_pos = jnp.array([h * (length // 2) + b * block for h in range(2) for b in range(per_half)])
        last_pos = jnp.array(
            [min(h * (length // 2) + (b + 1) * block, (h + 1) * (length // 2)) - 1 for h in range(2) for b in range(per_half)]
        )
        lo = jnp.sum((seg[None, :] < seg[first_pos][:, None]).astype(jnp.int32), axis=1)
        hi = jnp.sum((seg[None, :] <= seg[last_pos][:, None]).astype(jnp.int32), axis=1) - 1
        place = lambda v: jnp.where(v >= length // 2, v + gap, v)
        start = place(lo) // stride
        count = (place(hi) - start * stride) // window + 1
        info = jnp.concatenate([side[None], start, count]).astype(jnp.int32)
        k_ids = jnp.pad(k_ids, (0, window), constant_values=-2)

        if made:
            x_low, rows_one, own, oth, wide, deep_shift = made
            gain_one = wide[0]
            x = x_low.astype(f32)
            hat_one, inv_one = norm_parts(x)
        else:
            small = small.reshape(n_dp, packed.shape[0], n_t, lanes).astype(f32)
            gain_one, shift_one, proj_shift, gain_two, shift_two, fc2_shift = [
                small[:, i, 0, :size].reshape(-1) for i in range(6)
            ]
            ordered = jnp.take(small[:, 6:8], inverse, axis=0)
            fc1_shift = jnp.transpose(ordered[:, 0, :, :size], (1, 0, 2)).reshape(-1)
            w_fc2 = w_fc2.reshape(width, -1)
            x_low = ingest(order, jnp.int32(0), rows_in[0], rows_in[1], half)
            x = x_low.astype(f32)
            hat_one, inv_one = norm_parts(x)
            rows_one = (hat_one * gain_one + shift_one).astype(bf16)
            qv = ordered[:, 1, :, : qv_bias.size].reshape(n_dp, n_t, 2, heads_t, hd // n_dp)
            qv = jnp.transpose(qv, (1, 2, 3, 0, 4)).reshape(n_t, 2, heads_t * hd)
            shift = jnp.stack([qv[:, 0], jnp.zeros_like(qv[:, 0]), qv[:, 1]], axis=1).reshape(2, -1)
            shift = jnp.where(side == 0, shift, shift[::-1]).reshape(-1)
            near_cols = w_qkv.shape[1] // 2
            far = (dot_nn(rows_one, w_qkv[:, near_cols:]) + shift[near_cols:]).astype(bf16)
            oth = swap(far, 0)
            own = (dot_nn(rows_one, w_qkv[:, :near_cols]) + shift[:near_cols]).astype(bf16)
        if made:
            o_own, o_oth, lse = attend(info, own, oth, q_ids[None, :], k_ids[:, None])
            (
                heads, rows_two, act, g_pre, gy_low, g_hidden, g_attn, g_own, g_oth, y_a, y_b, _, _, sums, deep_sums,
            ) = mlp(
                o_own, o_oth, x_low, w_proj, w_fc1, w_fc2, cotangent[:, 0], wide, deep_shift, n_dp, n_t
            )
            proj_shift_grad, gain_two_grad, shift_two_grad, fc2_shift_grad = jnp.sum(sums, axis=1)
            fc1_shift_grad = jnp.sum(deep_sums, axis=0)
            parts = attend_back(
                info, own, oth, g_own, g_oth, o_own, o_oth, lse, q_ids[None, :], k_ids[:, None]
            )
            parts, (out_a, out_b) = lax.optimization_barrier((parts, give(y_a, y_b)))
            out = jnp.where(odd == 0, jnp.stack([out_a, out_b]), jnp.stack([out_b, out_a]))[:, None]
        else:
            own, oth, cot = lax.optimization_barrier((own, oth, cotangent))
            o_own, o_oth, lse = attend(info, own, oth, q_ids[None, :], k_ids[:, None])
            o_own, o_oth, lse, gy_a, gy_b = lax.optimization_barrier((o_own, o_oth, lse) + bring(cot))
            o_came = swap(o_oth, 0)
            heads = jnp.concatenate([o_own, o_came], axis=1)
            hidden = x + (dot_nt(heads, w_proj) + proj_shift)
            hat_two, inv_two = norm_parts(hidden)
            rows_two = (hat_two * gain_two + shift_two).astype(bf16)
            pre = dot_nn(rows_two, w_fc1) + fc1_shift
            cdf = 0.5 * (1.0 + lax.erf(pre * 0.7071067811865476))
            act = (pre * cdf).astype(bf16)
            slope = (cdf + pre * jnp.exp(-0.5 * pre * pre) * 0.3989422804014327).astype(bf16)
            y = hidden + (dot_nt(act, w_fc2) + fc2_shift)
            y_rows = egress(order, inverse, micro, y.astype(bf16), quarter)

            gy_low = ingest(order, micro, gy_a, gy_b, half)
            gy = gy_low.astype(f32)
            fc2_shift_grad = jnp.sum(gy, axis=0)
            g_pre = (dot_nn(gy_low, w_fc2) * slope.astype(f32)).astype(bf16)
            fc1_shift_grad = jnp.sum(g_pre, axis=0, dtype=f32)
            g_c = dot_nt(g_pre, w_fc1)
            gain_two_grad = jnp.sum(g_c * hat_two, axis=0)
            shift_two_grad = jnp.sum(g_c, axis=0)
            g_hidden = gy + norm_back(g_c * gain_two, hat_two, inv_two)
            g_attn = g_hidden.astype(bf16)
            proj_shift_grad = jnp.sum(g_attn, axis=0, dtype=f32)
            near_cols = w_proj.shape[1] // 2
            g_oth = swap(dot_nn(g_attn, w_proj[:, near_cols:]).astype(bf16), 0)
            g_own = dot_nn(g_attn, w_proj[:, :near_cols]).astype(bf16)
            own, y_rows = lax.optimization_barrier((own, y_rows))
            parts = attend_back(
                info, own, oth, g_own, g_oth, o_own, o_oth, lse, q_ids[None, :], k_ids[:, None]
            )
            parts, (out_a, out_b) = lax.optimization_barrier((parts, give(*y_rows)))
            out = jnp.where(odd == 0, jnp.stack([out_a, out_b]), jnp.stack([out_b, out_a]))[:, None]

        d_own, d_oth = parts
        d_qkv = jnp.concatenate([d_own, swap(d_oth, 0)], axis=1)
        qkv_sum = jnp.sum(d_qkv, axis=0, dtype=f32).reshape(2, n_t // 2, 3, -1)
        qkv_sum = jnp.where(side == 0, qkv_sum, qkv_sum[::-1]).reshape(n_t, 3, -1)
        g_a = dot_nt(d_qkv, w_qkv)
        gain_one_grad = jnp.sum(g_a * hat_one, axis=0)
        shift_one_grad = jnp.sum(g_a, axis=0)
        grad_rows = (g_hidden + norm_back(g_a * gain_one, hat_one, inv_one)).astype(bf16)
        grad_rows = jnp.stack(egress(order, inverse, jnp.int32(0), grad_rows, quarter))

        fields = [gain_one_grad, shift_one_grad, proj_shift_grad, gain_two_grad, shift_two_grad, fc2_shift_grad]
        wide_g = jnp.stack(fields).reshape(6, n_dp, 1, size)
        wide_g = jnp.transpose(jnp.broadcast_to(wide_g, (6, n_dp, n_t, size)), (1, 0, 2, 3))
        fc1_g = jnp.transpose(fc1_shift_grad.reshape(n_t, n_dp, 1, size), (1, 2, 0, 3))
        qv_g = jnp.stack([qkv_sum[:, 0], qkv_sum[:, 2]], axis=1).reshape(n_t, 2, heads_t, n_dp, -1)
        qv_g = jnp.transpose(qv_g, (3, 0, 1, 2, 4)).reshape(n_dp, 1, n_t, -1)
        pad = lambda v: jnp.pad(v, ((0, 0), (0, 0), (0, 0), (0, lanes - v.shape[-1])))
        hidden_g = jnp.take(jnp.concatenate([pad(fc1_g), pad(qv_g)], axis=1), order, axis=0)
        small_g = jnp.concatenate([pad(wide_g), hidden_g], axis=1)
        small_g = small_g.reshape((2,) * bits + (8, n_t * lanes))

        fc2_grad, fc1_grad, qkv_grad, proj_grad, small_sum, tokens_grad = reduce_all(
            (gy_low, rows_two, rows_one, g_attn), (act, g_pre, d_qkv, heads), small_g, grad_rows, n_dp, n_t, (2, 3)
        )
        wide_g = [small_sum[i, :size] for i in range(6)]
        fc1_g = small_sum[6:7, :size]
        qv_g = small_sum[7, : qv_bias.size].reshape(qv_bias.shape)
        return (
            out,
            tokens_grad[:, None],
            wide_g[0],
            wide_g[1],
            qkv_grad.reshape(qkv_weight.shape),
            qv_g,
            proj_grad if proj_grad.shape == proj_weight.shape else proj_grad.T,
            wide_g[2],
            wide_g[3],
            wide_g[4],
            fc1_grad,
            fc1_g,
            fc2_grad if fc2_grad.shape == fc2_weight.shape else fc2_grad.T,
            wide_g[5],
        )

    return body


def solution(mesh):
    in_specs = (
        P(None, "dp", "tensor", None),
        P(None, "dp", None),
        P(None, "dp", None),
        P(None, "dp", "tensor", None),
        P("dp"),
        P("dp"),
        P("dp", None, "tensor"),
        P(None, "tensor", "dp"),
        P("tensor", "dp"),
        P("dp"),
        P("dp"),
        P("dp"),
        P("dp", "tensor"),
        P("tensor", "dp"),
        P("tensor", "dp"),
        P("dp"),
    )
    out_specs = (
        P(None, "dp", "tensor", None),
        P(None, "dp", "tensor", None),
        P("dp"),
        P("dp"),
        P("dp", None, "tensor"),
        P(None, "tensor", "dp"),
        P("tensor", "dp"),
        P("dp"),
        P("dp"),
        P("dp"),
        P("dp", "tensor"),
        P("tensor", "dp"),
        P("tensor", "dp"),
        P("dp"),
    )
    body = make_body(mesh.shape["dp"], mesh.shape["tensor"])
    return jax.shard_map(body, mesh=mesh, in_specs=in_specs, out_specs=out_specs, check_vma=False)
```
